32 devices in a mesh: ctx: 8 (over y, x, core), batch: 4 (over z).
Axes of the slice: x: 2, y: 2, z: 4, core: 2. Of those that a mesh axis runs over, the one named last changes fastest.
Arguments:
- tokens: bfloat16 [4, 2048, 768], P('batch', 'ctx'), may hold values from -6 to 6
- seg_ids: int32 [4, 2048], P('batch', 'ctx'), may hold values from 0 to 7, never falling along the last dimension, each value on 1 to 1024 neighbouring positions
- routes: int32 [8, 4, 256, 1], P('ctx', 'batch'), may hold values from 0 to 3; in each aligned block of 256 rows (0 to 255, 256 to 511, ..., all dimensions but the last counted through in order) at most 128 rows name the same one
- attn_gain: bfloat16 [768], replicated, may hold values from 0.25 to 1.75
- query_key_value_weight: bfloat16 [768, 2304], P(('ctx', 'batch')), may hold values from -0.21875 to 0.21875
- attention_output_weight: bfloat16 [768, 768], P(('ctx', 'batch')), may hold values from -1.5 to 1.5
- bias_table: bfloat16 [32, 12], replicated, may hold values from -4 to 4
- ffn_gain: bfloat16 [768], replicated, may hold values from 0.25 to 1.75
- router_weight: bfloat16 [768, 4], P(('ctx', 'batch')), may hold values from -0.15625 to 0.15625
- expert_in: bfloat16 [4, 768, 3072], P('batch'), may hold values from -0.21875 to 0.21875
- expert_out: bfloat16 [4, 3072, 768], P('batch'), may hold values from -3 to 3
- out_grad: bfloat16 [4, 2048, 768], P('batch', 'ctx'), may hold values from -6 to 6
Outputs:
- layer_out: bfloat16 [4, 2048, 768], P('batch', 'ctx')
- tokens_grad: bfloat16 [4, 2048, 768], P('batch', 'ctx')
- attn_gain_grad: float32 [768], replicated
- qkv_weight_grad: float32 [768, 2304], P(('ctx', 'batch'))
- attn_out_weight_grad: float32 [768, 768], P(('ctx', 'batch'))
- bias_table_grad: float32 [32, 12], replicated
- ffn_gain_grad: float32 [768], replicated
- router_weight_grad: float32 [768, 4], P(('ctx', 'batch'))
- expert_in_grad: float32 [4, 768, 3072], P('batch', 'ctx')
- expert_out_grad: float32 [4, 3072, 768], P('batch', 'ctx')
The draws below stay inside these ranges and needn't reach their ends.
Inputs may be any that keep to these rules, and one draw needn't show every extreme that they name: In each aligned block of 256 rows of routes, taken in the array's order (the rows of one device), no expert is named by more than 128 rows, and some block names some expert exactly 128 times. `seg_ids`: segment numbers never fall along a sequence; a segment holds at most 1024 tokens, and some segment holds exactly that many.
All inputs are finite; a program needn't handle non-finite values.
Results may differ from the reference program's by a relative error of at most 0.019.
Values may be sent and summed in bfloat16 or wider, within the bound.
No kernel may reach another device: no remote copies, remote signals or barrier semaphores. Data moves between devices by JAX's collectives and lax.ppermute only.
A program may use at most 192 MiB of HBM per device.

```python
import math
import jax
import jax.numpy as jnp
import numpy as np
from jax import lax

D = 768
HEADS = 12
HEAD_DIM = 64
FF = 3072
BUCKETS = 32
MAX_DIST = 128
SEQ_LEN = 2048
SEG_COUNT = 8
PER = 256
TOK_DEV = 256
SEQS_ALL = 4
EXPERTS = 4
CAP = 128
SEG_MOST = 1024
N_CTX = 8
N_BATCH = 4


def block_levels(stream_key, extent, shards, smallest, largest):
    factor_of, own = 1.0, jax.random.fold_in(stream_key, 6)
    for dim, shards_of in shards:
        draws = jnp.exp(jax.random.uniform(jax.random.fold_in(own, dim), (shards_of,), jnp.float32, smallest / len(shards), largest / len(shards)))
        factor_of = factor_of * jnp.repeat(draws, extent[dim] // shards_of).reshape([-1 if axis == dim else 1 for axis in range(len(extent))])
    return factor_of


def length_profile(count, total, bound, slope):
    portions = [(1 << 20) // math.isqrt(grade ** slope) + 1 for grade in range(2, count + 1)]
    surplus, counts = total - bound - (count - 1), [1] * (count - 1)
    while surplus > 0:
        movable = [i for i in range(count - 1) if counts[i] < bound]
        whole, remaining = sum([portions[i] for i in movable]), surplus
        for i in movable:
            extra = min(bound - counts[i], max(1, remaining * portions[i] // whole), surplus)
            counts[i] = counts[i] + extra
            surplus = surplus - extra
    return np.array([bound] + counts)


def uneven_parts(rng, amount, total, reach, skew):
    if amount == 2:
        one = jax.random.randint(rng, (), max(1, total - reach), min(reach, total - 1) + 1)
        return jnp.stack([one, total - one])
    tallies = jnp.asarray(length_profile(amount, total, reach, skew), jnp.int32)
    couples = (amount - 1) // 2
    donor, sink = tallies[1:1 + 2 * couples:2], tallies[2:2 + 2 * couples:2]
    slack = jnp.minimum(donor - 1, reach - sink)
    passed = jax.random.randint(jax.random.fold_in(rng, 1), (couples,), 0, 1 << 20) % (slack + 1)
    tallies = tallies.at[1:1 + 2 * couples:2].set(donor - passed).at[2:2 + 2 * couples:2].set(sink + passed)
    return tallies[jax.random.permutation(jax.random.fold_in(rng, 2), amount)]


def shared_out(rng, own, number, rows, amount, top, most, lean):
    order = jax.random.permutation(rng, amount)
    crowded, usual = portions_of(amount, rows * top, most, lean, True), portions_of(amount, rows * top, most, lean, False)
    places = jnp.arange(amount)

    def named(sizes, turn):
        used = int((sizes > 0).sum())
        fixed = max(1, used // 4)
        shifted = fixed + (places - fixed + turn * (used - fixed)) % max(1, amount - fixed)
        return jnp.zeros((amount,), jnp.int32).at[order[jnp.where(places < fixed, places, shifted)]].set(jnp.asarray(sizes, jnp.int32))

    sizes = jnp.where(number % 4 == 0, named(crowded, number // 4), named(usual, number - number // 4 - 1))
    mixed = jax.random.permutation(jax.random.fold_in(own, 3), amount)
    source_of, receiver = mixed[0:amount // 2 * 2:2], mixed[1:amount // 2 * 2:2]
    slack = jnp.minimum(sizes[source_of] - 1, most - sizes[receiver]) // 2
    slack = jnp.where((source_of == order[0]) | (receiver == order[0]) | (sizes[receiver] == 0), 0, jnp.maximum(slack, 0))
    shifted = jax.random.randint(jax.random.fold_in(own, 4), (amount // 2,), 0, 1 << 20) % (slack + 1)
    sizes = sizes.at[source_of].add(-shifted).at[receiver].add(shifted)
    items = jnp.searchsorted(jnp.cumsum(sizes), jnp.arange(rows * top), side="right").astype(jnp.int32)
    table = items.reshape(top, rows).T
    table = table[jax.random.permutation(jax.random.fold_in(own, 1), rows)]
    turn = jax.random.randint(jax.random.fold_in(own, 2), (rows, 1), 0, top)
    return jnp.take_along_axis(table, (jnp.arange(top)[None, :] + turn) % top, axis=1)


def portions_of(number_of, total, reach, slope, full):
    portions = [(1 << 20) // math.isqrt(grade ** slope) + 1 for grade in range(1, number_of + 1)]
    largest = reach if full else min(reach, max(-(-total // number_of), total * portions[0] // sum(portions)))
    least = 1 if total - largest >= number_of - 1 else 0
    given, surplus = [largest] + [least] * (number_of - 1), total - largest - least * (number_of - 1)
    while surplus > 0:
        free = [i for i in range(1, number_of) if given[i] < largest] or [i for i in range(1, number_of) if given[i] < reach]
        whole, budget = sum([portions[i] for i in free]), surplus
        for i in free:
            more = min(reach - given[i], max(1, budget * portions[i] // whole), surplus)
            given[i] = given[i] + more
            surplus = surplus - more
    return np.array(given)


def centred(key, shape, scale, bound, split=(), kind=jnp.bfloat16):
    level = block_levels(key, shape, split, -0.22, 0.18) if split else 1.0
    drawn = jax.random.normal(key, shape, jnp.float32) * scale * level
    return jnp.minimum(jnp.maximum(drawn, -bound), bound).astype(kind)


def setup_inputs(seed: int = 0) -> dict:
    key_of = jax.random.split(jax.random.key(seed), 13)
    tokens = centred(key_of[0], (SEQS_ALL, SEQ_LEN, D), 1.0, 6.0, ((0, 4), (1, 8)))
    seg_ids = jax.vmap(lambda own: jnp.searchsorted(jnp.cumsum(uneven_parts(own, SEG_COUNT, SEQ_LEN, SEG_MOST, 2)), jnp.arange(SEQ_LEN), side="right"))(jax.random.split(key_of[1], SEQS_ALL)).reshape((SEQS_ALL, SEQ_LEN)).astype(jnp.int32)
    routes_keys = jax.random.split(jax.random.fold_in(key_of[2], 1), (SEQ_LEN // PER) * SEQS_ALL * PER // TOK_DEV)
    routes_turns = jax.random.permutation(jax.random.fold_in(key_of[2], 3), (SEQ_LEN // PER) * SEQS_ALL * PER // TOK_DEV)
    routes = jax.vmap(lambda own, number: shared_out(jax.random.fold_in(key_of[2], 2), own, number, TOK_DEV, EXPERTS, 1, CAP, 2))(routes_keys, routes_turns).reshape((SEQ_LEN // PER, SEQS_ALL, PER, 1))
    attn_gain = jnp.clip(1.0 + 0.15 * jax.random.normal(key_of[3], (D,), jnp.float32), 0.25, 1.75).astype(jnp.bfloat16)
    query_key_value_weight = centred(key_of[4], (D, 3 * D), D ** -0.5, 0.21875, ((0, 32),))
    attention_output_weight = centred(key_of[5], (D, D), (max(1, D // 48)) ** -0.5, 1.5, ((0, 32),))
    bias_table = centred(key_of[6], (BUCKETS, HEADS), 1.0, 4.0)
    ffn_gain = jnp.clip(1.0 + 0.15 * jax.random.normal(key_of[7], (D,), jnp.float32), 0.25, 1.75).astype(jnp.bfloat16)
    router_weight = centred(key_of[8], (D, EXPERTS), (2 * D) ** -0.5, 0.15625, ((0, 32),))
    expert_in = centred(key_of[9], (EXPERTS, D, FF), D ** -0.5, 0.21875, ((0, 4),))
    expert_out = centred(key_of[10], (EXPERTS, FF, D), (max(1, FF // 768)) ** -0.5, 3.0, ((0, 4),))
    out_grad = centred(key_of[11], (SEQS_ALL, SEQ_LEN, D), 1.0, 6.0, ((0, 4), (1, 8)))
    return {"tokens": tokens, "seg_ids": seg_ids, "routes": routes, "attn_gain": attn_gain, "query_key_value_weight": query_key_value_weight, "attention_output_weight": attention_output_weight, "bias_table": bias_table, "ffn_gain": ffn_gain, "router_weight": router_weight, "expert_in": expert_in, "expert_out": expert_out, "out_grad": out_grad}


EPSILON = 1e-06
MASKED = -1e+30
HIGHEST_ACCURACY = lax.Precision.HIGHEST

@jax.custom_vjp
def low(v):
    return lax.optimization_barrier(v.astype(jnp.bfloat16)).astype(jnp.float32)

@jax.custom_vjp
def low_back(v):
    return v

def low_keep(v):
    return (low(v), None)

def low_pass(kept, grad):
    return (grad,)

def back_keep(v):
    return (v, None)

def back_low(kept, grad):
    return (low(grad),)
low.defvjp(low_keep, low_pass)
low_back.defvjp(back_keep, back_low)

def bucket_limits():
    half_span = BUCKETS // 2
    exact_span = half_span // 2
    log_levels = half_span - exact_span
    limits = []
    for level_at in range(1, log_levels):
        bound_row = exact_span
        while bound_row ** log_levels * exact_span ** level_at < MAX_DIST ** level_at * exact_span ** log_levels:
            bound_row = bound_row + 1
        limits.append(bound_row)
    return limits

def relative_bucket(offsets):
    half_span = BUCKETS // 2
    exact_span = half_span // 2
    offsets = offsets.astype(jnp.int32)
    distance = jnp.abs(offsets).astype(jnp.int32)
    far_bucket = jnp.full(distance.shape, exact_span, jnp.int32)
    for bound_row in bucket_limits():
        far_bucket = far_bucket + (distance >= bound_row).astype(jnp.int32)
    near_bucket = jnp.where(distance < exact_span, distance, far_bucket).astype(jnp.int32)
    upper_half = jnp.where(offsets > 0, jnp.int32(half_span), jnp.int32(0)).astype(jnp.int32)
    return (near_bucket + upper_half).astype(jnp.int32)

def rms_scale(rows_in, gain_in):
    inverse = lax.rsqrt(lax.optimization_barrier(jnp.mean(rows_in * rows_in, axis=-1, keepdims=True)) + EPSILON)
    return rows_in * inverse * gain_in

def attend_sequence(packed_seq, seg_seq, bias_full):
    length = packed_seq.shape[0]
    model_width = packed_seq.shape[1] // 3
    queries = packed_seq[:, :model_width].reshape(length, HEADS, HEAD_DIM)
    keys_seq = packed_seq[:, model_width:2 * model_width].reshape(length, HEADS, HEAD_DIM)
    values_seq = packed_seq[:, 2 * model_width:].reshape(length, HEADS, HEAD_DIM)
    scaled = jnp.einsum('qhd,khd->hqk', queries, keys_seq, precision=HIGHEST_ACCURACY) * HEAD_DIM ** (-0.5) + bias_full
    scaled = low_back(scaled)
    live_pairs = (seg_seq[:, None] == seg_seq[None, :])[None]
    scaled = jnp.where(live_pairs, scaled, MASKED)
    top_vals = lax.optimization_barrier(jnp.max(scaled, axis=-1, keepdims=True))
    expo_vals = jnp.where(live_pairs, jnp.exp(scaled - top_vals), 0.0)
    totals = lax.optimization_barrier(jnp.sum(expo_vals, axis=-1, keepdims=True))
    mixed_heads = jnp.einsum('hqk,khd->hqd', low(expo_vals), values_seq, precision=HIGHEST_ACCURACY) / totals
    return jnp.transpose(mixed_heads, (1, 0, 2)).reshape(length, model_width)

def expert_apply(triple):
    rows_in, first_weight, second_weight = triple
    pre_act = jnp.dot(rows_in, first_weight, precision=HIGHEST_ACCURACY)
    hidden = low(jax.nn.gelu(pre_act, approximate=False))
    return low(low_back(jnp.dot(hidden, second_weight, precision=HIGHEST_ACCURACY)))

def forward(tokens, attn_gain, query_key_value_weight, attention_output_weight, bias_table, ffn_gain, router_weight, expert_in, expert_out, seg_ids, route_rows):
    normalized_input = low(rms_scale(tokens, attn_gain))
    packed_documents = low(low_back(jnp.einsum('ntc,cm->ntm', normalized_input, query_key_value_weight, precision=HIGHEST_ACCURACY)))
    positions = jnp.arange(SEQ_LEN, dtype=jnp.int32)
    bucket_ids = relative_bucket(positions[None, :] - positions[:, None])
    bias_full = jnp.transpose(bias_table[bucket_ids], (2, 0, 1))
    checked = jax.checkpoint(attend_sequence)
    mixed_f = lax.map(lambda pair_in: checked(pair_in[0], pair_in[1], bias_full), (packed_documents, seg_ids))
    mixed_tokens = low(low_back(mixed_f))
    middle_state = tokens + low_back(jnp.einsum('ntc,cm->ntm', mixed_tokens, attention_output_weight, precision=HIGHEST_ACCURACY))
    row_total = SEQS_ALL * SEQ_LEN
    normed2 = low(rms_scale(middle_state, ffn_gain)).reshape(row_total, D)
    logits = low_back(jnp.dot(normed2, router_weight, precision=HIGHEST_ACCURACY))
    router_probs = jax.nn.softmax(logits, axis=-1)
    chosen = route_rows[:, None] == jnp.arange(EXPERTS, dtype=jnp.int32)[None, :]
    gate_vals = lax.optimization_barrier(jnp.sum(jnp.where(chosen, router_probs, 0.0), axis=-1))
    rank_rows = (jnp.cumsum(chosen.astype(jnp.int32), axis=0, dtype=jnp.int32) - 1).astype(jnp.int32)
    slot_ids = lax.optimization_barrier(jnp.sum(jnp.where(chosen, rank_rows, jnp.int32(0)).astype(jnp.int32), axis=-1, dtype=jnp.int32)).astype(jnp.int32)
    expert_room = N_CTX * N_BATCH * CAP
    slot_table = jnp.zeros((EXPERTS, expert_room, D), normed2.dtype).at[route_rows, slot_ids].set(normed2)
    slot_table = low_back(slot_table)
    produced = lax.map(jax.checkpoint(expert_apply), (slot_table, expert_in, expert_out))
    returned = produced[route_rows, slot_ids]
    result = middle_state.reshape(row_total, D) + gate_vals[:, None] * returned
    return result.reshape(SEQS_ALL, SEQ_LEN, D)

def reference(tokens, seg_ids, routes, attn_gain, query_key_value_weight, attention_output_weight, bias_table, ffn_gain, router_weight, expert_in, expert_out, out_grad):
    route_rows = jnp.transpose(routes[:, :, :, 0], (1, 0, 2)).reshape(SEQS_ALL * SEQ_LEN).astype(jnp.int32)
    seg_rows = seg_ids.astype(jnp.int32)
    floats = tuple((array_in.astype(jnp.float32) for array_in in (tokens, attn_gain, query_key_value_weight, attention_output_weight, bias_table, ffn_gain, router_weight, expert_in, expert_out)))

    def closed(*params):
        return forward(*params, seg_rows, route_rows)
    result, pullback = jax.vjp(closed, *floats)
    gradients = pullback(out_grad.astype(jnp.float32))
    return (result.astype(jnp.bfloat16), gradients[0].astype(jnp.bfloat16), gradients[1], gradients[2], gradients[3], gradients[4], gradients[5], gradients[6], gradients[7], gradients[8])
```

```python
import functools
import math

import jax
import jax.numpy as jnp
import numpy as np
from jax import lax
from jax.experimental import pallas as pl
from jax.experimental.pallas import tpu as pltpu
from jax.sharding import PartitionSpec as P

BUCKETS = 32
MAX_DIST = 128
EPSILON = 1e-06
MASKED = -1e30
F32 = jnp.float32
BF16 = jnp.bfloat16


def bucket_limits():
    half_span = BUCKETS // 2
    exact_span = half_span // 2
    log_levels = half_span - exact_span
    limits = []
    for level_at in range(1, log_levels):
        bound_row = exact_span
        while (
            bound_row**log_levels * exact_span**level_at
            < MAX_DIST**level_at * exact_span**log_levels
        ):
            bound_row = bound_row + 1
        limits.append(bound_row)
    return limits


def relative_bucket(offsets):
    half_span = BUCKETS // 2
    exact_span = half_span // 2
    distance = np.abs(offsets)
    far = np.full(distance.shape, exact_span, np.int32)
    for bound_row in bucket_limits():
        far = far + (distance >= bound_row).astype(np.int32)
    near = np.where(distance < exact_span, distance, far)
    return near + np.where(offsets > 0, half_span, 0)


def band_onehot(block):
    column = np.arange(2 * block)
    rows = []
    for d in range(5):
        if d in (0, 4):
            offsets = np.full((2 * block,), (d - 2) * max(block, MAX_DIST), np.int64)
        else:
            offsets = (d - 2) * block + block - column
        rows.append(relative_bucket(offsets)[None, :] == np.arange(BUCKETS)[:, None])
    return np.stack(rows)


def dot(a, b, dims, precision=None):
    return lax.dot_general(a, b, (dims, ((), ())), preferred_element_type=F32, precision=precision)


NN = ((1,), (0,))
NT = ((1,), (1,))
TN = ((0,), (0,))


def xor_order(parts, index):
    parts = list(parts)
    step = 1
    while step < len(parts):
        odd = (index // step) % 2 == 1
        parts = [jnp.where(odd, parts[i ^ step], parts[i]) for i in range(len(parts))]
        step = step * 2
    return parts


def swap(value, axis, size, mask):
    return lax.ppermute(value, axis, [(i, i ^ mask) for i in range(size)])


def pair_sum(parts):
    while len(parts) > 1:
        parts = [parts[i] + parts[i + 1] for i in range(0, len(parts), 2)]
    return parts[0]


def small_sum(value, axes):
    for axis, size in axes:
        step = 1
        while step < size:
            masks = [0, step, 2 * step, 3 * step] if 4 * step <= size else [0, step]
            value = pair_sum([value if m == 0 else swap(value, axis, size, m) for m in masks])
            step = step * len(masks)
    return value


def head_mask(value, half):
    lane = lax.broadcasted_iota(jnp.int32, value.shape, 1)
    return jnp.where((lane // 64) == half, value, jnp.zeros_like(value))


def set_bias(band_ref, bias_s, heads, block):
    for h in range(heads):
        for d in range(5):
            row = jnp.broadcast_to(band_ref[h, d : d + 1, :], (block, 2 * block))
            bias_s[h, d] = pltpu.roll(row, block, 1, stride=1, stride_axis=0)[:, :block]


def key_at(kb, info_ref, ring, groups):
    return ((kb % ring) ^ info_ref[1]) * groups + ((kb // ring) ^ info_ref[0])


def attend_kernel(
    info_ref,
    span_ref,
    qkv_ref,
    kv_ref,
    segq_ref,
    segk_ref,
    band_ref,
    ot_ref,
    mixed_ref,
    lse_ref,
    bias_s,
    vt_s,
    mask_s,
    stat_s,
    acc_s,
    *,
    heads,
    groups,
    ring,
    block,
):
    wide = 256
    set_bias(band_ref, bias_s, heads, block)
    blocks = groups * ring
    for kb in range(blocks):
        rows = slice(kb * block, (kb + 1) * block)
        vt_s[kb] = kv_ref[rows, wide:].astype(F32).T.astype(BF16)
    for i in range(groups):
        qb = (i ^ info_ref[0]) * ring + info_ref[1]
        rows = slice(i * block, (i + 1) * block)
        segq = segq_ref[i, 0:1, :]
        stat_s[0:heads] = jnp.full((heads, 1, block), MASKED, F32)
        stat_s[heads : 2 * heads] = jnp.zeros((heads, 1, block), F32)
        acc_s[...] = jnp.zeros_like(acc_s)

        @pl.loop(span_ref[i, 0], span_ref[i, 1])
        def _(kb):
            at = key_at(kb, info_ref, ring, groups)
            start = pl.multiple_of(at * block, block)
            segk = segk_ref[pl.ds(start, block), :]
            mask_s[...] = jnp.where(segk == segq, 0.0, MASKED).astype(F32)
            d = jnp.clip(kb - qb, -2, 2) + 2
            for h in range(heads):
                lane = (h // 2) * 128
                query = head_mask(qkv_ref[rows, lane : lane + 128], h % 2) * 0.125
                key = kv_ref[pl.ds(start, block), lane : lane + 128]
                scores = dot(key, query.astype(BF16), NT) + bias_s[h, d] + mask_s[...]
                top = stat_s[h]
                top_next = jnp.maximum(top, jnp.max(scores, axis=0, keepdims=True))
                expo = jnp.exp(scores - top_next)
                decay = jnp.exp(top - top_next)
                stat_s[h] = top_next
                stat_s[heads + h] = stat_s[heads + h] * decay + jnp.sum(
                    expo, axis=0, keepdims=True
                )
                value_t = vt_s[at, h * 64 : (h + 1) * 64, :]
                acc_s[h] = acc_s[h] * decay + dot(value_t, expo.astype(BF16), NN)

        for h in range(heads):
            total = stat_s[heads + h]
            out_t = acc_s[h] / total
            ot_ref[i, h * 64 : (h + 1) * 64, :] = out_t
            lse_ref[i, h : h + 1, :] = stat_s[h] + jnp.log(total)
        full = ot_ref[i].T
        mixed_ref[rows, :] = full.astype(BF16)


def attend(info, span, qkv, kv, segq, segk, band, heads, groups, ring, block):
    width = heads * 64
    return pl.pallas_call(
        functools.partial(attend_kernel, heads=heads, groups=groups, ring=ring, block=block),
        out_shape=(
            jax.ShapeDtypeStruct((groups, width, block), F32),
            jax.ShapeDtypeStruct((groups * block, width), BF16),
            jax.ShapeDtypeStruct((groups, 8, block), F32),
        ),
        in_specs=[pl.BlockSpec(memory_space=pltpu.SMEM)] * 2
        + [pl.BlockSpec(memory_space=pltpu.VMEM)] * 5,
        out_specs=[pl.BlockSpec(memory_space=pltpu.VMEM)] * 3,
        scratch_shapes=[
            pltpu.VMEM((heads, 5, block, block), F32),
            pltpu.VMEM((groups * ring, 256, block), BF16),
            pltpu.VMEM((block, block), F32),
            pltpu.VMEM((2 * heads, 1, block), F32),
            pltpu.VMEM((heads, 64, block), F32),
        ],
        compiler_params=pltpu.CompilerParams(vmem_limit_bytes=48 << 20),
        name="attend",
    )(info, span, qkv, kv, segq, segk, band)


def attend_back_kernel(
    info_ref,
    span_ref,
    qkv_ref,
    kv_ref,
    segq_ref,
    segk_ref,
    band_ref,
    dmix_ref,
    ot_ref,
    lse_ref,
    dq_ref,
    own_ref,
    other_ref,
    dband_ref,
    bias_s,
    kt_s,
    mask_s,
    delta_s,
    dqt_s,
    dkv_s,
    dbias_s,
    *,
    heads,
    groups,
    ring,
    block,
):
    wide = 256
    set_bias(band_ref, bias_s, heads, block)
    blocks = groups * ring
    for kb in range(blocks):
        rows = slice(kb * block, (kb + 1) * block)
        kt_s[kb] = kv_ref[rows, :wide].astype(F32).T.astype(BF16)
    dkv_s[...] = jnp.zeros_like(dkv_s)
    dbias_s[...] = jnp.zeros_like(dbias_s)
    for i in range(groups):
        qb = (i ^ info_ref[0]) * ring + info_ref[1]
        rows = slice(i * block, (i + 1) * block)
        segq = segq_ref[i, 0:1, :]
        dmix_t = dmix_ref[rows, :].astype(F32).T
        for h in range(heads):
            cut = slice(h * 64, (h + 1) * 64)
            delta_s[h] = jnp.sum(dmix_t[cut, :] * ot_ref[i, cut, :], axis=0, keepdims=True)
        dqt_s[...] = jnp.zeros_like(dqt_s)

        @pl.loop(span_ref[i, 0], span_ref[i, 1])
        def _(kb):
            at = key_at(kb, info_ref, ring, groups)
            start = pl.multiple_of(at * block, block)
            segk = segk_ref[pl.ds(start, block), :]
            mask_s[...] = jnp.where(segk == segq, 0.0, MASKED).astype(F32)
            d = jnp.clip(kb - qb, -2, 2) + 2
            for h in range(heads):
                lane = (h // 2) * 128
                query = (head_mask(qkv_ref[rows, lane : lane + 128], h % 2) * 0.125).astype(BF16)
                d_out = head_mask(dmix_ref[rows, lane : lane + 128], h % 2)
                key = kv_ref[pl.ds(start, block), lane : lane + 128]
                value = kv_ref[pl.ds(start, block), wide + lane : wide + lane + 128]
                scores = dot(key, query, NT) + bias_s[h, d] + mask_s[...]
                soft = jnp.exp(scores - lse_ref[i, h : h + 1, :])
                d_soft = dot(value, d_out, NT)
                d_scores = (soft * (d_soft - delta_s[h])).astype(BF16)
                dkv_s[pl.ds(start, block), wide + lane : wide + lane + 128] += dot(
                    soft.astype(BF16), d_out, NN
                )
                dkv_s[pl.ds(start, block), lane : lane + 128] += dot(d_scores, query, NN)
                dqt_s[h * 64 : (h + 1) * 64, :] += dot(
                    kt_s[at, h * 64 : (h + 1) * 64, :], d_scores, NN
                )
                dbias_s[h, d] += d_scores.astype(F32)

        pad = jnp.zeros((wide - heads * 64, block), F32)
        dq_ref[rows, :] = (jnp.concatenate([dqt_s[...], pad], axis=0) * 0.125).T.astype(BF16)
    own = groups * block
    own_ref[...] = dkv_s[:own, :]
    other_ref[...] = dkv_s[own:, :].astype(BF16)
    zero = jnp.zeros((block, block), F32)
    for h in range(heads):
        for d in range(5):
            if d in (0, 4):
                tile = jnp.sum(dbias_s[h, d], axis=0, keepdims=True)
                tile = jnp.concatenate([tile, zero[:1]], axis=1)
            else:
                tile = jnp.concatenate([zero, dbias_s[h, d]], axis=1)
                tall = block
                while tall > 1:
                    tall = tall // 2
                    tile = tile[:tall] + pltpu.roll(tile[tall:], 2 * block - tall, 1)
            dband_ref[h, d : d + 1, :] = tile


def attend_back(
    info, span, qkv, kv, segq, segk, band, dmix, out_t, lse, heads, groups, ring, block
):
    own = groups * block
    return pl.pallas_call(
        functools.partial(attend_back_kernel, heads=heads, groups=groups, ring=ring, block=block),
        out_shape=(
            jax.ShapeDtypeStruct((own, 256), BF16),
            jax.ShapeDtypeStruct((own, 512), F32),
            jax.ShapeDtypeStruct((own * (ring - 1), 512), BF16),
            jax.ShapeDtypeStruct((heads, 8, 2 * block), F32),
        ),
        in_specs=[pl.BlockSpec(memory_space=pltpu.SMEM)] * 2
        + [pl.BlockSpec(memory_space=pltpu.VMEM)] * 8,
        out_specs=[pl.BlockSpec(memory_space=pltpu.VMEM)] * 4,
        scratch_shapes=[
            pltpu.VMEM((heads, 5, block, block), F32),
            pltpu.VMEM((groups * ring, 256, block), BF16),
            pltpu.VMEM((block, block), F32),
            pltpu.VMEM((heads, 1, block), F32),
            pltpu.VMEM((heads * 64, block), F32),
            pltpu.VMEM((own * ring, 512), F32),
            pltpu.VMEM((heads, 5, block, block), F32),
        ],
        compiler_params=pltpu.CompilerParams(vmem_limit_bytes=56 << 20),
        name="attend_back",
    )(info, span, qkv, kv, segq, segk, band, dmix, out_t, lse)


def expert_kernel(
    info_ref,
    rows_ref,
    dz_ref,
    router_ref,
    w1_ref,
    w2_ref,
    prod_ref,
    back_ref,
    rpart_ref,
    g1_ref,
    g2_ref,
    rows_t,
    dret_s,
    prob_s,
    prod_s,
    back_s,
    *,
    experts,
    groups,
    ring,
):
    step = pl.program_id(0)
    me = info_ref[2]
    lane = lax.broadcasted_iota(jnp.int32, prob_s.shape, 1)

    @pl.when(step == 0)
    def _():
        rows = rows_ref[...]
        rows_t[...] = rows.astype(F32).T.astype(BF16)
        logits = dot(rows, router_ref[...], NT)
        logits = jnp.where(lane < experts, logits, MASKED)
        expo = jnp.exp(logits - jnp.max(logits, axis=1, keepdims=True))
        probs = expo / jnp.sum(expo, axis=1, keepdims=True)
        prob_s[...] = probs
        gate = jnp.sum(jnp.where(lane == me, probs, 0.0), axis=1, keepdims=True)
        dret_s[...] = (gate * dz_ref[...].astype(F32)).astype(BF16)
        prod_s[...] = jnp.zeros_like(prod_s)
        back_s[...] = jnp.zeros_like(back_s)

    w1 = w1_ref[...]
    w2 = w2_ref[...]
    d_ret = dret_s[...]
    pre = dot(rows_ref[...], w1, NN)
    cumulative = 0.5 * (1.0 + lax.erf(pre * (1.0 / math.sqrt(2.0))))
    density = jnp.exp(-0.5 * pre * pre) * (1.0 / math.sqrt(2.0 * math.pi))
    hidden = (pre * cumulative).astype(BF16)
    d_hidden = dot(d_ret, w2, NT)
    d_pre = (d_hidden * (cumulative + pre * density)).astype(BF16)
    prod_s[...] += dot(hidden, w2, NN)
    back_s[...] += dot(d_pre, w1, NT)
    g2 = dot(hidden, d_ret, TN).astype(BF16)
    joint, share = g2_ref.shape[0], g2_ref.shape[1]
    for c in range(joint):
        g2_ref[c ^ (info_ref[1] % joint)] = g2[c * share : (c + 1) * share, :]
    g1 = dot(rows_t[...], d_pre, NN).astype(BF16)
    tall = g1.shape[0] // (groups * ring)
    for c in range(groups * ring):
        g1_ref[(c % ring) ^ info_ref[1], (c // ring) ^ info_ref[0]] = g1[
            c * tall : (c + 1) * tall, :
        ]

    @pl.when(step == pl.num_programs(0) - 1)
    def _():
        produced = prod_s[...].astype(BF16)
        prod_ref[...] = produced
        d_gate = jnp.sum(
            dz_ref[...].astype(F32) * produced.astype(F32), axis=1, keepdims=True
        )
        probs = prob_s[...]
        gate = jnp.sum(jnp.where(lane == me, probs, 0.0), axis=1, keepdims=True)
        chosen = jnp.where(lane == me, 1.0, 0.0)
        d_logits = (d_gate * probs * (chosen - gate)).astype(BF16)
        back = back_s[...].astype(BF16).astype(F32) + dot(d_logits, router_ref[...], NN)
        back_ref[...] = back.astype(BF16)
        rpart_ref[...] = dot(d_logits, rows_t[...], ((0,), (1,)))


def expert_layer(info, rows, dz, router_t, w1, w2, experts, groups, ring):
    slots, width = rows.shape
    hidden = w1.shape[1]
    devices = groups * ring
    share = hidden // devices
    joint = 1
    while (share * joint) % 128:
        joint = joint * 2
    cut = share * joint
    turns = ring // joint
    grid = (hidden // cut,)
    fixed = lambda j, info_ref: (0, 0)
    return pl.pallas_call(
        functools.partial(expert_kernel, experts=experts, groups=groups, ring=ring),
        grid_spec=pltpu.PrefetchScalarGridSpec(
            num_scalar_prefetch=1,
            grid=grid,
            in_specs=[
                pl.BlockSpec((slots, width), fixed),
                pl.BlockSpec((slots, width), fixed),
                pl.BlockSpec(router_t.shape, fixed),
                pl.BlockSpec((width, cut), lambda j, info_ref: (0, j)),
                pl.BlockSpec((cut, width), lambda j, info_ref: (j, 0)),
            ],
            out_specs=[
                pl.BlockSpec((slots, width), fixed),
                pl.BlockSpec((slots, width), fixed),
                pl.BlockSpec((router_t.shape[0], width), fixed),
                pl.BlockSpec(
                    (ring, groups, width // devices, cut), lambda j, info_ref: (0, 0, 0, j)
                ),
                pl.BlockSpec(
                    (joint, None, share, width),
                    lambda j, info_ref: (
                        (j % turns) ^ (info_ref[1] // joint),
                        (j // turns) ^ info_ref[0],
                        0,
                        0,
                    ),
                ),
            ],
            scratch_shapes=[
                pltpu.VMEM((width, slots), BF16),
                pltpu.VMEM((slots, width), BF16),
                pltpu.VMEM((slots, router_t.shape[0]), F32),
                pltpu.VMEM((slots, width), F32),
                pltpu.VMEM((slots, width), F32),
            ],
        ),
        out_shape=(
            jax.ShapeDtypeStruct((slots, width), BF16),
            jax.ShapeDtypeStruct((slots, width), BF16),
            jax.ShapeDtypeStruct((router_t.shape[0], width), F32),
            jax.ShapeDtypeStruct((ring, groups, width // devices, hidden), BF16),
            jax.ShapeDtypeStruct((ring, groups, share, width), BF16),
        ),
        compiler_params=pltpu.CompilerParams(
            dimension_semantics=("arbitrary",), vmem_limit_bytes=56 << 20
        ),
        name="experts",
    )(info, rows, dz, router_t, w1, w2)


def body(
    tokens,
    seg_ids,
    routes,
    attn_gain,
    query_key_value_weight,
    attention_output_weight,
    bias_table,
    ffn_gain,
    router_weight,
    expert_in,
    expert_out,
    out_grad,
):
    n_ctx = lax.axis_size("ctx")
    n_batch = lax.axis_size("batch")
    per, width = tokens.shape[1:]
    head_count = bias_table.shape[1]
    groups = math.gcd(head_count, n_ctx)
    ring = n_ctx // groups
    heads = head_count // groups
    part = heads * 64
    tall = query_key_value_weight.shape[0]
    ctx = lax.axis_index("ctx").astype(jnp.int32)
    zed = lax.axis_index("batch").astype(jnp.int32)
    group, own = ctx // ring, ctx % ring
    info = jnp.stack([group, own, zed])
    over_groups = lambda parts: [
        parts[m] if m == 0 else swap(parts[m], "ctx", n_ctx, ring * m) for m in range(groups)
    ]
    over_ring = lambda parts: [
        parts[m] if m == 0 else swap(parts[m], "ctx", n_ctx, m) for m in range(ring)
    ]
    over_batch = lambda parts: [
        parts[m] if m == 0 else swap(parts[m], "batch", n_batch, m) for m in range(n_batch)
    ]

    row_w = query_key_value_weight
    cuts = [
        jnp.concatenate(
            [row_w[:, k * width + g * part : k * width + (g + 1) * part] for k in range(3)], axis=1
        )
        for g in range(groups)
    ]
    cuts = over_groups(xor_order(cuts, group))
    cuts = jnp.stack(cuts)
    cuts = over_batch([cuts] * n_batch)
    cuts = jnp.stack(cuts)
    cuts = over_ring([cuts] * ring)
    cuts = xor_order(cuts, own)
    cuts = [xor_order([c[z] for z in range(n_batch)], zed) for c in cuts]
    cuts = [[xor_order([b[g] for g in range(groups)], group) for b in c] for c in cuts]
    w_head = jnp.concatenate(
        [
            cuts[r][z][g]
            for g in range(groups)
            for r in range(ring)
            for z in range(n_batch)
        ],
        axis=0,
    )
    wide = 256
    gap = jnp.zeros((width, wide - part), BF16)
    w_head = jnp.concatenate(
        [x for k in range(3) for x in (w_head[:, k * part : (k + 1) * part], gap)], axis=1
    )

    flat = tokens[0].astype(F32)
    gain1 = attn_gain.astype(F32)[None, :]
    r1 = lax.rsqrt(jnp.mean(flat * flat, axis=1, keepdims=True) + EPSILON)
    normed = (flat * r1 * gain1).astype(BF16)
    seg_row = jnp.pad(seg_ids.astype(BF16), ((0, 15), (0, width - per)))
    message = jnp.concatenate([normed, seg_row], axis=0)
    arrived = over_groups([message] * groups)
    x_all = jnp.concatenate([a[:per] for a in arrived], axis=0)
    seg_own = jnp.stack([a[per, :per] for a in arrived])

    capacity = max(2, 2 * per // n_batch)
    route_rows = routes.reshape(per)
    chosen = route_rows[:, None] == jnp.arange(n_batch, dtype=jnp.int32)[None, :]
    rank = jnp.cumsum(chosen.astype(jnp.int32), axis=0, dtype=jnp.int32) - 1
    slot = jnp.sum(jnp.where(chosen, rank, 0), axis=1, dtype=jnp.int32)
    target = route_rows * capacity + slot
    dispatch = (
        target[:, None] == jnp.arange(n_batch * capacity, dtype=jnp.int32)[None, :]
    ).astype(BF16)
    d_result = out_grad[0]

    def send(rows):
        out = dot(dispatch, rows, TN).astype(BF16).reshape(n_batch, capacity, width)
        got = lax.all_to_all(out, "batch", split_axis=0, concat_axis=0, tiled=True)
        return got.reshape(n_batch * capacity, width)

    def fetch(rows):
        rows = rows.reshape(n_batch, capacity, width)
        got = lax.all_to_all(rows, "batch", split_axis=0, concat_axis=0, tiled=True)
        return dot(dispatch, got.reshape(n_batch * capacity, width), NN)

    dz_there = send(d_result)

    lanes = 128
    both = jnp.concatenate(
        [attention_output_weight, jnp.pad(router_weight, ((0, 0), (0, lanes - n_batch)))], axis=1
    )
    both = jnp.stack(over_batch([both] * n_batch))
    both = jnp.stack(over_groups([both] * groups))
    both = over_ring([both] * ring)
    both = xor_order(both, own)
    both = [xor_order([c[g] for g in range(groups)], group) for c in both]
    both = [[xor_order([b[z] for z in range(n_batch)], zed) for b in c] for c in both]
    both = jnp.concatenate(
        [both[r][g][z] for g in range(groups) for r in range(ring) for z in range(n_batch)],
        axis=0,
    )
    w_out, router = both[:, :width], both[:, width : width + n_batch]
    router_t = jnp.pad(router.T, ((0, lanes - n_batch), (0, 0)))

    packed = dot(x_all, w_head, NN).astype(BF16)
    seg_pad = jnp.pad(seg_own, ((0, 0), (0, 2 * wide - per)))
    kv_message = jnp.concatenate([packed[:, wide:], seg_pad], axis=0)
    kv_all = over_ring([kv_message] * ring)
    seg_all = [a[groups * per :, :per] for a in kv_all]
    kv_all = jnp.concatenate([a[: groups * per] for a in kv_all], axis=0)
    seg_keys = jnp.stack(seg_all).astype(jnp.int32)
    seg_k = seg_keys.reshape(n_ctx * per, 1)
    seg_q = jnp.broadcast_to(seg_keys[0][:, None, :], (groups, 8, per))
    low = seg_keys[:, :, 0].reshape(-1)
    high = seg_keys[:, :, per - 1].reshape(-1)
    places = np.arange(n_ctx)
    ring_of, group_of = places // groups, places % groups
    natural = (group_of ^ group) * ring + (ring_of ^ own)
    meets = (low[None, :] <= high[:groups, None]) & (high[None, :] >= low[:groups, None])
    first = jnp.min(jnp.where(meets, natural[None, :], n_ctx), axis=1)
    last = jnp.max(jnp.where(meets, natural[None, :], -1), axis=1)
    span = jnp.stack([first, last + 1], axis=1).astype(jnp.int32)
    table = sum(
        jnp.where(group == g, bias_table[:, g * heads : (g + 1) * heads], 0) for g in range(groups)
    )
    onehot = band_onehot(per)
    band = jnp.einsum(
        "dbc,bh->hdc", jnp.asarray(onehot, BF16), table, preferred_element_type=F32
    )
    band = jnp.pad(band, ((0, 0), (0, 3), (0, 0)))
    out_t, mixed, lse = attend(
        info, span, packed, kv_all, seg_q, seg_k, band, heads, groups, ring, per
    )

    mixed = over_groups([mixed[m * per : (m + 1) * per] for m in range(groups)])
    mixed = jnp.concatenate(xor_order(mixed, group), axis=1)
    middle = flat + dot(mixed, w_out, NN)
    gain2 = ffn_gain.astype(F32)[None, :]
    r2 = lax.rsqrt(jnp.mean(middle * middle, axis=1, keepdims=True) + EPSILON)
    normed2 = (middle * r2 * gain2).astype(BF16)
    logits = dot(normed2, router, NN)
    probs = jax.nn.softmax(logits, axis=-1)
    gate = jnp.sum(jnp.where(chosen, probs, 0.0), axis=1, keepdims=True)

    rows_there = send(normed2)
    produced, back, router_part, g1, g2 = expert_layer(
        info, rows_there, dz_there, router_t, expert_in[0], expert_out[0], n_batch, groups, ring
    )
    d_normed2 = fetch(back)
    returned = fetch(produced)
    layer_out = (middle + gate * returned).astype(BF16)[None]

    def expert_sum(grads):
        got = over_ring([grads[m] for m in range(ring)])
        half = sum(g.astype(F32) for g in got).astype(BF16)
        got = over_groups([half[m] for m in range(groups)])
        return sum(g.astype(F32) for g in got)[None]

    expert_in_grad = expert_sum(g1)
    expert_out_grad = expert_sum(g2)

    scaled = gain2 * d_normed2
    d_middle = (
        d_result.astype(F32)
        + r2 * scaled
        - middle * (r2 * r2 * r2) * jnp.mean(scaled * middle, axis=1, keepdims=True)
    )
    ffn_gain_part = jnp.sum(d_normed2 * middle * r2, axis=0)
    d_branch = d_middle.astype(BF16)
    d_mixed = dot(d_branch, w_out, NT).astype(BF16)
    out_part = dot(mixed, d_branch, TN)
    pieces = xor_order([d_mixed[:, g * part : (g + 1) * part] for g in range(groups)], group)
    pieces = over_groups(pieces)
    d_mix = jnp.pad(jnp.concatenate(pieces, axis=0), ((0, 0), (0, wide - part)))

    dq, dkv_own, dkv_other, dband = attend_back(
        info, span, packed, kv_all, seg_q, seg_k, band, d_mix, out_t, lse, heads, groups, ring, per
    )
    rows_own = groups * per
    others = [dkv_other[m * rows_own : (m + 1) * rows_own] for m in range(ring - 1)]
    got = over_ring([dkv_own] + others)
    dkv = sum(g.astype(F32) for g in got).astype(BF16)
    d_packed = jnp.concatenate([dq, dkv], axis=1)

    d_normed = dot(d_packed, w_head, NT)
    attn_gain_part = jnp.sum(d_normed * x_all.astype(F32), axis=0) / gain1[0]
    sent = d_normed.astype(BF16)
    got = over_groups([sent[m * per : (m + 1) * per] for m in range(groups)])
    d_norm_tok = d_normed[:per] + sum(g.astype(F32) for g in got[1:])
    scaled1 = gain1 * d_norm_tok
    tokens_grad = (
        d_middle
        + r1 * scaled1
        - flat * (r1 * r1 * r1) * jnp.mean(scaled1 * flat, axis=1, keepdims=True)
    ).astype(BF16)[None]

    def weight_sum(grad, columns):
        grad = grad.reshape(groups, ring, n_batch, tall, columns)
        parts = xor_order([grad[:, r] for r in range(ring)], own)
        got = over_ring([parts[0]] + [p.astype(BF16) for p in parts[1:]])
        half = sum(g.astype(F32) for g in got)
        parts = xor_order([half[:, z] for z in range(n_batch)], zed)
        got = over_batch([parts[0]] + [p.astype(BF16) for p in parts[1:]])
        half = sum(g.astype(F32) for g in got)
        return xor_order([half[g] for g in range(groups)], group)

    packed_part = dot(x_all, d_packed, TN)
    packed_part = jnp.concatenate(
        [packed_part[:, k * wide : k * wide + part] for k in range(3)], axis=1
    )
    parts = weight_sum(packed_part, 3 * part)
    parts = over_groups([p.astype(BF16) for p in parts])
    parts = xor_order(parts, group)
    qkv_grad = jnp.concatenate(
        [p[:, k * part : (k + 1) * part] for k in range(3) for p in parts], axis=1
    ).astype(F32)
    parts = weight_sum(out_part, width)
    got = over_groups([parts[0]] + [p.astype(BF16) for p in parts[1:]])
    out_weight_grad = sum(g.astype(F32) for g in got)

    axes = (("ctx", n_ctx), ("batch", n_batch))
    router_rows = router_part[:n_batch]
    early = small_sum(jnp.concatenate([ffn_gain_part[None], router_rows], axis=0), axes)
    ffn_gain_grad = early[0]
    mine = zed + n_batch * ctx
    router_grad = lax.dynamic_slice(early[1:].T, (mine * tall, 0), (tall, n_batch))
    d_table = jnp.einsum(
        "dbc,hdc->bh",
        jnp.asarray(onehot, F32),
        dband[:, :5],
        precision=lax.Precision.HIGHEST,
        preferred_element_type=F32,
    )
    d_table = jnp.concatenate(
        [jnp.where(group == g, d_table, 0.0) for g in range(groups)], axis=1
    )
    late = small_sum(jnp.concatenate([attn_gain_part, d_table.reshape(-1)]), axes)
    attn_gain_grad = late[:width]
    bias_grad = late[width:].reshape(bias_table.shape)
    return (
        layer_out,
        tokens_grad,
        attn_gain_grad,
        qkv_grad,
        out_weight_grad,
        bias_grad,
        ffn_gain_grad,
        router_grad,
        expert_in_grad,
        expert_out_grad,
    )


def solution(mesh):
    return jax.shard_map(
        body,
        mesh=mesh,
        in_specs=(
            P("batch", "ctx", None),
            P("batch", "ctx"),
            P("ctx", "batch", None, None),
            P(),
            P(("ctx", "batch"), None),
            P(("ctx", "batch"), None),
            P(),
            P(),
            P(("ctx", "batch"), None),
            P("batch", None, None),
            P("batch", None, None),
            P("batch", "ctx", None),
        ),
        out_specs=(
            P("batch", "ctx", None),
            P("batch", "ctx", None),
            P(),
            P(("ctx", "batch"), None),
            P(("ctx", "batch"), None),
            P(),
            P(),
            P(("ctx", "batch"), None),
            P("batch", "ctx", None),
            P("batch", "ctx", None),
        ),
        check_vma=False,
    )
```

```python
import functools
import math

import jax
import jax.numpy as jnp
import numpy as np
from jax import lax
from jax.experimental import pallas as pl
from jax.experimental.pallas import tpu as pltpu
from jax.sharding import PartitionSpec as P

BUCKETS = 32
MAX_DIST = 128
EPSILON = 1e-06
MASKED = -1e30
F32 = jnp.float32
BF16 = jnp.bfloat16


def bucket_limits():
    half_span = BUCKETS // 2
    exact_span = half_span // 2
    log_levels = half_span - exact_span
    limits = []
    for level_at in range(1, log_levels):
        bound_row = exact_span
        while (
            bound_row**log_levels * exact_span**level_at
            < MAX_DIST**level_at * exact_span**log_levels
        ):
            bound_row = bound_row + 1
        limits.append(bound_row)
    return limits


def relative_bucket(offsets):
    half_span = BUCKETS // 2
    exact_span = half_span // 2
    distance = np.abs(offsets)
    far = np.full(distance.shape, exact_span, np.int32)
    for bound_row in bucket_limits():
        far = far + (distance >= bound_row).astype(np.int32)
    near = np.where(distance < exact_span, distance, far)
    return near + np.where(offsets > 0, half_span, 0)


def band_onehot(block):
    column = np.arange(2 * block)
    rows = []
    for d in range(5):
        if d in (0, 4):
            offsets = np.full((2 * block,), (d - 2) * max(block, MAX_DIST), np.int64)
        else:
            offsets = (d - 2) * block + block - column
        rows.append(relative_bucket(offsets)[None, :] == np.arange(BUCKETS)[:, None])
    return np.stack(rows)


def dot(a, b, dims, precision=None):
    return lax.dot_general(a, b, (dims, ((), ())), preferred_element_type=F32, precision=precision)


NN = ((1,), (0,))
NT = ((1,), (1,))
TN = ((0,), (0,))


def xor_order(parts, index):
    parts = list(parts)
    step = 1
    while step < len(parts):
        odd = (index // step) % 2 == 1
        parts = [jnp.where(odd, parts[i ^ step], parts[i]) for i in range(len(parts))]
        step = step * 2
    return parts


def vmem(count):
    return [pl.BlockSpec(memory_space=pltpu.VMEM)] * count


def smem(count):
    return [pl.BlockSpec(memory_space=pltpu.SMEM)] * count


def kernel_call(kernel, name, scalars, arrays, out_shape, scratch=()):
    return pl.pallas_call(
        kernel,
        out_shape=tuple(jax.ShapeDtypeStruct(shape, kind) for shape, kind in out_shape),
        in_specs=smem(len(scalars)) + vmem(len(arrays)),
        out_specs=vmem(len(out_shape)),
        scratch_shapes=[pltpu.VMEM(shape, kind) for shape, kind in scratch],
        compiler_params=pltpu.CompilerParams(vmem_limit_bytes=56 << 20),
        cost_estimate=pl.CostEstimate(flops=1, transcendentals=1, bytes_accessed=1),
        name=name,
    )(*scalars, *arrays)


def swap(value, axis, size, mask):
    return lax.ppermute(value, axis, [(i, i ^ mask) for i in range(size)])


def column(row, size):
    return jnp.broadcast_to(row, (size, row.shape[1])).T


def first_kernel(info_ref, tokens_ref, seg_ref, gain_ref, row_ref, message_ref, *cut_refs, part):
    tokens = tokens_ref[...].astype(F32)
    per, width = tokens.shape
    scale = lax.rsqrt(jnp.mean(tokens * tokens, axis=1, keepdims=True) + EPSILON)
    message_ref[:per, :] = (tokens * scale * gain_ref[...].astype(F32)).astype(BF16)
    message_ref[per:, :] = jnp.zeros((message_ref.shape[0] - per, width), BF16)
    message_ref[per:, :per] = jnp.broadcast_to(
        seg_ref[...].astype(F32), (message_ref.shape[0] - per, per)
    ).astype(BF16)
    rows = row_ref[...].astype(F32)
    groups = len(cut_refs)
    cuts = [
        jnp.concatenate(
            [rows[:, k * width + g * part : k * width + (g + 1) * part] for k in range(3)], axis=1
        )
        for g in range(groups)
    ]
    for ref, cut in zip(cut_refs, xor_order(cuts, info_ref[0])):
        ref[...] = cut.astype(BF16)


def row_place(info_ref, g, r, z, ring, batch):
    return ((g ^ info_ref[0]) * ring + (r ^ info_ref[1])) * batch + (z ^ info_ref[2])


def assemble(info_ref, piece_refs, dest_ref, groups, batch, tall):
    ring = len(piece_refs)
    for r in range(ring):
        for z in range(batch):
            for g in range(groups):
                place = row_place(info_ref, g, r, z, ring, batch)
                at = (z * groups + g) * tall
                dest_ref[pl.ds(pl.multiple_of(place * tall, 8), tall), :] = piece_refs[r][
                    at : at + tall, :
                ].astype(F32)


def project_kernel(info_ref, *refs, groups, ring, batch, tall, part, per, pieces):
    x_refs, refs = refs[:groups], refs[groups:]
    w_refs, refs = refs[:pieces], refs[pieces:]
    q_ref, kv_ref, w_out, x_out, w_s = refs
    wide = 256
    if tall % 8 == 0:
        assemble(info_ref, w_refs, w_s, groups, batch, tall)
    else:
        w_s[...] = w_refs[0][...].astype(F32)
    gap = jnp.zeros((w_s.shape[0], wide - part), BF16)
    w = jnp.concatenate(
        [x for k in range(3) for x in (w_s[:, k * part : (k + 1) * part].astype(BF16), gap)],
        axis=1,
    )
    w_out[...] = w
    kv_ref[groups * per :, :] = jnp.zeros((kv_ref.shape[0] - groups * per, 2 * wide), BF16)
    seg = jnp.concatenate([x_ref[per : per + 1, :wide].astype(F32) for x_ref in x_refs], axis=0)
    seg = jnp.concatenate(
        [seg, jnp.zeros((kv_ref.shape[0] - groups * per - groups, wide), F32)], axis=0
    )
    kv_ref[groups * per :, :wide] = seg.astype(BF16)
    for m in range(groups):
        x = x_refs[m][:per, :]
        x_out[m * per : (m + 1) * per, :] = x
        packed = dot(x, w_out[...], NN).astype(BF16)
        q_ref[m * per : (m + 1) * per, :] = packed[:, :wide]
        kv_ref[m * per : (m + 1) * per, :] = packed[:, wide:]


def slot_row(route, capacity):
    per = route.shape[1]
    earlier = lax.broadcasted_iota(jnp.int32, (per, per), 0) < lax.broadcasted_iota(
        jnp.int32, (per, per), 1
    )
    same = jnp.where((column(route, per) == route) & earlier, 1.0, 0.0)
    return route * capacity + jnp.sum(same, axis=0, keepdims=True)


def dispatch_kernel(route_ref, dz_ref, pick_ref, pick_t_ref, sent_ref, *, capacity):
    target = slot_row(route_ref[...].astype(F32), capacity).astype(jnp.int32)
    slots, per = pick_ref.shape
    slot = lax.broadcasted_iota(jnp.int32, (slots, per), 0)
    pick = jnp.where(slot == target, 1.0, 0.0)
    pick_ref[...] = pick.astype(BF16)
    pick_t_ref[...] = pick.T.astype(BF16)
    sent_ref[...] = dot(pick.astype(BF16), dz_ref[...], NN).astype(BF16)


def middle_kernel(info_ref, *refs, groups, ring, batch, tall, part, pieces, lanes):
    mixed_refs, refs = refs[:groups], refs[groups:]
    w_refs, refs = refs[:pieces], refs[pieces:]
    tokens_ref, gain_ref, pick_ref, route_ref = refs[:4]
    w_out, router_out, middle_ref, gate_ref, sent_ref, w_s = refs[4:]
    if tall % 8 == 0:
        assemble(info_ref, w_refs, w_s, groups, batch, tall)
    else:
        w_s[...] = w_refs[0][...].astype(F32)
    width = tokens_ref.shape[1]
    w_out[...] = w_s[:, :width].astype(BF16)
    router = w_s[:, width:]
    router_out[...] = router.T.astype(BF16)
    middle = tokens_ref[...].astype(F32)
    for m in range(groups):
        start = pl.multiple_of((info_ref[0] ^ m) * part, 16)
        middle += dot(mixed_refs[m][...], w_out[pl.ds(start, part), :], NN)
    middle_ref[...] = middle
    scale = lax.rsqrt(jnp.mean(middle * middle, axis=1, keepdims=True) + EPSILON)
    normed = (middle * scale * gain_ref[...].astype(F32)).astype(BF16)
    logits = dot(normed, router.astype(BF16), NN)
    lane = lax.broadcasted_iota(jnp.int32, logits.shape, 1)
    logits = jnp.where(lane < batch, logits, MASKED)
    expo = jnp.exp(logits - jnp.max(logits, axis=1, keepdims=True))
    probs = expo / jnp.sum(expo, axis=1, keepdims=True)
    route = column(route_ref[...].astype(F32), lanes).astype(jnp.int32)
    gate_ref[...] = jnp.sum(jnp.where(lane == route, probs, 0.0), axis=1, keepdims=True)
    sent_ref[...] = dot(pick_ref[...], normed, NN).astype(BF16)


def scatter_rows(info_ref, value, g, own_ref, other_refs, ring, batch, tall):
    for r in range(ring):
        for z in range(batch):
            rows = value[(r * batch + z) * tall : (r * batch + z + 1) * tall, :]
            place = z ^ info_ref[2]
            for m in range(ring):

                @pl.when((info_ref[1] ^ m) == r)
                def _():
                    if m == 0:
                        own_ref[place, g] = rows
                    else:
                        other_refs[m - 1][place, g] = rows.astype(BF16)


def branch_kernel(info_ref, back_ref, *refs, groups, ring, batch, tall, part, lanes):
    mixed_refs, refs = refs[:groups], refs[groups:]
    pick_t_ref, middle_ref, dz_ref, gain_ref, w_ref, rpart_ref = refs[:6]
    d_middle_ref, gain_part_ref = refs[6:8]
    d_mixed_refs, grad_refs = refs[8 : 8 + groups], refs[8 + groups :]
    d_normed = dot(pick_t_ref[...], back_ref[...], NN)
    middle = middle_ref[...]
    scale = lax.rsqrt(jnp.mean(middle * middle, axis=1, keepdims=True) + EPSILON)
    gain_part_ref[...] = jnp.sum(d_normed * middle * scale, axis=0, keepdims=True)
    scaled = gain_ref[...].astype(F32) * d_normed
    d_middle = (
        dz_ref[...].astype(F32)
        + scale * scaled
        - middle
        * (scale * scale * scale)
        * jnp.mean(scaled * middle, axis=1, keepdims=True)
    )
    d_middle_ref[...] = d_middle
    d_branch = d_middle.astype(BF16)
    for m in range(groups):
        start = pl.multiple_of((info_ref[0] ^ m) * part, 16)
        d_mixed_refs[m][...] = dot(d_branch, w_ref[pl.ds(start, part), :], NT).astype(BF16)
    for m in range(groups):
        start = pl.multiple_of((info_ref[0] ^ m) * part, 16)
        grad = dot(mixed_refs[m][...], d_branch, TN)
        grad = jnp.concatenate([grad, rpart_ref[pl.ds(start, part), :]], axis=1)
        if tall % 8 == 0:
            scatter_rows(info_ref, grad, m, grad_refs[0], grad_refs[1:], ring, batch, tall)
        else:
            grad_refs[0][pl.ds(start, part), :] = grad


def weight_kernel(info_ref, dq_ref, *refs, groups, ring, batch, tall, part, per):
    got_refs, refs = refs[:ring], refs[ring:]
    x_ref, dp_ref, grad_refs = refs[0], refs[1], refs[2:]
    wide = 256
    for m in range(groups):
        rows = slice(m * per, (m + 1) * per)
        dkv = got_refs[0][rows, :]
        for ref in got_refs[1:]:
            dkv += ref[rows, :].astype(F32)
        dp_ref[rows, :wide] = dq_ref[rows, :]
        dp_ref[rows, wide:] = dkv.astype(BF16)
    share = ring * batch * tall
    for g in range(groups):
        grad = dot(x_ref[:, g * share : (g + 1) * share], dp_ref[...], TN)
        grad = jnp.concatenate([grad[:, k * wide : k * wide + part] for k in range(3)], axis=1)
        if tall % 8 == 0:
            scatter_rows(
                info_ref, grad, g ^ info_ref[0], grad_refs[0], grad_refs[1:], ring, batch, tall
            )
        else:
            grad_refs[0][g * share : (g + 1) * share, :] = grad


def unproject_kernel(dp_ref, x_ref, w_ref, gain_ref, *refs, per):
    d_refs, gain_part_ref = refs[:-1], refs[-1]
    total = jnp.zeros(gain_part_ref.shape, F32)
    for m, ref in enumerate(d_refs):
        rows = slice(m * per, (m + 1) * per)
        d_normed = dot(dp_ref[rows, :], w_ref[...], NT)
        ref[...] = d_normed.astype(ref.dtype)
        total += jnp.sum(d_normed * x_ref[rows, :].astype(F32), axis=0, keepdims=True)
    gain_part_ref[...] = total / gain_ref[...].astype(F32)


def combine_kernel(got_ref, pick_t_ref, middle_ref, gate_ref, out_ref):
    returned = dot(pick_t_ref[...], got_ref[...], NN)
    out_ref[...] = (middle_ref[...] + gate_ref[...] * returned).astype(BF16)


def head_mask(value, half):
    lane = lax.broadcasted_iota(jnp.int32, value.shape, 1)
    return jnp.where((lane // 64) == half, value, jnp.zeros_like(value))


def set_bias(band_ref, bias_s, heads, block):
    for h in range(heads):
        for d in range(5):
            row = jnp.broadcast_to(band_ref[h, d : d + 1, :], (block, 2 * block))
            bias_s[h, d] = pltpu.roll(row, block, 1, stride=1, stride_axis=0)[:, :block]


def key_at(kb, info_ref, ring, groups):
    return ((kb % ring) ^ info_ref[1]) * groups + ((kb // ring) ^ info_ref[0])


def set_keys(info_ref, kv_refs, seg_s, groups, ring, block):
    rows = [ref[groups * block : groups * block + groups, :block].astype(F32) for ref in kv_refs]
    seg = jnp.concatenate(rows, axis=0)
    blocks = groups * ring
    for at in range(blocks):
        seg_s[at * block : (at + 1) * block, :] = column(seg[at : at + 1, :], 128)
    low, high = seg[:, 0:1], seg[:, block - 1 : block]
    place = lax.broadcasted_iota(jnp.int32, (blocks, 1), 0)
    natural = ((place % groups) ^ info_ref[0]) * ring + ((place // groups) ^ info_ref[1])
    natural = natural.astype(F32)
    spans = []
    for i in range(groups):
        meets = (low <= high[i : i + 1, :]) & (high >= low[i : i + 1, :])
        first = jnp.min(jnp.where(meets, natural, float(blocks)))
        last = jnp.max(jnp.where(meets, natural, -1.0))
        spans.append((first.astype(jnp.int32), last.astype(jnp.int32) + 1))
    return seg, spans


def set_mask(mask_s, seg_s, segq, start, block):
    segk = seg_s[pl.ds(start, block), :]
    for cut in range(block // 128):
        lanes = slice(cut * 128, (cut + 1) * 128)
        mask_s[:, lanes] = jnp.where(segk == segq[:, lanes], 0.0, MASKED).astype(F32)


def attend_kernel(info_ref, q_ref, *refs, heads, groups, ring, block):
    kv_refs, refs = refs[:ring], refs[ring:]
    band_ref, ot_ref, lse_ref = refs[:3]
    mixed_refs, refs = refs[3 : 3 + groups], refs[3 + groups :]
    bias_s, key_s, vt_s, seg_s, mask_s, stat_s, acc_s = refs
    wide = 256
    set_bias(band_ref, bias_s, heads, block)
    seg, spans = set_keys(info_ref, kv_refs, seg_s, groups, ring, block)
    for r in range(ring):
        for g in range(groups):
            at, rows = r * groups + g, slice(g * block, (g + 1) * block)
            key_s[at] = kv_refs[r][rows, :wide]
            vt_s[at] = kv_refs[r][rows, wide:].astype(F32).T.astype(BF16)
    for i in range(groups):
        qb = (i ^ info_ref[0]) * ring + info_ref[1]
        rows = slice(i * block, (i + 1) * block)
        segq = seg[i : i + 1, :]
        stat_s[0:heads] = jnp.full((heads, 1, block), MASKED, F32)
        stat_s[heads : 2 * heads] = jnp.zeros((heads, 1, block), F32)
        acc_s[...] = jnp.zeros_like(acc_s)

        @pl.loop(spans[i][0], spans[i][1])
        def _(kb):
            at = key_at(kb, info_ref, ring, groups)
            set_mask(mask_s, seg_s, segq, pl.multiple_of(at * block, block), block)
            d = jnp.clip(kb - qb, -2, 2) + 2
            for h in range(heads):
                lane = (h // 2) * 128
                query = head_mask(q_ref[rows, lane : lane + 128], h % 2) * 0.125
                key = key_s[at, :, lane : lane + 128]
                scores = dot(key, query.astype(BF16), NT) + bias_s[h, d] + mask_s[...]
                top = stat_s[h]
                top_next = jnp.maximum(top, jnp.max(scores, axis=0, keepdims=True))
                expo = jnp.exp(scores - top_next)
                decay = jnp.exp(top - top_next)
                stat_s[h] = top_next
                stat_s[heads + h] = stat_s[heads + h] * decay + jnp.sum(
                    expo, axis=0, keepdims=True
                )
                value_t = vt_s[at, h * 64 : (h + 1) * 64, :]
                acc_s[h] = acc_s[h] * decay + dot(value_t, expo.astype(BF16), NN)

        for h in range(heads):
            total = stat_s[heads + h]
            ot_ref[i, h * 64 : (h + 1) * 64, :] = acc_s[h] / total
            lse_ref[i, h : h + 1, :] = stat_s[h] + jnp.log(total)
        mixed_refs[i][...] = ot_ref[i].T.astype(BF16)


def attend(info, q, kv_all, band, heads, groups, ring, block):
    width = heads * 64
    return kernel_call(
        functools.partial(attend_kernel, heads=heads, groups=groups, ring=ring, block=block),
        "attend",
        [info],
        [q, *kv_all, band],
        [((groups, width, block), F32), ((groups, 8, block), F32)]
        + [((block, width), BF16)] * groups,
        [
            ((heads, 5, block, block), F32),
            ((groups * ring, block, 256), BF16),
            ((groups * ring, 256, block), BF16),
            ((groups * ring * block, 128), F32),
            ((block, block), F32),
            ((2 * heads, 1, block), F32),
            ((heads, 64, block), F32),
        ],
    )


def attend_back_kernel(info_ref, q_ref, *refs, heads, groups, ring, block):
    kv_refs, refs = refs[:ring], refs[ring:]
    band_ref, refs = refs[0], refs[1:]
    dmix_refs, refs = refs[:groups], refs[groups:]
    ot_ref, lse_ref, dq_ref, own_ref = refs[:4]
    other_refs, refs = refs[4 : 3 + ring], refs[3 + ring :]
    dband_ref, bias_s, key_s, value_s, kt_s, seg_s, mask_s, delta_s, dqt_s, dkv_s, dbias_s, dmix_s = refs
    wide = 256
    set_bias(band_ref, bias_s, heads, block)
    seg, spans = set_keys(info_ref, kv_refs, seg_s, groups, ring, block)
    for r in range(ring):
        for g in range(groups):
            at, rows = r * groups + g, slice(g * block, (g + 1) * block)
            key_s[at] = kv_refs[r][rows, :wide]
            value_s[at] = kv_refs[r][rows, wide:]
            kt_s[at] = kv_refs[r][rows, :wide].astype(F32).T.astype(BF16)
    dkv_s[...] = jnp.zeros_like(dkv_s)
    dbias_s[...] = jnp.zeros_like(dbias_s)
    spare = jnp.zeros((block, wide - heads * 64), BF16)
    for i in range(groups):
        qb = (i ^ info_ref[0]) * ring + info_ref[1]
        rows = slice(i * block, (i + 1) * block)
        segq = seg[i : i + 1, :]
        dmix_s[...] = jnp.concatenate([dmix_refs[i][...], spare], axis=1)
        dmix_t = dmix_s[...].astype(F32).T
        for h in range(heads):
            cut = slice(h * 64, (h + 1) * 64)
            delta_s[h] = jnp.sum(dmix_t[cut, :] * ot_ref[i, cut, :], axis=0, keepdims=True)
        dqt_s[...] = jnp.zeros_like(dqt_s)

        @pl.loop(spans[i][0], spans[i][1])
        def _(kb):
            at = key_at(kb, info_ref, ring, groups)
            set_mask(mask_s, seg_s, segq, pl.multiple_of(at * block, block), block)
            d = jnp.clip(kb - qb, -2, 2) + 2
            for h in range(heads):
                lane = (h // 2) * 128
                query = (head_mask(q_ref[rows, lane : lane + 128], h % 2) * 0.125).astype(BF16)
                d_out = head_mask(dmix_s[:, lane : lane + 128], h % 2)
                key = key_s[at, :, lane : lane + 128]
                value = value_s[at, :, lane : lane + 128]
                scores = dot(key, query, NT) + bias_s[h, d] + mask_s[...]
                soft = jnp.exp(scores - lse_ref[i, h : h + 1, :])
                d_soft = dot(value, d_out, NT)
                d_scores = (soft * (d_soft - delta_s[h])).astype(BF16)
                dkv_s[at, :, wide + lane : wide + lane + 128] += dot(soft.astype(BF16), d_out, NN)
                dkv_s[at, :, lane : lane + 128] += dot(d_scores, query, NN)
                dqt_s[h * 64 : (h + 1) * 64, :] += dot(
                    kt_s[at, h * 64 : (h + 1) * 64, :], d_scores, NN
                )
                dbias_s[h, d] += d_scores.astype(F32)

        pad = jnp.zeros((wide - heads * 64, block), F32)
        dq_ref[rows, :] = (jnp.concatenate([dqt_s[...], pad], axis=0) * 0.125).T.astype(BF16)
    for r in range(ring):
        for g in range(groups):
            at, rows = r * groups + g, slice(g * block, (g + 1) * block)
            if r == 0:
                own_ref[rows, :] = dkv_s[at]
            else:
                other_refs[r - 1][rows, :] = dkv_s[at].astype(BF16)
    zero = jnp.zeros((block, block), F32)
    for h in range(heads):
        for d in range(5):
            if d in (0, 4):
                tile = jnp.sum(dbias_s[h, d], axis=0, keepdims=True)
                tile = jnp.concatenate([tile, zero[:1]], axis=1)
            else:
                tile = jnp.concatenate([zero, dbias_s[h, d]], axis=1)
                tall = block
                while tall > 1:
                    tall = tall // 2
                    tile = tile[:tall] + pltpu.roll(tile[tall:], 2 * block - tall, 1)
            dband_ref[h, d : d + 1, :] = tile


def attend_back(info, q, kv_all, band, d_mix, out_t, lse, heads, groups, ring, block):
    own = groups * block
    return kernel_call(
        functools.partial(attend_back_kernel, heads=heads, groups=groups, ring=ring, block=block),
        "attend_back",
        [info],
        [q, *kv_all, band, *d_mix, out_t, lse],
        [((own, 256), BF16), ((own, 512), F32)]
        + [((own, 512), BF16)] * (ring - 1)
        + [((heads, 8, 2 * block), F32)],
        [
            ((heads, 5, block, block), F32),
            ((groups * ring, block, 256), BF16),
            ((groups * ring, block, 256), BF16),
            ((groups * ring, 256, block), BF16),
            ((groups * ring * block, 128), F32),
            ((block, block), F32),
            ((heads, 1, block), F32),
            ((heads * 64, block), F32),
            ((groups * ring, block, 512), F32),
            ((heads, 5, block, block), F32),
            ((block, 256), BF16),
        ],
    )


def expert_kernel(info_ref, *refs, experts, groups, ring):
    rows_ref, dz_ref, router_ref, w1_ref, w2_ref, prod_ref, back_ref, rpart_ref = refs[:8]
    g1_refs, g2_refs = refs[8 : 8 + ring], refs[8 + ring : 8 + 2 * ring]
    rows_t, dret_s, prob_s, prod_s, back_s = refs[8 + 2 * ring :]
    step = pl.program_id(0)
    me = info_ref[2]
    lane = lax.broadcasted_iota(jnp.int32, prob_s.shape, 1)

    @pl.when(step == 0)
    def _():
        rows = rows_ref[...]
        rows_t[...] = rows.astype(F32).T.astype(BF16)
        logits = dot(rows, router_ref[...], NT)
        logits = jnp.where(lane < experts, logits, MASKED)
        expo = jnp.exp(logits - jnp.max(logits, axis=1, keepdims=True))
        probs = expo / jnp.sum(expo, axis=1, keepdims=True)
        prob_s[...] = probs
        gate = jnp.sum(jnp.where(lane == me, probs, 0.0), axis=1, keepdims=True)
        dret_s[...] = (gate * dz_ref[...].astype(F32)).astype(BF16)
        prod_s[...] = jnp.zeros_like(prod_s)
        back_s[...] = jnp.zeros_like(back_s)

    w1 = w1_ref[...]
    w2 = w2_ref[...]
    d_ret = dret_s[...]
    pre = dot(rows_ref[...], w1, NN)
    cumulative = 0.5 * (1.0 + lax.erf(pre * (1.0 / math.sqrt(2.0))))
    density = jnp.exp(-0.5 * pre * pre) * (1.0 / math.sqrt(2.0 * math.pi))
    hidden = (pre * cumulative).astype(BF16)
    d_hidden = dot(d_ret, w2, NT)
    d_pre = (d_hidden * (cumulative + pre * density)).astype(BF16)
    prod_s[...] += dot(hidden, w2, NN)
    back_s[...] += dot(d_pre, w1, NT)
    g2 = dot(hidden, d_ret, TN).astype(BF16)
    share = g2_refs[0].shape[0]
    joint = g2.shape[0] // share
    for c in range(joint):
        where = ((step * joint + c) % ring) ^ info_ref[1]
        for m in range(ring):

            @pl.when(where == m)
            def _():
                g2_refs[m][...] = g2[c * share : (c + 1) * share, :]

    g1 = dot(rows_t[...], d_pre, NN).astype(BF16)
    tall = g1.shape[0] // (groups * ring)
    for c in range(groups * ring):
        for m in range(ring):

            @pl.when(((c % ring) ^ info_ref[1]) == m)
            def _():
                g1_refs[m][(c // ring) ^ info_ref[0]] = g1[c * tall : (c + 1) * tall, :]

    @pl.when(step == pl.num_programs(0) - 1)
    def _():
        probs = prob_s[...]
        gate = jnp.sum(jnp.where(lane == me, probs, 0.0), axis=1, keepdims=True)
        chosen = jnp.where(lane == me, 1.0, 0.0)
        produced = prod_s[...].astype(BF16)
        prod_ref[...] = produced
        d_gate = jnp.sum(
            dz_ref[...].astype(F32) * produced.astype(F32), axis=1, keepdims=True
        )
        d_logits = (d_gate * probs * (chosen - gate)).astype(BF16)
        back = back_s[...].astype(BF16).astype(F32) + dot(d_logits, router_ref[...], NN)
        back_ref[...] = back.astype(BF16)
        rpart_ref[...] = dot(rows_t[...], d_logits, NN)


def expert_layer(info, rows, dz, router_t, w1, w2, experts, groups, ring):
    slots, width = rows.shape
    lanes = router_t.shape[0]
    hidden = w1.shape[1]
    devices = groups * ring
    share = hidden // devices
    joint = 1
    while (share * joint) % 128:
        joint = joint * 2
    cut = share * joint
    grid = (hidden // cut,)
    fixed = lambda j, info_ref: (0, 0)
    piece = pl.BlockSpec((slots, width), fixed)
    return pl.pallas_call(
        functools.partial(expert_kernel, experts=experts, groups=groups, ring=ring),
        grid_spec=pltpu.PrefetchScalarGridSpec(
            num_scalar_prefetch=1,
            grid=grid,
            in_specs=[piece] * 2
            + [
                pl.BlockSpec((lanes, width), fixed),
                pl.BlockSpec((width, cut), lambda j, info_ref: (0, j)),
                pl.BlockSpec((cut, width), lambda j, info_ref: (j, 0)),
            ],
            out_specs=[piece] * 2
            + [pl.BlockSpec((width, lanes), fixed)]
            + [pl.BlockSpec((groups, width // devices, cut), lambda j, info_ref: (0, 0, j))] * ring
            + [
                pl.BlockSpec(
                    (None, share, width),
                    lambda j, info_ref: ((j * joint // ring) ^ info_ref[0], 0, 0),
                )
            ]
            * ring,
            scratch_shapes=[
                pltpu.VMEM((width, slots), BF16),
                pltpu.VMEM((slots, width), BF16),
                pltpu.VMEM((slots, lanes), F32),
                pltpu.VMEM((slots, width), F32),
                pltpu.VMEM((slots, width), F32),
            ],
        ),
        out_shape=(
            jax.ShapeDtypeStruct((slots, width), BF16),
            jax.ShapeDtypeStruct((slots, width), BF16),
            jax.ShapeDtypeStruct((width, lanes), F32),
        )
        + (jax.ShapeDtypeStruct((groups, width // devices, hidden), BF16),) * ring
        + (jax.ShapeDtypeStruct((groups, share, width), BF16),) * ring,
        compiler_params=pltpu.CompilerParams(
            dimension_semantics=("arbitrary",), vmem_limit_bytes=56 << 20
        ),
        cost_estimate=pl.CostEstimate(flops=1, transcendentals=1, bytes_accessed=1),
        name="experts",
    )(info, rows, dz, router_t, w1, w2)


def body(
    tokens,
    seg_ids,
    routes,
    attn_gain,
    query_key_value_weight,
    attention_output_weight,
    bias_table,
    ffn_gain,
    router_weight,
    expert_in,
    expert_out,
    out_grad,
):
    n_ctx = lax.axis_size("ctx")
    n_batch = lax.axis_size("batch")
    per, width = tokens.shape[1:]
    head_count = bias_table.shape[1]
    groups = math.gcd(head_count, n_ctx)
    ring = n_ctx // groups
    heads = head_count // groups
    part = heads * 64
    tall = query_key_value_weight.shape[0]
    lanes = 128
    wide = 256
    rows_own = groups * per
    capacity = max(2, 2 * per // n_batch)
    fine = tall % 8 == 0
    ctx = lax.axis_index("ctx").astype(jnp.int32)
    zed = lax.axis_index("batch").astype(jnp.int32)
    group, own = ctx // ring, ctx % ring
    info = jnp.stack([group, own, zed])

    def over_groups(parts):
        return [
            parts[m] if m == 0 else swap(parts[m], "ctx", n_ctx, ring * m) for m in range(groups)
        ]

    def over_ring(parts):
        return [parts[m] if m == 0 else swap(parts[m], "ctx", n_ctx, m) for m in range(ring)]

    def over_batch(parts):
        return [
            parts[m] if m == 0 else swap(parts[m], "batch", n_batch, m) for m in range(n_batch)
        ]

    def gather_batch(rows):
        step = 1
        while step < n_batch:
            rows = jnp.concatenate([rows, swap(rows, "batch", n_batch, step)], axis=0)
            step = step * 2
        return rows

    def turn_batch(rows):
        rows = rows.reshape(n_batch, capacity, width)
        rows = lax.all_to_all(rows, "batch", split_axis=0, concat_axis=0, tiled=True)
        return rows.reshape(n_batch * capacity, width)

    def natural(pieces, columns):
        pieces = [p.reshape(n_batch, groups, tall, columns) for p in pieces]
        pieces = xor_order(pieces, own)
        pieces = [xor_order([c[z] for z in range(n_batch)], zed) for c in pieces]
        pieces = [[xor_order([b[g] for g in range(groups)], group) for b in c] for c in pieces]
        order = [(g, r, z) for g in range(groups) for r in range(ring) for z in range(n_batch)]
        return [jnp.concatenate([pieces[r][z][g] for g, r, z in order], axis=0)]

    first = kernel_call(
        functools.partial(first_kernel, part=part),
        "first",
        [info],
        [tokens[0], seg_ids, attn_gain[None, :], query_key_value_weight],
        [((per + 16, width), BF16)] + [((tall, 3 * part), BF16)] * groups,
    )
    message, cuts = first[0], list(first[1:])
    cuts = jnp.concatenate(over_groups(cuts), axis=0)
    arrived = over_groups([message] * groups)
    cuts = gather_batch(cuts)

    route_row = routes.reshape(1, per)
    d_result = out_grad[0]
    slots = n_batch * capacity
    pick, pick_t, dz_sent = kernel_call(
        functools.partial(dispatch_kernel, capacity=capacity),
        "dispatch",
        [],
        [route_row, d_result],
        [((slots, per), BF16), ((per, slots), BF16), ((slots, width), BF16)],
    )

    both = jnp.concatenate(
        [attention_output_weight, jnp.pad(router_weight, ((0, 0), (0, lanes - n_batch)))], axis=1
    )
    both = gather_batch(both)
    arrived, cuts = lax.optimization_barrier((arrived, cuts))
    cuts = over_ring([cuts] * ring)
    cuts, dz_sent, both = lax.optimization_barrier((cuts, dz_sent, both))
    dz_there = turn_batch(dz_sent)
    both = [both] + [swap(both, "ctx", n_ctx, ring * m) for m in range(1, groups)]
    if not fine:
        cuts = natural(cuts, 3 * part)
    kv_rows = rows_own + 16
    q, kv_own, w_head, x_all = kernel_call(
        functools.partial(
            project_kernel,
            groups=groups,
            ring=ring,
            batch=n_batch,
            tall=tall,
            part=part,
            per=per,
            pieces=len(cuts),
        ),
        "project",
        [info],
        [*arrived, *cuts],
        [
            ((rows_own, wide), BF16),
            ((kv_rows, 2 * wide), BF16),
            ((width, 3 * wide), BF16),
            ((rows_own, width), BF16),
        ],
        [((width, 3 * part), F32)],
    )
    kv_all = over_ring([kv_own] * ring)

    table = sum(
        jnp.where(group == g, bias_table[:, g * heads : (g + 1) * heads], 0) for g in range(groups)
    )
    onehot = band_onehot(per)
    band = jnp.einsum("dbc,bh->hdc", jnp.asarray(onehot, BF16), table, preferred_element_type=F32)
    band = jnp.pad(band, ((0, 0), (0, 3), (0, 0)))
    out_t, lse, *mixed = attend(info, q, kv_all, band, heads, groups, ring, per)

    mixed, both, dz_there = lax.optimization_barrier((mixed, both, dz_there))
    both = jnp.stack([b.reshape(n_batch, tall, -1) for b in both], axis=1)
    both = over_ring([both.reshape(n_batch * groups * tall, -1)] * ring)
    if not fine:
        both = natural(both, width + lanes)
    mixed = over_groups(mixed)
    shapes = dict(groups=groups, ring=ring, batch=n_batch, tall=tall, part=part, lanes=lanes)
    w_out, router_t, middle, gate, rows_sent = kernel_call(
        functools.partial(middle_kernel, pieces=len(both), **shapes),
        "middle",
        [info],
        [*mixed, *both, tokens[0], ffn_gain[None, :], pick, route_row],
        [
            ((width, width), BF16),
            ((lanes, width), BF16),
            ((per, width), F32),
            ((per, 1), F32),
            ((slots, width), BF16),
        ],
        [((width, width + lanes), F32)],
    )
    rows_there = turn_batch(rows_sent)
    outs = expert_layer(
        info, rows_there, dz_there, router_t, expert_in[0], expert_out[0], n_batch, groups, ring
    )
    produced, back, router_part = outs[:3]
    g1, g2 = list(outs[3 : 3 + ring]), list(outs[3 + ring :])
    back = turn_batch(back)

    def ring_sum(grads):
        return sum(g.astype(F32) for g in over_ring(grads)).astype(BF16)

    def group_sum(got):
        return sum(g.astype(F32) for g in got)[None]

    g1, g2 = ring_sum(g1), ring_sum(g2)
    g1 = over_groups([g1[m] for m in range(groups)])
    back, g2 = lax.optimization_barrier((back, g2))
    grads_shape = (
        [((n_batch, groups, tall, width + lanes), F32)]
        + [((n_batch, groups, tall, width + lanes), BF16)] * (ring - 1)
        if fine
        else [((width, width + lanes), F32)]
    )
    d_middle, ffn_gain_part, *rest = kernel_call(
        functools.partial(branch_kernel, **shapes),
        "branch",
        [info],
        [back, *mixed, pick_t, middle, d_result, ffn_gain[None, :], w_out, router_part],
        [((per, width), F32), ((1, width), F32)] + [((per, part), BF16)] * groups + grads_shape,
    )
    d_mix, out_parts = rest[:groups], rest[groups:]
    d_mix, g1 = lax.optimization_barrier((d_mix, g1))
    d_mix = over_groups(d_mix)
    expert_in_grad = group_sum(g1)
    d_mix, g2, produced = lax.optimization_barrier((d_mix, g2, produced))
    g2 = over_groups([g2[m] for m in range(groups)])
    returned = turn_batch(produced)

    dq, dkv_own, *rest = attend_back(
        info, q, kv_all, band, d_mix, out_t, lse, heads, groups, ring, per
    )
    dkv_other, dband = rest[: ring - 1], rest[ring - 1]
    dkv_other, g2, returned = lax.optimization_barrier((dkv_other, g2, returned))
    dkv_got = over_ring([dkv_own] + dkv_other)[1:]
    expert_out_grad = group_sum(g2)

    grads_shape = (
        [((n_batch, groups, tall, 3 * part), F32)]
        + [((n_batch, groups, tall, 3 * part), BF16)] * (ring - 1)
        if fine
        else [((width, 3 * part), F32)]
    )
    d_packed, *packed_parts = kernel_call(
        functools.partial(
            weight_kernel,
            groups=groups,
            ring=ring,
            batch=n_batch,
            tall=tall,
            part=part,
            per=per,
        ),
        "weight",
        [info],
        [dq, dkv_own, *dkv_got, x_all],
        [((rows_own, 3 * wide), BF16)] + grads_shape,
    )
    *d_normed, attn_gain_part = kernel_call(
        functools.partial(unproject_kernel, per=per),
        "unproject",
        [],
        [d_packed, x_all, w_head, attn_gain[None, :]],
        [((per, width), F32)] + [((per, width), BF16)] * (groups - 1) + [((1, width), F32)],
    )
    got = over_groups(d_normed)
    d_normed = sum(g.astype(F32) for g in got)
    flat = tokens[0].astype(F32)
    gain1 = attn_gain.astype(F32)[None, :]
    r1 = lax.rsqrt(jnp.mean(flat * flat, axis=1, keepdims=True) + EPSILON)
    scaled1 = gain1 * d_normed
    tokens_grad = (
        d_middle
        + r1 * scaled1
        - flat * (r1 * r1 * r1) * jnp.mean(scaled1 * flat, axis=1, keepdims=True)
    ).astype(BF16)[None]

    def weight_sum(parts):
        if not fine:
            grad = parts[0].reshape(groups, ring, n_batch, tall, parts[0].shape[1])
            parts = xor_order([grad[:, r] for r in range(ring)], own)
            parts = [xor_order([p[:, z] for z in range(n_batch)], zed) for p in parts]
            parts = [[xor_order([z[g] for g in range(groups)], group) for z in p] for p in parts]
            parts = [jnp.stack([jnp.stack(z) for z in p]) for p in parts]
            parts = [parts[0]] + [p.astype(BF16) for p in parts[1:]]
        got = over_ring(parts)
        half = sum(g.astype(F32) for g in got)
        got = over_batch([half[0]] + [half[m].astype(BF16) for m in range(1, n_batch)])
        return sum(g.astype(F32) for g in got)

    parts = weight_sum(packed_parts)
    parts = over_groups([parts[m].astype(BF16) for m in range(groups)])
    parts = xor_order(parts, group)
    qkv_grad = jnp.concatenate(
        [p[:, k * part : (k + 1) * part] for k in range(3) for p in parts], axis=1
    ).astype(F32)
    parts = weight_sum(out_parts)
    got = over_groups([parts[0]] + [parts[m].astype(BF16) for m in range(1, groups)])
    out_grad_sum = sum(g.astype(F32) for g in got)
    out_weight_grad = out_grad_sum[:, :width]
    router_grad = out_grad_sum[:, width : width + n_batch]

    d_table = jnp.einsum(
        "dbc,hdc->bh",
        jnp.asarray(onehot, F32),
        dband[:, :5],
        precision=lax.Precision.HIGHEST,
        preferred_element_type=F32,
    )
    d_table = jnp.concatenate(
        [jnp.where(group == g, d_table, 0.0) for g in range(groups)], axis=1
    )
    late = jnp.concatenate([attn_gain_part[0], ffn_gain_part[0], d_table.reshape(-1)])
    late = jnp.pad(late, (0, -late.shape[0] % lanes)).reshape(-1, lanes)
    late = jnp.broadcast_to(late[None], (n_ctx * n_batch, *late.shape))
    late = lax.all_to_all(late, ("ctx", "batch"), split_axis=0, concat_axis=0, tiled=True)
    late = jnp.sum(late, axis=0).reshape(-1)
    attn_gain_grad = late[:width]
    ffn_gain_grad = late[width : 2 * width]
    bias_grad = late[2 * width : 2 * width + bias_table.size].reshape(bias_table.shape)
    layer_out = kernel_call(
        combine_kernel,
        "combine",
        [],
        [returned, pick_t, middle, gate],
        [((per, width), BF16)],
    )[0][None]
    return (
        layer_out,
        tokens_grad,
        attn_gain_grad,
        qkv_grad,
        out_weight_grad,
        bias_grad,
        ffn_gain_grad,
        router_grad,
        expert_in_grad,
        expert_out_grad,
    )


def solution(mesh):
    return jax.shard_map(
        body,
        mesh=mesh,
        in_specs=(
            P("batch", "ctx", None),
            P("batch", "ctx"),
            P("ctx", "batch", None, None),
            P(),
            P(("ctx", "batch"), None),
            P(("ctx", "batch"), None),
            P(),
            P(),
            P(("ctx", "batch"), None),
            P("batch", None, None),
            P("batch", None, None),
            P("batch", "ctx", None),
        ),
        out_specs=(
            P("batch", "ctx", None),
            P("batch", "ctx", None),
            P(),
            P(("ctx", "batch"), None),
            P(("ctx", "batch"), None),
            P(),
            P(),
            P(("ctx", "batch"), None),
            P("batch", "ctx", None),
            P("batch", "ctx", None),
        ),
        check_vma=False,
    )
```

```python
import functools
import math

import jax
import jax.numpy as jnp
import numpy as np
from jax import lax
from jax.experimental import pallas as pl
from jax.experimental.pallas import tpu as pltpu
from jax.sharding import PartitionSpec as P

BUCKETS = 32
MAX_DIST = 128
EPSILON = 1e-06
MASKED = -1e30
F32 = jnp.float32
BF16 = jnp.bfloat16


def bucket_limits():
    half_span = BUCKETS // 2
    exact_span = half_span // 2
    log_levels = half_span - exact_span
    limits = []
    for level_at in range(1, log_levels):
        bound_row = exact_span
        while (
            bound_row**log_levels * exact_span**level_at
            < MAX_DIST**level_at * exact_span**log_levels
        ):
            bound_row = bound_row + 1
        limits.append(bound_row)
    return limits


def relative_bucket(offsets):
    half_span = BUCKETS // 2
    exact_span = half_span // 2
    distance = np.abs(offsets)
    far = np.full(distance.shape, exact_span, np.int32)
    for bound_row in bucket_limits():
        far = far + (distance >= bound_row).astype(np.int32)
    near = np.where(distance < exact_span, distance, far)
    return near + np.where(offsets > 0, half_span, 0)


def band_buckets(block):
    column = np.arange(2 * block)
    rows = []
    for d in range(5):
        if d in (0, 4):
            offsets = np.full((2 * block,), (d - 2) * max(block, MAX_DIST), np.int64)
        else:
            offsets = (d - 2) * block + block - column
        rows.append(relative_bucket(offsets))
    return np.stack(rows)


def band_onehot(block):
    return band_buckets(block)[:, None, :] == np.arange(BUCKETS)[None, :, None]


def dot(a, b, dims, precision=None):
    return lax.dot_general(a, b, (dims, ((), ())), preferred_element_type=F32, precision=precision)


NN = ((1,), (0,))
NT = ((1,), (1,))
TN = ((0,), (0,))


def xor_order(parts, index):
    parts = list(parts)
    step = 1
    while step < len(parts):
        odd = (index // step) % 2 == 1
        parts = [jnp.where(odd, parts[i ^ step], parts[i]) for i in range(len(parts))]
        step = step * 2
    return parts


def vmem(count):
    return [pl.BlockSpec(memory_space=pltpu.VMEM)] * count


def place(ring):
    ctx = lax.axis_index("ctx").astype(jnp.int32)
    return ctx // ring, ctx % ring, lax.axis_index("batch").astype(jnp.int32)


def kernel_call(kernel, name, arrays, out_shape, scratch=()):
    return pl.pallas_call(
        kernel,
        out_shape=tuple(jax.ShapeDtypeStruct(shape, kind) for shape, kind in out_shape),
        in_specs=vmem(len(arrays)),
        out_specs=vmem(len(out_shape)),
        scratch_shapes=[
            pltpu.SMEM(shape, kind) if kind == jnp.int32 else pltpu.VMEM(shape, kind)
            for shape, kind in scratch
        ],
        compiler_params=pltpu.CompilerParams(vmem_limit_bytes=56 << 20),
        name=name,
    )(*arrays)


def swap(value, axis, size, mask):
    return lax.ppermute(value, axis, [(i, i ^ mask) for i in range(size)])


def column(row, size):
    return jnp.broadcast_to(row, (size, row.shape[1])).T


def first_kernel(tokens_ref, seg_ref, gain_ref, row_ref, message_ref, *cut_refs, part, ring):
    info = place(ring)
    tokens = tokens_ref[...].astype(F32)
    per, width = tokens.shape
    scale = lax.rsqrt(jnp.mean(tokens * tokens, axis=1, keepdims=True) + EPSILON)
    message_ref[:per, :] = (tokens * scale * gain_ref[...].astype(F32)[None, :]).astype(BF16)
    message_ref[per:, :] = jnp.zeros((message_ref.shape[0] - per, width), BF16)
    message_ref[per:, :per] = jnp.broadcast_to(
        seg_ref[...].astype(F32), (message_ref.shape[0] - per, per)
    ).astype(BF16)
    rows = row_ref[...].astype(F32)
    groups = len(cut_refs)
    cuts = [
        jnp.concatenate(
            [rows[:, k * width + g * part : k * width + (g + 1) * part] for k in range(3)], axis=1
        )
        for g in range(groups)
    ]
    for ref, cut in zip(cut_refs, xor_order(cuts, info[0])):
        ref[...] = cut.astype(BF16)


def row_place(info, g, r, z, ring, batch):
    return ((g ^ info[0]) * ring + (r ^ info[1])) * batch + (z ^ info[2])


def assemble(info, piece_refs, dest_ref, groups, batch, tall):
    ring = len(piece_refs)
    for r in range(ring):
        for z in range(batch):
            for g in range(groups):
                block = row_place(info, g, r, z, ring, batch)
                at = (z * groups + g) * tall
                dest_ref[pl.ds(pl.multiple_of(block * tall, 8), tall), :] = piece_refs[r][
                    at : at + tall, :
                ].astype(F32)


def project_kernel(*refs, groups, ring, batch, tall, part, per, pieces):
    x_refs, refs = refs[:groups], refs[groups:]
    w_refs, refs = refs[:pieces], refs[pieces:]
    q_ref, kv_ref, w_out, w_s = refs
    wide = 256
    if tall % 8 == 0:
        assemble(place(ring), w_refs, w_s, groups, batch, tall)
    else:
        w_s[...] = w_refs[0][...].astype(F32)
    gap = jnp.zeros((w_s.shape[0], wide - part), BF16)
    w = jnp.concatenate(
        [x for k in range(3) for x in (w_s[:, k * part : (k + 1) * part].astype(BF16), gap)],
        axis=1,
    )
    w_out[...] = w
    kv_ref[groups * per :, :] = jnp.zeros((kv_ref.shape[0] - groups * per, 2 * wide), BF16)
    seg = jnp.concatenate([x_ref[per : per + 1, :wide].astype(F32) for x_ref in x_refs], axis=0)
    seg = jnp.concatenate(
        [seg, jnp.zeros((kv_ref.shape[0] - groups * per - groups, wide), F32)], axis=0
    )
    kv_ref[groups * per :, :wide] = seg.astype(BF16)
    for m in range(groups):
        packed = dot(x_refs[m][:per, :], w_out[...], NN).astype(BF16)
        q_ref[m * per : (m + 1) * per, :] = packed[:, :wide]
        kv_ref[m * per : (m + 1) * per, :] = packed[:, wide:]


def slot_row(route, capacity):
    per = route.shape[1]
    earlier = lax.broadcasted_iota(jnp.int32, (per, per), 0) < lax.broadcasted_iota(
        jnp.int32, (per, per), 1
    )
    same = jnp.where((column(route, per) == route) & earlier, 1.0, 0.0)
    return route * capacity + jnp.sum(same, axis=0, keepdims=True)


def dispatch_kernel(route_ref, dz_ref, pick_ref, pick_t_ref, sent_ref, *, capacity):
    target = slot_row(route_ref[...].astype(F32), capacity).astype(jnp.int32)
    slots, per = pick_ref.shape
    slot = lax.broadcasted_iota(jnp.int32, (slots, per), 0)
    pick = jnp.where(slot == target, 1.0, 0.0)
    pick_ref[...] = pick.astype(BF16)
    pick_t_ref[...] = pick.T.astype(BF16)
    sent_ref[...] = dot(pick.astype(BF16), dz_ref[...], NN).astype(BF16)


def middle_kernel(*refs, groups, ring, batch, tall, part, capacity, pieces):
    info = place(ring)
    mixed_refs, refs = refs[:groups], refs[groups:]
    w_refs, refs = refs[:pieces], refs[pieces:]
    tokens_ref, gain_ref, pick_ref, route_ref, w_ref, middle_ref, gate_ref = refs[:7]
    sent_refs, w_s = refs[7:-1], refs[-1]
    width = tokens_ref.shape[1]
    if tall % 8 == 0:
        assemble(info, w_refs, w_s, groups, batch, tall)
    else:
        w_s[...] = w_refs[0][...].astype(F32)
    w_ref[...] = w_s[...].astype(BF16)
    middle = tokens_ref[...].astype(F32)
    for m in range(groups):
        start = pl.multiple_of((info[0] ^ m) * part, 16)
        middle += dot(mixed_refs[m][...], w_ref[pl.ds(start, part), :width], NN)
    middle_ref[...] = middle
    scale = lax.rsqrt(jnp.mean(middle * middle, axis=1, keepdims=True) + EPSILON)
    normed = (middle * scale * gain_ref[...].astype(F32)[None, :]).astype(BF16)
    for m, ref in enumerate(sent_refs):
        start = pl.multiple_of((info[2] ^ m) * capacity, capacity)
        ref[...] = dot(pick_ref[pl.ds(start, capacity), :], normed, NN).astype(BF16)
    logits = dot(normed, w_ref[:, width:], NN)
    lane = lax.broadcasted_iota(jnp.int32, logits.shape, 1)
    logits = jnp.where(lane < batch, logits, MASKED)
    expo = jnp.exp(logits - jnp.max(logits, axis=1, keepdims=True))
    probs = expo / jnp.sum(expo, axis=1, keepdims=True)
    route = column(route_ref[...].astype(F32), logits.shape[1]).astype(jnp.int32)
    gate_ref[...] = jnp.sum(jnp.where(lane == route, probs, 0.0), axis=1, keepdims=True)


def branch_kernel(back_ref, *refs, groups, ring, batch, tall, part):
    info = place(ring)
    mixed_refs, refs = refs[:groups], refs[groups:]
    pick_t_ref, middle_ref, dz_ref, gain_ref, w_ref, rpart_ref = refs[:6]
    d_middle_ref, gain_part_ref = refs[6:8]
    d_mixed_refs, grad_refs = refs[8 : 8 + groups], refs[8 + groups :]
    width = middle_ref.shape[1]
    d_normed = dot(pick_t_ref[...], back_ref[...], NN)
    middle = middle_ref[...]
    scale = lax.rsqrt(jnp.mean(middle * middle, axis=1, keepdims=True) + EPSILON)
    gain_part_ref[...] = jnp.sum(d_normed * middle * scale, axis=0, keepdims=True)
    scaled = gain_ref[...].astype(F32)[None, :] * d_normed
    d_middle = (
        dz_ref[...].astype(F32)
        + scale * scaled
        - middle
        * (scale * scale * scale)
        * jnp.mean(scaled * middle, axis=1, keepdims=True)
    )
    d_middle_ref[...] = d_middle
    d_branch = d_middle.astype(BF16)
    for m in range(groups):
        start = pl.multiple_of((info[0] ^ m) * part, 16)
        d_mixed_refs[m][...] = dot(d_branch, w_ref[pl.ds(start, part), :width], NT).astype(BF16)
    for m in range(groups):
        start = pl.multiple_of((info[0] ^ m) * part, 16)
        grad = dot(mixed_refs[m][...], d_branch, TN)
        grad = jnp.concatenate([grad, rpart_ref[pl.ds(start, part), :]], axis=1)
        if tall % 8 == 0:
            scatter_rows(info, grad, m, grad_refs, ring, batch, tall)
        else:
            grad_refs[0][pl.ds(start, part), :] = grad


def scatter_rows(info, grad, g, grad_refs, ring, batch, tall):
    for z in range(batch):
        rows = [
            grad[(r * batch + z) * tall : (r * batch + z + 1) * tall, :] for r in range(ring)
        ]
        for ref, row in zip(grad_refs, xor_order(rows, info[1])):
            ref[z ^ info[2], g] = row.astype(ref.dtype)


def weight_kernel(dq_ref, *refs, groups, ring, batch, tall, part, per):
    info = place(ring)
    got_refs, refs = refs[:ring], refs[ring:]
    x_refs, dp_ref, grad_refs, x_s = refs[:groups], refs[groups], refs[groups + 1 : -1], refs[-1]
    wide = 256
    for m in range(groups):
        rows = slice(m * per, (m + 1) * per)
        dkv = got_refs[0][rows, :]
        for ref in got_refs[1:]:
            dkv += ref[rows, :].astype(F32)
        dp_ref[rows, :wide] = dq_ref[rows, :]
        dp_ref[rows, wide:] = dkv.astype(BF16)
        x_s[rows, :] = x_refs[m][:per, :]
    share = ring * batch * tall
    for g in range(groups):
        grad = dot(x_s[:, g * share : (g + 1) * share], dp_ref[...], TN)
        grad = jnp.concatenate([grad[:, k * wide : k * wide + part] for k in range(3)], axis=1)
        if tall % 8 == 0:
            scatter_rows(info, grad, g ^ info[0], grad_refs, ring, batch, tall)
        else:
            grad_refs[0][g * share : (g + 1) * share, :] = grad


def unproject_kernel(
    dp_ref, w_ref, gain_ref, gain2_ref, table_ref, *refs, per, ring, heads, groups
):
    x_refs, d_refs, late_ref = refs[:groups], refs[groups : 2 * groups], refs[-1]
    width = gain2_ref.shape[1]
    total = jnp.zeros((1, width), F32)
    for m, ref in enumerate(d_refs):
        rows = slice(m * per, (m + 1) * per)
        d_normed = dot(dp_ref[rows, :], w_ref[...], NT)
        ref[...] = d_normed.astype(ref.dtype)
        total += jnp.sum(d_normed * x_refs[m][:per, :].astype(F32), axis=0, keepdims=True)
    total = total / gain_ref[...].astype(F32)[None, :]
    late_ref[0] = jnp.zeros(late_ref.shape[1:], F32)
    count = width // 128
    for k in range(count):
        late_ref[0, k : k + 1, :] = total[:, k * 128 : (k + 1) * 128]
        late_ref[0, count + k : count + k + 1, :] = gain2_ref[:, k * 128 : (k + 1) * 128]
    group = place(ring)[0]
    for h in range(heads):
        late_ref[0, pl.ds(2 * count + group * heads + h, 1), :] = table_ref[h : h + 1, :]
    whole = late_ref[0]

    @pl.loop(1, late_ref.shape[0])
    def _(k):
        late_ref[k] = whole


def late_kernel(got_ref, gain1_ref, gain2_ref, table_ref):
    total = jnp.sum(got_ref[...], axis=0)
    count, heads = gain1_ref.shape[0], table_ref.shape[0]
    gain1_ref[...] = total[:count, :]
    gain2_ref[...] = total[count : 2 * count, :]
    table_ref[...] = total[2 * count : 2 * count + heads, :]


def half_kernel(*refs, ring):
    total = refs[0][...]
    for ref in refs[1:ring]:
        total += ref[...].astype(F32)
    for m, ref in enumerate(refs[ring:]):
        ref[...] = total[m].astype(ref.dtype)


def quarter_kernel(*refs, batch):
    one, two = refs[0][...], refs[batch][...]
    for ref in refs[1:batch]:
        one += ref[...].astype(F32)
    for ref in refs[batch + 1 : 2 * batch]:
        two += ref[...].astype(F32)
    cut = one.shape[2]
    for m, ref in enumerate(refs[2 * batch :]):
        ref[:, :cut] = one[m].astype(BF16)
        ref[:, cut:] = two[m].astype(BF16)


def columns_kernel(*refs, groups, ring, part):
    qkv_ref, out_ref, router_ref = refs[groups:]
    cut, width = 3 * part, out_ref.shape[1]
    parts = xor_order([ref[:, :cut].astype(F32) for ref in refs[:groups]], place(ring)[0])
    qkv_ref[...] = jnp.concatenate(
        [p[:, k * part : (k + 1) * part] for k in range(3) for p in parts], axis=1
    )
    total = sum(ref[:, cut:].astype(F32) for ref in refs[:groups])
    out_ref[...] = total[:, :width]
    router_ref[...] = total[:, width:]


def tokens_kernel(*refs, groups):
    tokens_ref, gain_ref, d_middle_ref, out_ref = refs[groups:]
    d_normed = refs[0][...]
    for ref in refs[1:groups]:
        d_normed += ref[...].astype(F32)
    tokens = tokens_ref[...].astype(F32)
    scale = lax.rsqrt(jnp.mean(tokens * tokens, axis=1, keepdims=True) + EPSILON)
    scaled = gain_ref[...].astype(F32)[None, :] * d_normed
    out_ref[...] = (
        d_middle_ref[...]
        + scale * scaled
        - tokens
        * (scale * scale * scale)
        * jnp.mean(scaled * tokens, axis=1, keepdims=True)
    ).astype(BF16)


def combine_kernel(got_ref, pick_t_ref, middle_ref, gate_ref, out_ref):
    returned = dot(pick_t_ref[...], got_ref[...], NN)
    out_ref[...] = (middle_ref[...] + gate_ref[...] * returned).astype(BF16)


def merge_kernel(*refs, groups, ring):
    g1_refs, g2_refs, one_ref = refs[:ring], refs[ring : 2 * ring], refs[2 * ring]
    g1 = sum(ref[...].astype(F32) for ref in g1_refs)
    g2 = sum(ref[...].astype(F32) for ref in g2_refs)
    rows, more = g1.shape[0], one_ref.shape[0] - g1.shape[0]
    one_ref[:rows, :] = g1.astype(BF16)
    one_ref[rows:, :] = g2[:more, :].astype(BF16)
    for m, ref in enumerate(refs[2 * ring + 1 :]):

        @pl.when((pl.program_id(0) ^ place(ring)[0]) == m)
        def _():
            ref[...] = g2[more:, :].astype(BF16)


def merge(g1, g2, more):
    groups, rows, width = g1[0].shape
    ring = len(g1)
    left = g2[0].shape[1] - more
    outs = pl.pallas_call(
        functools.partial(merge_kernel, groups=groups, ring=ring),
        grid=(groups,),
        out_shape=(jax.ShapeDtypeStruct((groups, rows + more, width), BF16),)
        + (jax.ShapeDtypeStruct((left, width), BF16),) * groups,
        in_specs=[pl.BlockSpec((None, rows, width), lambda g: (g, 0, 0))] * ring
        + [pl.BlockSpec((None, left + more, width), lambda g: (g, 0, 0))] * ring,
        out_specs=[pl.BlockSpec((None, rows + more, width), lambda g: (g, 0, 0))]
        + [pl.BlockSpec((left, width), lambda g: (0, 0))] * groups,
        compiler_params=pltpu.CompilerParams(
            dimension_semantics=("arbitrary",), vmem_limit_bytes=56 << 20
        ),
        name="merge",
    )(*g1, *g2)
    return outs[0], list(outs[1:])


def finish_kernel(one_ref, *refs):
    two_refs, in_ref, out_ref = refs[:-2], *refs[-2:]
    one = jnp.sum(one_ref[...].astype(F32), axis=0)
    tall, width = in_ref.shape[0], out_ref.shape[1]
    tiles = in_ref.shape[1] // width
    for j in range(tiles):
        in_ref[:, j * width : (j + 1) * width] = one[j * tall : (j + 1) * tall, :]
    more = one.shape[0] - tiles * tall
    out_ref[:more, :] = one[tiles * tall :, :]
    out_ref[more:, :] = sum(ref[...].astype(F32) for ref in two_refs)


SEGMENTS = 8


def set_bias(band_ref, bias_s, heads, block):
    @pl.loop(0, heads)
    def _(h):
        @pl.loop(0, 5)
        def _(d):
            row = jnp.broadcast_to(band_ref[h, pl.ds(d, 1), :], (block, 2 * block))
            bias_s[h, d] = pltpu.roll(row, block, 1, stride=1, stride_axis=0)[:, :block]


def key_at(kb, info, ring, groups):
    return ((kb % ring) ^ info[1]) * groups + ((kb // ring) ^ info[0])


def set_spans(info, kv_refs, seg_s, span_s, groups, ring, block):
    rows = [ref[groups * block : groups * block + groups, :block].astype(F32) for ref in kv_refs]
    seg = jnp.concatenate(rows, axis=0)
    seg_s[...] = seg
    blocks = groups * ring
    low, high = seg[:, 0:1], seg[:, block - 1 : block]
    at = lax.broadcasted_iota(jnp.int32, (blocks, 1), 0)
    natural = (((at % groups) ^ info[0]) * ring + ((at // groups) ^ info[1])).astype(F32)
    for i in range(groups):
        meets = (low <= high[i : i + 1, :]) & (high >= low[i : i + 1, :])
        first = jnp.min(jnp.where(meets, natural, float(blocks)))
        last = jnp.max(jnp.where(meets, natural, -1.0))
        span_s[i, 0] = first.astype(jnp.int32)
        span_s[i, 1] = last.astype(jnp.int32) + 1


def with_extras(pair, half, extras):
    lane = lax.broadcasted_iota(jnp.int32, pair.shape, 1)
    kept = jnp.where(lane // 64 == half, pair, 0.0)
    spot = lane - (1 - half) * 64
    for at, extra in extras:
        if at is None:
            kept = jnp.where((spot >= 0) & (spot < SEGMENTS), extra(spot), kept)
        else:
            kept = jnp.where(spot == at, extra, kept)
    return kept


def key_extras(seg_col):
    return (None, lambda spot: jnp.where(spot.astype(F32) == seg_col, 0.0, MASKED))


def query_extras(seg_col):
    return (None, lambda spot: jnp.where(spot.astype(F32) == seg_col, 1.0, 0.0))


def three_parts(value):
    high = value.astype(BF16).astype(F32)
    middle = (value - high).astype(BF16).astype(F32)
    return high, middle, value - high - middle


def set_keys(kv_refs, seg_s, heads, groups, block, ones, key_s, turned_s, turn, value_s=None):
    wide = 256
    for r, ref in enumerate(kv_refs):

        @pl.loop(0, groups)
        def _(g):
            at, rows = r * groups + g, pl.ds(pl.multiple_of(g * block, block), block)
            seg_col = column(seg_s[pl.ds(at, 1), :], 128)
            turned_s[at] = ref[rows, turn : turn + wide].astype(F32).T.astype(BF16)
            for h in range(heads):
                lane = (h // 2) * 128
                extras = [key_extras(seg_col)] + [(SEGMENTS + n, 1.0) for n in range(ones)]
                key = with_extras(ref[rows, lane : lane + 128].astype(F32), h % 2, extras)
                key_s[at, h] = key.astype(BF16)
                if value_s is not None:
                    lane = wide + lane
                    extras = [(n, 1.0) for n in range(ones)]
                    value = with_extras(ref[rows, lane : lane + 128].astype(F32), h % 2, extras)
                    value_s[at, h] = value.astype(BF16)


def attend_kernel(q_ref, *refs, heads, groups, ring, block):
    info = place(ring)
    kv_refs, refs = refs[:ring], refs[ring:]
    band_ref, ot_ref, lse_ref = refs[:3]
    mixed_refs, refs = refs[3 : 3 + groups], refs[3 + groups :]
    bias_s, seg_s, span_s, key_s, vt_s, query_s, stat_s, acc_s = refs
    set_bias(band_ref, bias_s, heads, block)
    set_spans(info, kv_refs, seg_s, span_s, groups, ring, block)
    set_keys(kv_refs, seg_s, heads, groups, block, 0, key_s, vt_s, 256)

    @pl.loop(0, groups)
    def _(i):
        qb = (i ^ info[0]) * ring + info[1]
        rows = pl.ds(pl.multiple_of(i * block, block), block)
        seg_col = column(seg_s[pl.ds(i, 1), :], 128)
        for h in range(heads):
            lane = (h // 2) * 128
            query = q_ref[rows, lane : lane + 128].astype(F32) * 0.125
            query_s[h] = with_extras(query, h % 2, [query_extras(seg_col)]).astype(BF16)
        stat_s[0:heads] = jnp.full((heads, 1, block), MASKED, F32)
        stat_s[heads : 2 * heads] = jnp.zeros((heads, 1, block), F32)
        acc_s[...] = jnp.zeros_like(acc_s)

        @pl.loop(span_s[i, 0], span_s[i, 1])
        def _(kb):
            at = key_at(kb, info, ring, groups)
            d = jnp.clip(kb - qb, -2, 2) + 2
            scores = [dot(key_s[at, h], query_s[h], NT) + bias_s[h, d] for h in range(heads)]
            tops = [
                jnp.maximum(stat_s[h], jnp.max(scores[h], axis=0, keepdims=True))
                for h in range(heads)
            ]
            expos = [jnp.exp(scores[h] - tops[h]) for h in range(heads)]
            for h in range(heads):
                decay = jnp.exp(stat_s[h] - tops[h])
                stat_s[h] = tops[h]
                stat_s[heads + h] = stat_s[heads + h] * decay + jnp.sum(
                    expos[h], axis=0, keepdims=True
                )
                value_t = vt_s[at, h * 64 : (h + 1) * 64, :]
                acc_s[h] = acc_s[h] * decay + dot(value_t, expos[h].astype(BF16), NN)

        for h in range(heads):
            total = stat_s[heads + h]
            ot_ref[i, h * 64 : (h + 1) * 64, :] = acc_s[h] / total
            lse_ref[i, h : h + 1, :] = stat_s[h] + jnp.log(total)

    for i in range(groups):
        mixed_refs[i][...] = ot_ref[i].T.astype(BF16)


def attend(q, kv_all, band, heads, groups, ring, block):
    width = heads * 64
    return kernel_call(
        functools.partial(attend_kernel, heads=heads, groups=groups, ring=ring, block=block),
        "attend",
        [q, *kv_all, band],
        [((groups, width, block), F32), ((groups, 8, block), F32)]
        + [((block, width), BF16)] * groups,
        [
            ((heads, 5, block, block), F32),
            ((groups * ring, block), F32),
            ((groups, 2), jnp.int32),
            ((groups * ring, heads, block, 128), BF16),
            ((groups * ring, 256, block), BF16),
            ((heads, block, 128), BF16),
            ((2 * heads, 1, block), F32),
            ((heads, 64, block), F32),
        ],
    )


def attend_back_kernel(q_ref, *refs, heads, groups, ring, block):
    info = place(ring)
    kv_refs, refs = refs[:ring], refs[ring:]
    band_ref, refs = refs[0], refs[1:]
    dmix_refs, refs = refs[:groups], refs[groups:]
    ot_ref, lse_ref, dq_ref, own_ref = refs[:4]
    other_refs, refs = refs[4 : 3 + ring], refs[3 + ring :]
    dband_ref, bias_s, seg_s, span_s, key_s, value_s, kt_s, query_s, plain_s, dout_s = refs[:10]
    dplain_s, dqt_s, dkv_s, dbias_s, dmix_s = refs[10:]
    wide = 256
    blocks = groups * ring
    set_bias(band_ref, bias_s, heads, block)
    set_spans(info, kv_refs, seg_s, span_s, groups, ring, block)
    set_keys(kv_refs, seg_s, heads, groups, block, 3, key_s, kt_s, 0, value_s)
    for i in range(groups):
        dmix_s[i, :, : heads * 64] = dmix_refs[i][...].astype(F32)
        dmix_s[i, :, heads * 64 :] = jnp.zeros((block, wide - heads * 64), F32)

    @pl.loop(0, blocks)
    def _(at):
        dkv_s[at] = jnp.zeros(dkv_s.shape[1:], F32)

    @pl.loop(0, heads)
    def _(h):
        dbias_s[h] = jnp.zeros(dbias_s.shape[1:], F32)

    @pl.loop(0, groups)
    def _(i):
        qb = (i ^ info[0]) * ring + info[1]
        rows = pl.ds(pl.multiple_of(i * block, block), block)
        seg_col = column(seg_s[pl.ds(i, 1), :], 128)
        dmix = dmix_s[i]
        dmix_t = dmix.T
        for h in range(heads):
            cut, lane = slice(h * 64, (h + 1) * 64), (h // 2) * 128
            delta = jnp.sum(dmix_t[cut, :] * ot_ref[i, cut, :], axis=0, keepdims=True)
            delta = three_parts(column(-delta, 128))
            lse = three_parts(column(-lse_ref[i, h : h + 1, :], 128))
            query = q_ref[rows, lane : lane + 128].astype(F32) * 0.125
            extras = [query_extras(seg_col)] + [(SEGMENTS + n, lse[n]) for n in range(3)]
            query_s[h] = with_extras(query, h % 2, extras).astype(BF16)
            plain_s[h] = with_extras(query, h % 2, []).astype(BF16)
            d_out = dmix[:, lane : lane + 128]
            extras = [(n, delta[n]) for n in range(3)]
            dout_s[h] = with_extras(d_out, h % 2, extras).astype(BF16)
            dplain_s[h] = with_extras(d_out, h % 2, []).astype(BF16)
        dqt_s[...] = jnp.zeros_like(dqt_s)

        @pl.loop(span_s[i, 0], span_s[i, 1])
        def _(kb):
            at = key_at(kb, info, ring, groups)
            d = jnp.clip(kb - qb, -2, 2) + 2
            softs = [
                jnp.exp(dot(key_s[at, h], query_s[h], NT) + bias_s[h, d]) for h in range(heads)
            ]
            d_scores = [
                (softs[h] * dot(value_s[at, h], dout_s[h], NT)).astype(BF16) for h in range(heads)
            ]
            for h in range(heads):
                lane = (h // 2) * 128
                dkv_s[at, :, wide + lane : wide + lane + 128] += dot(
                    softs[h].astype(BF16), dplain_s[h], NN
                )
                dkv_s[at, :, lane : lane + 128] += dot(d_scores[h], plain_s[h], NN)
                dqt_s[h * 64 : (h + 1) * 64, :] += dot(
                    kt_s[at, h * 64 : (h + 1) * 64, :], d_scores[h], NN
                )
                dbias_s[h, d] += d_scores[h].astype(F32)

        pad = jnp.zeros((wide - heads * 64, block), F32)
        dq_ref[rows, :] = (jnp.concatenate([dqt_s[...], pad], axis=0) * 0.125).T.astype(BF16)

    for r in range(ring):

        @pl.loop(0, groups)
        def _(g):
            at, rows = r * groups + g, pl.ds(pl.multiple_of(g * block, block), block)
            if r == 0:
                own_ref[rows, :] = dkv_s[at]
            else:
                other_refs[r - 1][rows, :] = dkv_s[at].astype(BF16)

    buckets = band_buckets(block)
    zero = jnp.zeros((block, block), F32)
    lane = lax.broadcasted_iota(jnp.int32, (1, 128), 1)
    column_at = lax.broadcasted_iota(jnp.int32, (1, 2 * block), 1)
    dband_ref[...] = jnp.zeros_like(dband_ref)

    @pl.loop(0, heads)
    def _(h):
        table = jnp.zeros((1, 128), F32)
        for d in range(5):
            if d in (0, 4):
                tile = jnp.sum(dbias_s[h, d], axis=0, keepdims=True)
                tile = jnp.concatenate([tile, zero[:1]], axis=1)
            else:
                tile = jnp.concatenate([zero, dbias_s[h, d]], axis=1)
                tall = block
                while tall > 1:
                    tall = tall // 2
                    tile = tile[:tall] + pltpu.roll(tile[tall:], 2 * block - tall, 1)
            for bucket in sorted(set(buckets[d].tolist())):
                held = np.nonzero(buckets[d] == bucket)[0]
                keep = (column_at >= int(held[0])) & (column_at <= int(held[-1]))
                held_sum = jnp.sum(jnp.where(keep, tile, 0.0), axis=1, keepdims=True)
                table += jnp.where(lane == bucket, held_sum, 0.0)
        dband_ref[pl.ds(h, 1), :] = table


def attend_back(q, kv_all, band, d_mix, out_t, lse, heads, groups, ring, block):
    own = groups * block
    blocks = groups * ring
    return kernel_call(
        functools.partial(attend_back_kernel, heads=heads, groups=groups, ring=ring, block=block),
        "attend_back",
        [q, *kv_all, band, *d_mix, out_t, lse],
        [((own, 256), BF16), ((own, 512), F32)]
        + [((own, 512), BF16)] * (ring - 1)
        + [((8, 128), F32)],
        [((heads, 5, block, block), F32), ((blocks, block), F32), ((groups, 2), jnp.int32)]
        + [((blocks, heads, block, 128), BF16)] * 2
        + [((blocks, 256, block), BF16)]
        + [((heads, block, 128), BF16)] * 4
        + [
            ((heads * 64, block), F32),
            ((blocks, block, 512), F32),
            ((heads, 5, block, block), F32),
            ((groups, block, 256), F32),
        ],
    )


def expert_kernel(*refs, experts, ring, batch):
    info = place(ring)
    piece_refs, refs = refs[:batch], refs[batch:]
    dz_ref, router_ref, w1_ref, w2_ref = refs[:4]
    prod_ref, back_ref, rpart_ref, rows_t, dret_ref, hidden_ref, d_pre_ref = refs[4:11]
    rows_ref, prob_s, prod_s, back_s = refs[11:]
    capacity = piece_refs[0].shape[0]
    step = pl.program_id(0)
    me = info[2]
    lane = lax.broadcasted_iota(jnp.int32, prob_s.shape, 1)

    @pl.when(step == 0)
    def _():
        for m, ref in enumerate(piece_refs):
            start = pl.multiple_of((me ^ m) * capacity, capacity)
            rows_ref[pl.ds(start, capacity), :] = ref[...]
        rows = rows_ref[...]
        rows_t[...] = rows.astype(F32).T.astype(BF16)
        logits = dot(rows, router_ref[...], NN)
        logits = jnp.where(lane < experts, logits, MASKED)
        expo = jnp.exp(logits - jnp.max(logits, axis=1, keepdims=True))
        probs = expo / jnp.sum(expo, axis=1, keepdims=True)
        prob_s[...] = probs
        gate = jnp.sum(jnp.where(lane == me, probs, 0.0), axis=1, keepdims=True)
        dret_ref[...] = (gate * dz_ref[...].astype(F32)).astype(BF16)
        prod_s[...] = jnp.zeros_like(prod_s)
        back_s[...] = jnp.zeros_like(back_s)

    w1 = w1_ref[...]
    w2 = w2_ref[...]
    pre = dot(rows_ref[...], w1, NN)
    cumulative = 0.5 * (1.0 + lax.erf(pre * (1.0 / math.sqrt(2.0))))
    density = jnp.exp(-0.5 * pre * pre) * (1.0 / math.sqrt(2.0 * math.pi))
    hidden = (pre * cumulative).astype(BF16)
    d_hidden = dot(dret_ref[...], w2, NT)
    d_pre = (d_hidden * (cumulative + pre * density)).astype(BF16)
    hidden_ref[...] = hidden
    d_pre_ref[...] = d_pre
    prod_s[...] += dot(hidden, w2, NN)
    back_s[...] += dot(d_pre, w1, NT)

    @pl.when(step == pl.num_programs(0) - 1)
    def _():
        probs = prob_s[...]
        gate = jnp.sum(jnp.where(lane == me, probs, 0.0), axis=1, keepdims=True)
        chosen = jnp.where(lane == me, 1.0, 0.0)
        produced = prod_s[...].astype(BF16)
        prod_ref[...] = produced
        d_gate = jnp.sum(
            dz_ref[...].astype(F32) * produced.astype(F32), axis=1, keepdims=True
        )
        d_logits = (d_gate * probs * (chosen - gate)).astype(BF16)
        back = back_s[...].astype(BF16).astype(F32) + dot(d_logits, router_ref[...], NT)
        back_ref[...] = back.astype(BF16)
        rpart_ref[...] = dot(rows_t[...], d_logits, NN)


def expert_layer(pieces, dz, w_both, w1, w2, ring):
    batch = len(pieces)
    capacity, width = pieces[0].shape
    slots = batch * capacity
    lanes = 128
    hidden = w1.shape[1]
    cut = width
    fixed = lambda j: (0, 0)
    whole = pl.BlockSpec((slots, width), fixed)
    return pl.pallas_call(
        functools.partial(expert_kernel, experts=batch, ring=ring, batch=batch),
        grid=(hidden // cut,),
        in_specs=[pl.BlockSpec((capacity, width), fixed)] * batch
        + [
            whole,
            pl.BlockSpec((width, lanes), lambda j: (0, width // lanes)),
            pl.BlockSpec((width, cut), lambda j: (0, j)),
            pl.BlockSpec((cut, width), lambda j: (j, 0)),
        ],
        out_specs=[
            whole,
            whole,
            pl.BlockSpec((width, lanes), fixed),
            pl.BlockSpec((width, slots), fixed),
            whole,
            pl.BlockSpec((slots, cut), lambda j: (0, j)),
            pl.BlockSpec((slots, cut), lambda j: (0, j)),
        ],
        scratch_shapes=[
            pltpu.VMEM((slots, width), BF16),
            pltpu.VMEM((slots, lanes), F32),
            pltpu.VMEM((slots, width), F32),
            pltpu.VMEM((slots, width), F32),
        ],
        out_shape=(
            jax.ShapeDtypeStruct((slots, width), BF16),
            jax.ShapeDtypeStruct((slots, width), BF16),
            jax.ShapeDtypeStruct((width, lanes), F32),
            jax.ShapeDtypeStruct((width, slots), BF16),
            jax.ShapeDtypeStruct((slots, width), BF16),
            jax.ShapeDtypeStruct((slots, hidden), BF16),
            jax.ShapeDtypeStruct((slots, hidden), BF16),
        ),
        compiler_params=pltpu.CompilerParams(
            dimension_semantics=("arbitrary",), vmem_limit_bytes=56 << 20
        ),
        name="experts",
    )(*pieces, dz, w_both, w1, w2)


def expert_grad_kernel(rows_t, dret_ref, hidden_ref, d_pre_ref, *refs, groups, ring):
    info = place(ring)
    g1_refs, g2_refs = refs[:ring], refs[ring:]
    g2 = dot(hidden_ref[...], dret_ref[...], TN).astype(BF16)
    share = g2.shape[0] // ring
    parts = [g2[c * share : (c + 1) * share, :] for c in range(ring)]
    for ref, rows in zip(g2_refs, xor_order(parts, info[1])):
        ref[...] = rows
    g1 = dot(rows_t[...], d_pre_ref[...], NN).astype(BF16)
    tall = g1.shape[0] // (groups * ring)
    for g in range(groups):
        parts = [
            g1[(g * ring + c) * tall : (g * ring + c + 1) * tall, :] for c in range(ring)
        ]
        for ref, rows in zip(g1_refs, xor_order(parts, info[1])):
            ref[g] = rows


def expert_grads(rows_t, d_ret, hidden, d_pre, groups, ring):
    width, slots = rows_t.shape
    devices = groups * ring
    share = hidden.shape[1] // devices
    cut = share * ring
    tall = width // devices
    tiles = hidden.shape[1] // cut
    return pl.pallas_call(
        functools.partial(expert_grad_kernel, groups=groups, ring=ring),
        grid=(tiles,),
        in_specs=[
            pl.BlockSpec((width, slots), lambda j: (0, 0)),
            pl.BlockSpec((slots, width), lambda j: (0, 0)),
            pl.BlockSpec((slots, cut), lambda j: (0, j)),
            pl.BlockSpec((slots, cut), lambda j: (0, j)),
        ],
        out_specs=[pl.BlockSpec((groups, tall, cut), lambda j: (0, j, 0))] * ring
        + [pl.BlockSpec((None, share, width), lambda j: (j, 0, 0))] * ring,
        out_shape=(jax.ShapeDtypeStruct((groups, tiles * tall, cut), BF16),) * ring
        + (jax.ShapeDtypeStruct((groups, share, width), BF16),) * ring,
        compiler_params=pltpu.CompilerParams(
            dimension_semantics=("arbitrary",), vmem_limit_bytes=56 << 20
        ),
        name="expert_grads",
    )(rows_t, d_ret, hidden, d_pre)


def body(
    tokens,
    seg_ids,
    routes,
    attn_gain,
    query_key_value_weight,
    attention_output_weight,
    bias_table,
    ffn_gain,
    router_weight,
    expert_in,
    expert_out,
    out_grad,
):
    n_ctx = lax.axis_size("ctx")
    n_batch = lax.axis_size("batch")
    per, width = tokens.shape[1:]
    head_count = bias_table.shape[1]
    groups = math.gcd(head_count, n_ctx)
    ring = n_ctx // groups
    heads = head_count // groups
    part = heads * 64
    tall = query_key_value_weight.shape[0]
    lanes = 128
    wide = 256
    rows_own = groups * per
    capacity = max(2, 2 * per // n_batch)
    slots = n_batch * capacity
    fine = tall % 8 == 0
    ctx = lax.axis_index("ctx").astype(jnp.int32)
    zed = lax.axis_index("batch").astype(jnp.int32)
    group, own = ctx // ring, ctx % ring

    def over_groups(parts):
        return [
            parts[m] if m == 0 else swap(parts[m], "ctx", n_ctx, ring * m) for m in range(groups)
        ]

    def over_ring(parts):
        return [parts[m] if m == 0 else swap(parts[m], "ctx", n_ctx, m) for m in range(ring)]

    def over_batch(parts):
        return [
            parts[m] if m == 0 else swap(parts[m], "batch", n_batch, m) for m in range(n_batch)
        ]

    def turn_batch(rows):
        rows = rows.reshape(n_batch, capacity, width)
        rows = lax.all_to_all(rows, "batch", split_axis=0, concat_axis=0, tiled=True)
        return rows.reshape(slots, width)

    def natural(pieces, columns):
        pieces = [p.reshape(n_batch, groups, tall, columns) for p in pieces]
        pieces = xor_order(pieces, own)
        pieces = [xor_order([c[z] for z in range(n_batch)], zed) for c in pieces]
        pieces = [[xor_order([b[g] for g in range(groups)], group) for b in c] for c in pieces]
        order = [(g, r, z) for g in range(groups) for r in range(ring) for z in range(n_batch)]
        return [jnp.concatenate([pieces[r][z][g] for g, r, z in order], axis=0)]

    first = kernel_call(
        functools.partial(first_kernel, part=part, ring=ring),
        "first",
        [tokens[0], seg_ids, attn_gain, query_key_value_weight],
        [((per + 16, width), BF16)] + [((tall, 3 * part), BF16)] * groups,
    )
    message, cuts = first[0], list(first[1:])
    cuts = over_groups(cuts)
    message, cuts = lax.optimization_barrier((message, cuts))
    arrived = over_groups([message] * groups)
    both = jnp.concatenate(
        [attention_output_weight, jnp.pad(router_weight, ((0, 0), (0, lanes - n_batch)))], axis=1
    )
    cuts = jnp.concatenate(cuts, axis=0)
    step = 1
    while step < n_batch:
        cuts = jnp.concatenate([cuts, swap(cuts, "batch", n_batch, step)], axis=0)
        cuts, both = lax.optimization_barrier((cuts, both)) if step == 1 else (cuts, both)
        step = step * 2
    both = jnp.concatenate([both, swap(both, "batch", n_batch, 1)], axis=0)

    route_row = routes.reshape(1, per)
    d_result = out_grad[0]
    pick, pick_t, dz_sent = kernel_call(
        functools.partial(dispatch_kernel, capacity=capacity),
        "dispatch",
        [route_row, d_result],
        [((slots, per), BF16), ((per, slots), BF16), ((slots, width), BF16)],
    )
    table = sum(
        jnp.where(group == g, bias_table[:, g * heads : (g + 1) * heads], 0) for g in range(groups)
    )
    band = jnp.einsum(
        "dbc,bh->hdc",
        jnp.asarray(band_onehot(per), BF16),
        table,
        preferred_element_type=F32,
    )
    band = jnp.pad(band, ((0, 0), (0, 3), (0, 0)))
    arrived, cuts, dz_sent, band, both = lax.optimization_barrier(
        (arrived, cuts, dz_sent, band, both)
    )
    cuts = over_ring([cuts] * ring)
    step = 2
    while step < n_batch:
        both = jnp.concatenate([both, swap(both, "batch", n_batch, step)], axis=0)
        step = step * 2
    dz_there = turn_batch(dz_sent)
    if not fine:
        cuts = natural(cuts, 3 * part)
    kv_rows = rows_own + 16
    q, kv_own, w_head = kernel_call(
        functools.partial(
            project_kernel,
            groups=groups,
            ring=ring,
            batch=n_batch,
            tall=tall,
            part=part,
            per=per,
            pieces=len(cuts),
        ),
        "project",
        [*arrived, *cuts],
        [
            ((rows_own, wide), BF16),
            ((kv_rows, 2 * wide), BF16),
            ((width, 3 * wide), BF16),
        ],
        [((width, 3 * part), F32)],
    )
    kv_own, both = lax.optimization_barrier((kv_own, both))
    kv_all = over_ring([kv_own] * ring)
    both = over_groups([both] * groups)

    out_t, lse, *mixed = attend(q, kv_all, band, heads, groups, ring, per)

    mixed, dz_there, both = lax.optimization_barrier((mixed, dz_there, both))
    both = jnp.stack([b.reshape(n_batch, tall, width + lanes) for b in both], axis=1)
    both = over_ring([both.reshape(n_batch * groups * tall, width + lanes)] * ring)
    if not fine:
        both = natural(both, width + lanes)
    mixed = over_groups(mixed)
    both, middle, gate, *rows_sent = kernel_call(
        functools.partial(
            middle_kernel,
            groups=groups,
            ring=ring,
            batch=n_batch,
            tall=tall,
            part=part,
            capacity=capacity,
            pieces=len(both),
        ),
        "middle",
        [*mixed, *both, tokens[0], ffn_gain, pick, route_row],
        [((width, width + lanes), BF16), ((per, width), F32), ((per, 1), F32)]
        + [((capacity, width), BF16)] * n_batch,
        [((width, width + lanes), F32)],
    )
    rows_there = over_batch(rows_sent)
    produced, back, router_part, *saved = expert_layer(
        rows_there, dz_there, both, expert_in[0], expert_out[0], ring
    )
    back = turn_batch(back)
    grads = expert_grads(*saved, groups, ring)
    g1, g2 = grads[:ring], grads[ring:]

    def turn_groups(grads):
        sets = [[g * ring + r for g in range(groups)] for r in range(ring)]
        return lax.all_to_all(
            grads, "ctx", split_axis=0, concat_axis=0, tiled=True, axis_index_groups=sets
        )

    back, g1, g2 = lax.optimization_barrier((back, g1, g2))
    g1, g2 = over_ring(g1), over_ring(g2)
    grads_one, grads_two = merge(g1, g2, g2[0].shape[1] // 4)
    sums_shape = (n_batch, groups, tall, width + lanes)
    sums_shape = (
        [(sums_shape, F32)] + [(sums_shape, BF16)] * (ring - 1)
        if fine
        else [((width, width + lanes), F32)]
    )
    d_middle, ffn_gain_part, *rest = kernel_call(
        functools.partial(
            branch_kernel,
            groups=groups,
            ring=ring,
            batch=n_batch,
            tall=tall,
            part=part,
        ),
        "branch",
        [back, *mixed, pick_t, middle, d_result, ffn_gain, both, router_part],
        [((per, width), F32), ((1, width), F32)] + [((per, part), BF16)] * groups + sums_shape,
    )
    d_mix, out_parts = rest[:groups], rest[groups:]

    def by_place(parts):
        if fine:
            return parts
        grad = parts[0].reshape(groups, ring, n_batch, tall, parts[0].shape[1])
        parts = xor_order([grad[:, r] for r in range(ring)], own)
        parts = [xor_order([p[:, z] for z in range(n_batch)], zed) for p in parts]
        parts = [[xor_order([z[g] for g in range(groups)], group) for z in p] for p in parts]
        parts = [jnp.stack([jnp.stack(z) for z in p]) for p in parts]
        return [parts[0]] + [p.astype(BF16) for p in parts[1:]]

    d_mix = over_groups(d_mix)
    out_parts = over_ring(by_place(out_parts))
    d_mix, grads_one, grads_two, out_parts = lax.optimization_barrier(
        (d_mix, grads_one, grads_two, out_parts)
    )
    shape = out_parts[0].shape[1:]
    out_parts = kernel_call(
        functools.partial(half_kernel, ring=ring),
        "half_out",
        out_parts,
        [(shape, F32)] + [(shape, BF16)] * (n_batch - 1),
    )
    out_parts = over_batch(out_parts)
    grads_one = turn_groups(grads_one)

    dq, dkv_own, *rest = attend_back(
        q, kv_all, band, d_mix, out_t, lse, heads, groups, ring, per
    )
    dkv_other, table_part = rest[: ring - 1], rest[ring - 1]
    dkv_other, grads_one, grads_two, out_parts, produced = lax.optimization_barrier(
        (dkv_other, grads_one, grads_two, out_parts, produced)
    )
    dkv_got = over_ring([dkv_own] + dkv_other)[1:]
    returned = turn_batch(produced)

    grads_shape = (
        [((n_batch, groups, tall, 3 * part), F32)]
        + [((n_batch, groups, tall, 3 * part), BF16)] * (ring - 1)
        if fine
        else [((width, 3 * part), F32)]
    )
    d_packed, *packed_parts = kernel_call(
        functools.partial(
            weight_kernel,
            groups=groups,
            ring=ring,
            batch=n_batch,
            tall=tall,
            part=part,
            per=per,
        ),
        "weight",
        [dq, dkv_own, *dkv_got, *arrived],
        [((rows_own, 3 * wide), BF16)] + grads_shape,
        [((rows_own, width), BF16)],
    )
    late_rows = -(-(2 * width // lanes + head_count) // 8) * 8
    *d_normed, late = kernel_call(
        functools.partial(unproject_kernel, per=per, ring=ring, heads=heads, groups=groups),
        "unproject",
        [d_packed, w_head, attn_gain, ffn_gain_part, table_part, *arrived],
        [((per, width), F32)]
        + [((per, width), BF16)] * (groups - 1)
        + [((n_ctx * n_batch, late_rows, lanes), F32)],
    )
    packed_parts = over_ring(by_place(packed_parts))
    packed_parts, d_normed = lax.optimization_barrier((packed_parts, d_normed))
    got = over_groups(d_normed)
    shape = packed_parts[0].shape[1:]
    packed_parts = kernel_call(
        functools.partial(half_kernel, ring=ring),
        "half_packed",
        packed_parts,
        [(shape, F32)] + [(shape, BF16)] * (n_batch - 1),
    )
    grads_two, got[1] = lax.optimization_barrier((grads_two, got[1]))
    grads_two = over_groups(grads_two)
    late, returned = lax.optimization_barrier((late, returned))
    packed_parts = over_batch(packed_parts)
    layer_out = kernel_call(
        combine_kernel,
        "combine",
        [returned, pick_t, middle, gate],
        [((per, width), BF16)],
    )[0][None]
    tokens_grad = kernel_call(
        functools.partial(tokens_kernel, groups=groups),
        "tokens",
        [*got, tokens[0], attn_gain, d_middle],
        [((per, width), BF16)],
    )[0][None]
    packed_parts, layer_out, tokens_grad = lax.optimization_barrier(
        (packed_parts, layer_out, tokens_grad)
    )
    parts = kernel_call(
        functools.partial(quarter_kernel, batch=n_batch),
        "quarter",
        [*packed_parts, *out_parts],
        [((tall, 3 * part + width + lanes), BF16)] * groups,
    )

    expert_in_grad, expert_out_grad = kernel_call(
        finish_kernel,
        "finish",
        [grads_one, *grads_two],
        [
            ((width // n_ctx, expert_in.shape[2]), F32),
            ((expert_out.shape[1] // n_ctx, width), F32),
        ],
    )

    late = lax.all_to_all(late, ("ctx", "batch"), split_axis=0, concat_axis=0, tiled=True)
    attn_gain_grad, ffn_gain_grad, d_table = kernel_call(
        late_kernel,
        "late",
        [late],
        [((width // lanes, lanes), F32)] * 2 + [((head_count, lanes), F32)],
    )
    attn_gain_grad = attn_gain_grad.reshape(width)
    ffn_gain_grad = ffn_gain_grad.reshape(width)
    bias_grad = d_table[:, : bias_table.shape[0]].T
    qkv_grad, out_weight_grad, router_grad = kernel_call(
        functools.partial(columns_kernel, groups=groups, ring=ring, part=part),
        "columns",
        over_groups(parts),
        [((tall, 3 * width), F32), ((tall, width), F32), ((tall, lanes), F32)],
    )
    router_grad = router_grad[:, :n_batch]
    return (
        layer_out,
        tokens_grad,
        attn_gain_grad,
        qkv_grad,
        out_weight_grad,
        bias_grad,
        ffn_gain_grad,
        router_grad,
        expert_in_grad[None],
        expert_out_grad[None],
    )


def solution(mesh):
    return jax.shard_map(
        body,
        mesh=mesh,
        in_specs=(
            P("batch", "ctx", None),
            P("batch", "ctx"),
            P("ctx", "batch", None, None),
            P(),
            P(("ctx", "batch"), None),
            P(("ctx", "batch"), None),
            P(),
            P(),
            P(("ctx", "batch"), None),
            P("batch", None, None),
            P("batch", None, None),
            P("batch", "ctx", None),
        ),
        out_specs=(
            P("batch", "ctx", None),
            P("batch", "ctx", None),
            P(),
            P(("ctx", "batch"), None),
            P(("ctx", "batch"), None),
            P(),
            P(),
            P(("ctx", "batch"), None),
            P("batch", "ctx", None),
            P("batch", "ctx", None),
        ),
        check_vma=False,
    )
```

```python
import functools
import math

import jax
import jax.numpy as jnp
import numpy as np
from jax import lax
from jax.experimental import pallas as pl
from jax.experimental.pallas import tpu as pltpu
from jax.sharding import PartitionSpec as P

BUCKETS = 32
MAX_DIST = 128
EPSILON = 1e-06
MASKED = -1e30
F32 = jnp.float32
BF16 = jnp.bfloat16


def bucket_limits():
    half_span = BUCKETS // 2
    exact_span = half_span // 2
    log_levels = half_span - exact_span
    limits = []
    for level_at in range(1, log_levels):
        bound_row = exact_span
        while (
            bound_row**log_levels * exact_span**level_at
            < MAX_DIST**level_at * exact_span**log_levels
        ):
            bound_row = bound_row + 1
        limits.append(bound_row)
    return limits


def relative_bucket(offsets):
    half_span = BUCKETS // 2
    exact_span = half_span // 2
    distance = np.abs(offsets)
    far = np.full(distance.shape, exact_span, np.int32)
    for bound_row in bucket_limits():
        far = far + (distance >= bound_row).astype(np.int32)
    near = np.where(distance < exact_span, distance, far)
    return near + np.where(offsets > 0, half_span, 0)


def band_buckets(block):
    column = np.arange(2 * block)
    rows = []
    for d in range(5):
        if d in (0, 4):
            offsets = np.full((2 * block,), (d - 2) * max(block, MAX_DIST), np.int64)
        else:
            offsets = (d - 2) * block + block - column
        rows.append(relative_bucket(offsets))
    return np.stack(rows)


def band_onehot(block):
    return band_buckets(block)[:, None, :] == np.arange(BUCKETS)[None, :, None]


def dot(a, b, dims, precision=None):
    return lax.dot_general(a, b, (dims, ((), ())), preferred_element_type=F32, precision=precision)


NN = ((1,), (0,))
NT = ((1,), (1,))
TN = ((0,), (0,))


def xor_order(parts, index):
    parts = list(parts)
    step = 1
    while step < len(parts):
        odd = (index // step) % 2 == 1
        parts = [jnp.where(odd, parts[i ^ step], parts[i]) for i in range(len(parts))]
        step = step * 2
    return parts


def vmem(count):
    return [pl.BlockSpec(memory_space=pltpu.VMEM)] * count


def place(ring):
    ctx = lax.axis_index("ctx").astype(jnp.int32)
    return ctx // ring, ctx % ring, lax.axis_index("batch").astype(jnp.int32)


def kernel_call(kernel, name, arrays, out_shape, scratch=()):
    return pl.pallas_call(
        kernel,
        out_shape=tuple(jax.ShapeDtypeStruct(shape, kind) for shape, kind in out_shape),
        in_specs=vmem(len(arrays)),
        out_specs=vmem(len(out_shape)),
        scratch_shapes=[
            pltpu.SMEM(shape, kind) if kind == jnp.int32 else pltpu.VMEM(shape, kind)
            for shape, kind in scratch
        ],
        compiler_params=pltpu.CompilerParams(vmem_limit_bytes=56 << 20),
        name=name,
    )(*arrays)


def swap(value, axis, size, mask):
    return lax.ppermute(value, axis, [(i, i ^ mask) for i in range(size)])


def column(row, size):
    return jnp.broadcast_to(row, (size, row.shape[1])).T


def first_kernel(tokens_ref, seg_ref, gain_ref, row_ref, message_ref, *cut_refs, part, ring):
    info = place(ring)
    tokens = tokens_ref[...].astype(F32)
    per, width = tokens.shape
    scale = lax.rsqrt(jnp.mean(tokens * tokens, axis=1, keepdims=True) + EPSILON)
    message_ref[:per, :] = (tokens * scale * gain_ref[...].astype(F32)[None, :]).astype(BF16)
    message_ref[per:, :] = jnp.zeros((message_ref.shape[0] - per, width), BF16)
    message_ref[per:, :per] = jnp.broadcast_to(
        seg_ref[...].astype(F32), (message_ref.shape[0] - per, per)
    ).astype(BF16)
    rows = row_ref[...].astype(F32)
    groups = len(cut_refs)
    cuts = [
        jnp.concatenate(
            [rows[:, k * width + g * part : k * width + (g + 1) * part] for k in range(3)], axis=1
        )
        for g in range(groups)
    ]
    for ref, cut in zip(cut_refs, xor_order(cuts, info[0])):
        ref[...] = cut.astype(BF16)


def row_place(info, g, r, z, ring, batch):
    return ((g ^ info[0]) * ring + (r ^ info[1])) * batch + (z ^ info[2])


def assemble(info, piece_refs, dest_ref, groups, batch, tall):
    ring = len(piece_refs)
    for r in range(ring):
        for z in range(batch):
            for g in range(groups):
                block = row_place(info, g, r, z, ring, batch)
                at = (z * groups + g) * tall
                dest_ref[pl.ds(pl.multiple_of(block * tall, 8), tall), :] = piece_refs[r][
                    at : at + tall, :
                ].astype(F32)


def project_kernel(*refs, groups, ring, batch, tall, part, per, pieces):
    x_refs, refs = refs[:groups], refs[groups:]
    w_refs, refs = refs[:pieces], refs[pieces:]
    q_ref, kv_ref, w_out, w_s = refs
    wide = 256
    if tall % 8 == 0:
        assemble(place(ring), w_refs, w_s, groups, batch, tall)
    else:
        w_s[...] = w_refs[0][...].astype(F32)
    gap = jnp.zeros((w_s.shape[0], wide - part), BF16)
    w = jnp.concatenate(
        [x for k in range(3) for x in (w_s[:, k * part : (k + 1) * part].astype(BF16), gap)],
        axis=1,
    )
    w_out[...] = w
    kv_ref[groups * per :, :] = jnp.zeros((kv_ref.shape[0] - groups * per, 2 * wide), BF16)
    seg = jnp.concatenate([x_ref[per : per + 1, :wide].astype(F32) for x_ref in x_refs], axis=0)
    seg = jnp.concatenate(
        [seg, jnp.zeros((kv_ref.shape[0] - groups * per - groups, wide), F32)], axis=0
    )
    kv_ref[groups * per :, :wide] = seg.astype(BF16)
    for m in range(groups):
        packed = dot(x_refs[m][:per, :], w_out[...], NN).astype(BF16)
        q_ref[m * per : (m + 1) * per, :] = packed[:, :wide]
        kv_ref[m * per : (m + 1) * per, :] = packed[:, wide:]


def slot_row(route, capacity):
    per = route.shape[1]
    earlier = lax.broadcasted_iota(jnp.int32, (per, per), 0) < lax.broadcasted_iota(
        jnp.int32, (per, per), 1
    )
    same = jnp.where((column(route, per) == route) & earlier, 1.0, 0.0)
    return route * capacity + jnp.sum(same, axis=0, keepdims=True)


def dispatch_kernel(route_ref, dz_ref, pick_ref, pick_t_ref, sent_ref, *, capacity):
    target = slot_row(route_ref[...].astype(F32), capacity).astype(jnp.int32)
    slots, per = pick_ref.shape
    slot = lax.broadcasted_iota(jnp.int32, (slots, per), 0)
    pick = jnp.where(slot == target, 1.0, 0.0)
    pick_ref[...] = pick.astype(BF16)
    pick_t_ref[...] = pick.T.astype(BF16)
    sent_ref[...] = dot(pick.astype(BF16), dz_ref[...], NN).astype(BF16)


def gather_kernel(*refs, groups, ring, batch, tall):
    w_refs, w_ref, w_s = refs[:-2], refs[-2], refs[-1]
    assemble(place(ring), w_refs, w_s, groups, batch, tall)
    w_ref[...] = w_s[...].astype(BF16)


def middle_kernel(*refs, groups, ring, batch, part, capacity):
    info = place(ring)
    mixed_refs, refs = refs[:groups], refs[groups:]
    w_ref, tokens_ref, gain_ref, pick_ref, route_ref, middle_ref, gate_ref = refs[:7]
    sent_refs = refs[7:]
    width = tokens_ref.shape[1]
    middle = tokens_ref[...].astype(F32)
    for m in range(groups):
        start = pl.multiple_of((info[0] ^ m) * part, 16)
        middle += dot(mixed_refs[m][...], w_ref[pl.ds(start, part), :width], NN)
    middle_ref[...] = middle
    scale = lax.rsqrt(jnp.mean(middle * middle, axis=1, keepdims=True) + EPSILON)
    normed = (middle * scale * gain_ref[...].astype(F32)[None, :]).astype(BF16)
    for m, ref in enumerate(sent_refs):
        start = pl.multiple_of((info[2] ^ m) * capacity, capacity)
        ref[...] = dot(pick_ref[pl.ds(start, capacity), :], normed, NN).astype(BF16)
    logits = dot(normed, w_ref[:, width:], NN)
    lane = lax.broadcasted_iota(jnp.int32, logits.shape, 1)
    logits = jnp.where(lane < batch, logits, MASKED)
    expo = jnp.exp(logits - jnp.max(logits, axis=1, keepdims=True))
    probs = expo / jnp.sum(expo, axis=1, keepdims=True)
    route = column(route_ref[...].astype(F32), logits.shape[1]).astype(jnp.int32)
    gate_ref[...] = jnp.sum(jnp.where(lane == route, probs, 0.0), axis=1, keepdims=True)


def branch_kernel(back_ref, *refs, groups, ring, batch, tall, part):
    info = place(ring)
    mixed_refs, refs = refs[:groups], refs[groups:]
    pick_t_ref, middle_ref, dz_ref, gain_ref, w_ref, rpart_ref = refs[:6]
    d_middle_ref, gain_part_ref = refs[6:8]
    d_mixed_refs, grad_refs = refs[8 : 8 + groups], refs[8 + groups :]
    width = middle_ref.shape[1]
    d_normed = dot(pick_t_ref[...], back_ref[...], NN)
    middle = middle_ref[...]
    scale = lax.rsqrt(jnp.mean(middle * middle, axis=1, keepdims=True) + EPSILON)
    gain_part_ref[...] = jnp.sum(d_normed * middle * scale, axis=0, keepdims=True)
    scaled = gain_ref[...].astype(F32)[None, :] * d_normed
    d_middle = (
        dz_ref[...].astype(F32)
        + scale * scaled
        - middle
        * (scale * scale * scale)
        * jnp.mean(scaled * middle, axis=1, keepdims=True)
    )
    d_middle_ref[...] = d_middle
    d_branch = d_middle.astype(BF16)
    for m in range(groups):
        start = pl.multiple_of((info[0] ^ m) * part, 16)
        d_mixed_refs[m][...] = dot(d_branch, w_ref[pl.ds(start, part), :width], NT).astype(BF16)
    for m in range(groups):
        start = pl.multiple_of((info[0] ^ m) * part, 16)
        grad = dot(mixed_refs[m][...], d_branch, TN)
        grad = jnp.concatenate([grad, rpart_ref[pl.ds(start, part), :]], axis=1)
        if tall % 8 == 0:
            scatter_rows(info, grad, m, grad_refs, ring, batch, tall, info[2])
        else:
            grad_refs[0][pl.ds(start, part), :] = grad


def scatter_rows(info, grad, g, grad_refs, ring, batch, tall, turn):
    for z in range(batch):
        rows = [
            grad[(r * batch + z) * tall : (r * batch + z + 1) * tall, :] for r in range(ring)
        ]
        for ref, row in zip(grad_refs, xor_order(rows, info[1])):
            ref[z ^ turn, g] = row.astype(ref.dtype)


def weight_kernel(dq_ref, *refs, groups, ring, batch, tall, part, per):
    info = place(ring)
    got_refs, refs = refs[:ring], refs[ring:]
    x_refs, dp_ref, grad_refs, x_s = refs[:groups], refs[groups], refs[groups + 1 : -1], refs[-1]
    wide = 256
    for m in range(groups):
        rows = slice(m * per, (m + 1) * per)
        dkv = got_refs[0][rows, :]
        for ref in got_refs[1:]:
            dkv += ref[rows, :].astype(F32)
        dp_ref[rows, :wide] = dq_ref[rows, :]
        dp_ref[rows, wide:] = dkv.astype(BF16)
        x_s[rows, :] = x_refs[m][:per, :]
    share = ring * batch * tall
    for g in range(groups):
        grad = dot(x_s[:, g * share : (g + 1) * share], dp_ref[...], TN)
        grad = jnp.concatenate([grad[:, k * wide : k * wide + part] for k in range(3)], axis=1)
        if tall % 8 == 0:
            scatter_rows(info, grad, g ^ info[0], grad_refs, ring, batch, tall, info[2])
        else:
            grad_refs[0][g * share : (g + 1) * share, :] = grad


def unproject_kernel(
    dp_ref, w_ref, gain_ref, gain2_ref, table_ref, *refs, per, ring, heads, groups
):
    x_refs, d_refs, late_ref = refs[:groups], refs[groups : 2 * groups], refs[-1]
    width = gain2_ref.shape[1]
    total = jnp.zeros((1, width), F32)
    for m, ref in enumerate(d_refs):
        rows = slice(m * per, (m + 1) * per)
        d_normed = dot(dp_ref[rows, :], w_ref[...], NT)
        ref[...] = d_normed.astype(ref.dtype)
        total += jnp.sum(d_normed * x_refs[m][:per, :].astype(F32), axis=0, keepdims=True)
    total = total / gain_ref[...].astype(F32)[None, :]
    late_ref[0] = jnp.zeros(late_ref.shape[1:], F32)
    count = width // 128
    for k in range(count):
        late_ref[0, k : k + 1, :] = total[:, k * 128 : (k + 1) * 128]
        late_ref[0, count + k : count + k + 1, :] = gain2_ref[:, k * 128 : (k + 1) * 128]
    group = place(ring)[0]
    for h in range(heads):
        late_ref[0, pl.ds(2 * count + group * heads + h, 1), :] = table_ref[h : h + 1, :]
    whole = late_ref[0]

    @pl.loop(1, late_ref.shape[0])
    def _(k):
        late_ref[k] = whole


def late_kernel(got_ref, gain1_ref, gain2_ref, table_ref):
    total = jnp.sum(got_ref[...], axis=0)
    count, heads = gain1_ref.shape[0], table_ref.shape[0]
    gain1_ref[...] = total[:count, :]
    gain2_ref[...] = total[count : 2 * count, :]
    table_ref[...] = total[2 * count : 2 * count + heads, :]


def half_kernel(*refs, ring):
    total = refs[0][...]
    for ref in refs[1:ring]:
        total += ref[...].astype(F32)
    for m, ref in enumerate(refs[ring:]):
        ref[...] = total[m].astype(ref.dtype)


def quarter_kernel(*refs, batch):
    one, two = refs[0][...], refs[batch][...]
    for ref in refs[1:batch]:
        one += ref[...].astype(F32)
    for ref in refs[batch + 1 : 2 * batch]:
        two += ref[...].astype(F32)
    cut = one.shape[2]
    for m, ref in enumerate(refs[2 * batch :]):
        ref[:, :cut] = one[m].astype(BF16)
        ref[:, cut:] = two[m].astype(BF16)


def columns_kernel(*refs, groups, ring, part):
    qkv_ref, out_ref, router_ref = refs[groups:]
    cut, width = 3 * part, out_ref.shape[1]
    parts = xor_order([ref[:, :cut].astype(F32) for ref in refs[:groups]], place(ring)[0])
    qkv_ref[...] = jnp.concatenate(
        [p[:, k * part : (k + 1) * part] for k in range(3) for p in parts], axis=1
    )
    total = sum(ref[:, cut:].astype(F32) for ref in refs[:groups])
    out_ref[...] = total[:, :width]
    router_ref[...] = total[:, width:]


def tokens_kernel(*refs, groups):
    tokens_ref, gain_ref, d_middle_ref, out_ref = refs[groups:]
    d_normed = refs[0][...]
    for ref in refs[1:groups]:
        d_normed += ref[...].astype(F32)
    tokens = tokens_ref[...].astype(F32)
    scale = lax.rsqrt(jnp.mean(tokens * tokens, axis=1, keepdims=True) + EPSILON)
    scaled = gain_ref[...].astype(F32)[None, :] * d_normed
    out_ref[...] = (
        d_middle_ref[...]
        + scale * scaled
        - tokens
        * (scale * scale * scale)
        * jnp.mean(scaled * tokens, axis=1, keepdims=True)
    ).astype(BF16)


def combine_kernel(got_ref, pick_t_ref, middle_ref, gate_ref, out_ref):
    returned = dot(pick_t_ref[...], got_ref[...], NN)
    out_ref[...] = (middle_ref[...] + gate_ref[...] * returned).astype(BF16)


def merge_kernel(*refs, ring):
    g1_refs, g2_refs = refs[:ring], refs[ring : 2 * ring]
    own_ref, left_ref, right_ref, one_ref, two_ref = refs[2 * ring :]
    step = pl.program_id(0)
    g1 = sum(ref[...].astype(F32) for ref in g1_refs).astype(BF16)
    g2 = sum(ref[...].astype(F32) for ref in g2_refs).astype(BF16)
    rows, half = g1.shape[0], g1.shape[1] // 2

    def put(ref, cut):
        ref[:rows, :] = g1[:, cut]
        ref[rows:, :] = g2[:, cut]

    left, right = slice(0, half), slice(half, 2 * half)
    pl.when(step <= 1)(lambda: put(one_ref, left))
    pl.when((step == 1) | (step == 2))(lambda: put(two_ref, right))
    pl.when(step == 0)(lambda: put(right_ref, right))
    pl.when(step == 2)(lambda: put(left_ref, left))
    pl.when(step == 3)(lambda: put(own_ref, slice(0, 2 * half)))


def merge(g1, g2):
    groups, rows, width = g1[0].shape
    assert groups == 4
    ring = len(g1)
    tall, half = 2 * rows, width // 2
    order = lambda s: (jnp.where(s == 0, 1, jnp.where(s == 1, 3, jnp.where(s == 2, 2, 0))), 0, 0)
    block = lambda columns: pl.BlockSpec((tall, columns), lambda s: (0, 0))
    return pl.pallas_call(
        functools.partial(merge_kernel, ring=ring),
        grid=(groups,),
        out_shape=(
            jax.ShapeDtypeStruct((tall, width), BF16),
            jax.ShapeDtypeStruct((tall, half), BF16),
            jax.ShapeDtypeStruct((tall, half), BF16),
            jax.ShapeDtypeStruct((2, tall, half), BF16),
            jax.ShapeDtypeStruct((2, tall, half), BF16),
        ),
        in_specs=[pl.BlockSpec((None, rows, width), order)] * (2 * ring),
        out_specs=[
            block(width),
            block(half),
            block(half),
            pl.BlockSpec((None, tall, half), lambda s: (jnp.minimum(s, 1), 0, 0)),
            pl.BlockSpec((None, tall, half), lambda s: (jnp.where(s <= 1, 1, 0), 0, 0)),
        ],
        compiler_params=pltpu.CompilerParams(
            dimension_semantics=("arbitrary",), vmem_limit_bytes=56 << 20
        ),
        name="merge",
    )(*g1, *g2)


def fold_kernel(left_ref, right_ref, one_ref, two_ref, left_out, right_out):
    left_out[...] = (left_ref[...].astype(F32) + one_ref[...].astype(F32)).astype(BF16)
    right_out[...] = (right_ref[...].astype(F32) + two_ref[...].astype(F32)).astype(BF16)


def fold(left, right, one, two):
    tall, half = left.shape
    steps = 2
    plain = pl.BlockSpec((tall // steps, half), lambda s: (s, 0))
    second = pl.BlockSpec((None, tall // steps, half), lambda s: (1, s, 0))
    return pl.pallas_call(
        fold_kernel,
        grid=(steps,),
        out_shape=(jax.ShapeDtypeStruct((tall, half), BF16),) * 2,
        in_specs=[plain, plain, second, second],
        out_specs=[plain, plain],
        compiler_params=pltpu.CompilerParams(dimension_semantics=("arbitrary",)),
        name="fold",
    )(left, right, one, two)


def finish_kernel(own_ref, one_ref, two_ref, left_ref, right_ref, in_ref, out_ref):
    tall, width = in_ref.shape[0], out_ref.shape[1]
    half, rows = width // 2, out_ref.shape[0]
    for at, first_ref, last_ref in ((0, one_ref, left_ref), (half, two_ref, right_ref)):
        cut = slice(at, at + half)
        total = own_ref[:, cut].astype(F32) + first_ref[0].astype(F32) + last_ref[...].astype(F32)
        for j in range(in_ref.shape[1] // width):
            in_ref[:, j * width + at : j * width + at + half] = total[j * tall : (j + 1) * tall, :]
        out_ref[:, cut] = total[rows:, :]


SEGMENTS = 8


def set_bias(band_ref, bias_s, heads, block):
    @pl.loop(0, heads)
    def _(h):
        @pl.loop(0, 5)
        def _(d):
            row = jnp.broadcast_to(band_ref[h, pl.ds(d, 1), :], (block, 2 * block))
            bias_s[h, d] = pltpu.roll(row, block, 1, stride=1, stride_axis=0)[:, :block]


def key_at(kb, info, ring, groups):
    return ((kb % ring) ^ info[1]) * groups + ((kb // ring) ^ info[0])


def set_spans(info, kv_refs, seg_s, span_s, groups, ring, block):
    rows = [ref[groups * block : groups * block + groups, :block].astype(F32) for ref in kv_refs]
    seg = jnp.concatenate(rows, axis=0)
    seg_s[...] = seg
    blocks = groups * ring
    low, high = seg[:, 0:1], seg[:, block - 1 : block]
    at = lax.broadcasted_iota(jnp.int32, (blocks, 1), 0)
    natural = (((at % groups) ^ info[0]) * ring + ((at // groups) ^ info[1])).astype(F32)
    for i in range(groups):
        meets = (low <= high[i : i + 1, :]) & (high >= low[i : i + 1, :])
        first = jnp.min(jnp.where(meets, natural, float(blocks)))
        last = jnp.max(jnp.where(meets, natural, -1.0))
        span_s[i, 0] = first.astype(jnp.int32)
        span_s[i, 1] = last.astype(jnp.int32) + 1


def with_extras(pair, half, extras):
    lane = lax.broadcasted_iota(jnp.int32, pair.shape, 1)
    kept = jnp.where(lane // 64 == half, pair, 0.0)
    spot = lane - (1 - half) * 64
    for at, extra in extras:
        if at is None:
            kept = jnp.where((spot >= 0) & (spot < SEGMENTS), extra(spot), kept)
        else:
            kept = jnp.where(spot == at, extra, kept)
    return kept


def key_extras(seg_col):
    return (None, lambda spot: jnp.where(spot.astype(F32) == seg_col, 0.0, MASKED))


def query_extras(seg_col):
    return (None, lambda spot: jnp.where(spot.astype(F32) == seg_col, 1.0, 0.0))


def three_parts(value):
    high = value.astype(BF16).astype(F32)
    middle = (value - high).astype(BF16).astype(F32)
    return high, middle, value - high - middle


def set_keys(kv_refs, seg_s, heads, groups, block, ones, key_s, turned_s, turn, value_s=None):
    wide = 256
    for r, ref in enumerate(kv_refs):

        @pl.loop(0, groups)
        def _(g):
            at, rows = r * groups + g, pl.ds(pl.multiple_of(g * block, block), block)
            seg_col = column(seg_s[pl.ds(at, 1), :], 128)
            turned_s[at] = ref[rows, turn : turn + wide].astype(F32).T.astype(BF16)
            for h in range(heads):
                lane = (h // 2) * 128
                extras = [key_extras(seg_col)] + [(SEGMENTS + n, 1.0) for n in range(ones)]
                key = with_extras(ref[rows, lane : lane + 128].astype(F32), h % 2, extras)
                key_s[at, h] = key.astype(BF16)
                if value_s is not None:
                    lane = wide + lane
                    extras = [(n, 1.0) for n in range(ones)]
                    value = with_extras(ref[rows, lane : lane + 128].astype(F32), h % 2, extras)
                    value_s[at, h] = value.astype(BF16)


def two_step(first, last, start, finish, even, odd):
    start(first, even)

    @pl.loop(0, (last - first + 1) // 2)
    def _(j):
        kb = first + 2 * j
        start(jnp.minimum(kb + 1, last - 1), odd)
        finish(kb, even)

        @pl.when(kb + 1 < last)
        def _():
            start(jnp.minimum(kb + 2, last - 1), even)
            finish(kb + 1, odd)


def attend_kernel(q_ref, *refs, heads, groups, ring, block):
    info = place(ring)
    kv_refs, refs = refs[:ring], refs[ring:]
    band_ref, ot_ref, lse_ref = refs[:3]
    mixed_refs, refs = refs[3 : 3 + groups], refs[3 + groups :]
    bias_s, seg_s, span_s, key_s, vt_s, query_s, stat_s, acc_s, even_s, odd_s = refs
    set_bias(band_ref, bias_s, heads, block)
    set_spans(info, kv_refs, seg_s, span_s, groups, ring, block)
    set_keys(kv_refs, seg_s, heads, groups, block, 0, key_s, vt_s, 256)

    @pl.loop(0, groups)
    def _(i):
        qb = (i ^ info[0]) * ring + info[1]
        rows = pl.ds(pl.multiple_of(i * block, block), block)
        seg_col = column(seg_s[pl.ds(i, 1), :], 128)
        for h in range(heads):
            lane = (h // 2) * 128
            query = q_ref[rows, lane : lane + 128].astype(F32) * 0.125
            query_s[h] = with_extras(query, h % 2, [query_extras(seg_col)]).astype(BF16)
        stat_s[0:heads] = jnp.full((heads, 1, block), MASKED, F32)
        stat_s[heads : 2 * heads] = jnp.zeros((heads, 1, block), F32)
        acc_s[...] = jnp.zeros_like(acc_s)

        def start(kb, score_s):
            at = key_at(kb, info, ring, groups)
            d = jnp.clip(kb - qb, -2, 2) + 2
            for h in range(heads):
                score_s[h] = dot(key_s[at, h], query_s[h], NT) + bias_s[h, d]

        def finish(kb, score_s):
            at = key_at(kb, info, ring, groups)
            tops = [
                jnp.maximum(stat_s[h], jnp.max(score_s[h], axis=0, keepdims=True))
                for h in range(heads)
            ]
            expos = [jnp.exp(score_s[h] - tops[h]) for h in range(heads)]
            for h in range(heads):
                decay = jnp.exp(stat_s[h] - tops[h])
                stat_s[h] = tops[h]
                stat_s[heads + h] = stat_s[heads + h] * decay + jnp.sum(
                    expos[h], axis=0, keepdims=True
                )
                value_t = vt_s[at, h * 64 : (h + 1) * 64, :]
                acc_s[h] = acc_s[h] * decay + dot(value_t, expos[h].astype(BF16), NN)

        two_step(span_s[i, 0], span_s[i, 1], start, finish, even_s, odd_s)

        for h in range(heads):
            total = stat_s[heads + h]
            ot_ref[i, h * 64 : (h + 1) * 64, :] = acc_s[h] / total
            lse_ref[i, h : h + 1, :] = stat_s[h] + jnp.log(total)

    for i in range(groups):
        mixed_refs[i][...] = ot_ref[i].T.astype(BF16)


def attend(q, kv_all, band, heads, groups, ring, block):
    width = heads * 64
    return kernel_call(
        functools.partial(attend_kernel, heads=heads, groups=groups, ring=ring, block=block),
        "attend",
        [q, *kv_all, band],
        [((groups, width, block), F32), ((groups, 8, block), F32)]
        + [((block, width), BF16)] * groups,
        [
            ((heads, 5, block, block), F32),
            ((groups * ring, block), F32),
            ((groups, 2), jnp.int32),
            ((groups * ring, heads, block, 128), BF16),
            ((groups * ring, 256, block), BF16),
            ((heads, block, 128), BF16),
            ((2 * heads, 1, block), F32),
            ((heads, 64, block), F32),
            ((heads, block, block), F32),
            ((heads, block, block), F32),
        ],
    )


def attend_back_kernel(q_ref, *refs, heads, groups, ring, block):
    info = place(ring)
    kv_refs, refs = refs[:ring], refs[ring:]
    band_ref, refs = refs[0], refs[1:]
    dmix_refs, refs = refs[:groups], refs[groups:]
    ot_ref, lse_ref, dq_ref, own_ref = refs[:4]
    other_refs, refs = refs[4 : 3 + ring], refs[3 + ring :]
    dband_ref, bias_s, seg_s, span_s, key_s, value_s, kt_s, query_s, plain_s, dout_s = refs[:10]
    dplain_s, dqt_s, dkv_s, dbias_s, dmix_s = refs[10:]
    wide = 256
    blocks = groups * ring
    set_bias(band_ref, bias_s, heads, block)
    set_spans(info, kv_refs, seg_s, span_s, groups, ring, block)
    set_keys(kv_refs, seg_s, heads, groups, block, 3, key_s, kt_s, 0, value_s)
    for i in range(groups):
        dmix_s[i, :, : heads * 64] = dmix_refs[i][...].astype(F32)
        dmix_s[i, :, heads * 64 :] = jnp.zeros((block, wide - heads * 64), F32)

    @pl.loop(0, blocks)
    def _(at):
        dkv_s[at] = jnp.zeros(dkv_s.shape[1:], F32)

    @pl.loop(0, heads)
    def _(h):
        dbias_s[h] = jnp.zeros(dbias_s.shape[1:], F32)

    @pl.loop(0, groups)
    def _(i):
        qb = (i ^ info[0]) * ring + info[1]
        rows = pl.ds(pl.multiple_of(i * block, block), block)
        seg_col = column(seg_s[pl.ds(i, 1), :], 128)
        dmix = dmix_s[i]
        dmix_t = dmix.T
        for h in range(heads):
            cut, lane = slice(h * 64, (h + 1) * 64), (h // 2) * 128
            delta = jnp.sum(dmix_t[cut, :] * ot_ref[i, cut, :], axis=0, keepdims=True)
            delta = three_parts(column(-delta, 128))
            lse = three_parts(column(-lse_ref[i, h : h + 1, :], 128))
            query = q_ref[rows, lane : lane + 128].astype(F32) * 0.125
            extras = [query_extras(seg_col)] + [(SEGMENTS + n, lse[n]) for n in range(3)]
            query_s[h] = with_extras(query, h % 2, extras).astype(BF16)
            plain_s[h] = with_extras(query, h % 2, []).astype(BF16)
            d_out = dmix[:, lane : lane + 128]
            extras = [(n, delta[n]) for n in range(3)]
            dout_s[h] = with_extras(d_out, h % 2, extras).astype(BF16)
            dplain_s[h] = with_extras(d_out, h % 2, []).astype(BF16)
        dqt_s[...] = jnp.zeros_like(dqt_s)

        @pl.loop(span_s[i, 0], span_s[i, 1])
        def _(kb):
            at = key_at(kb, info, ring, groups)
            d = jnp.clip(kb - qb, -2, 2) + 2
            softs = [
                jnp.exp(dot(key_s[at, h], query_s[h], NT) + bias_s[h, d]) for h in range(heads)
            ]
            d_scores = [
                (softs[h] * dot(value_s[at, h], dout_s[h], NT)).astype(BF16) for h in range(heads)
            ]
            for h in range(heads):
                lane = (h // 2) * 128
                dkv_s[at, :, wide + lane : wide + lane + 128] += dot(
                    softs[h].astype(BF16), dplain_s[h], NN
                )
                dkv_s[at, :, lane : lane + 128] += dot(d_scores[h], plain_s[h], NN)
                dqt_s[h * 64 : (h + 1) * 64, :] += dot(
                    kt_s[at, h * 64 : (h + 1) * 64, :], d_scores[h], NN
                )
                dbias_s[h, d] += d_scores[h].astype(F32)

        pad = jnp.zeros((wide - heads * 64, block), F32)
        dq_ref[rows, :] = (jnp.concatenate([dqt_s[...], pad], axis=0) * 0.125).T.astype(BF16)

    for r in range(ring):

        @pl.loop(0, groups)
        def _(g):
            at, rows = r * groups + g, pl.ds(pl.multiple_of(g * block, block), block)
            if r == 0:
                own_ref[rows, :] = dkv_s[at]
            else:
                other_refs[r - 1][rows, :] = dkv_s[at].astype(BF16)

    buckets = band_buckets(block)
    zero = jnp.zeros((block, block), F32)
    lane = lax.broadcasted_iota(jnp.int32, (1, 128), 1)
    column_at = lax.broadcasted_iota(jnp.int32, (1, 2 * block), 1)
    dband_ref[...] = jnp.zeros_like(dband_ref)

    @pl.loop(0, heads)
    def _(h):
        table = jnp.zeros((1, 128), F32)
        for d in range(5):
            if d in (0, 4):
                tile = jnp.sum(dbias_s[h, d], axis=0, keepdims=True)
                tile = jnp.concatenate([tile, zero[:1]], axis=1)
            else:
                tile = jnp.concatenate([zero, dbias_s[h, d]], axis=1)
                tall = block
                while tall > 1:
                    tall = tall // 2
                    tile = tile[:tall] + pltpu.roll(tile[tall:], 2 * block - tall, 1)
            for bucket in sorted(set(buckets[d].tolist())):
                held = np.nonzero(buckets[d] == bucket)[0]
                keep = (column_at >= int(held[0])) & (column_at <= int(held[-1]))
                held_sum = jnp.sum(jnp.where(keep, tile, 0.0), axis=1, keepdims=True)
                table += jnp.where(lane == bucket, held_sum, 0.0)
        dband_ref[pl.ds(h, 1), :] = table


def attend_back(q, kv_all, band, d_mix, out_t, lse, heads, groups, ring, block):
    own = groups * block
    blocks = groups * ring
    return kernel_call(
        functools.partial(attend_back_kernel, heads=heads, groups=groups, ring=ring, block=block),
        "attend_back",
        [q, *kv_all, band, *d_mix, out_t, lse],
        [((own, 256), BF16), ((own, 512), F32)]
        + [((own, 512), BF16)] * (ring - 1)
        + [((8, 128), F32)],
        [((heads, 5, block, block), F32), ((blocks, block), F32), ((groups, 2), jnp.int32)]
        + [((blocks, heads, block, 128), BF16)] * 2
        + [((blocks, 256, block), BF16)]
        + [((heads, block, 128), BF16)] * 4
        + [
            ((heads * 64, block), F32),
            ((blocks, block, 512), F32),
            ((heads, 5, block, block), F32),
            ((groups, block, 256), F32),
        ],
    )


def expert_kernel(*refs, experts, ring, batch):
    info = place(ring)
    piece_refs, refs = refs[:batch], refs[batch:]
    dz_ref, router_ref, w1_ref, w2_ref = refs[:4]
    prod_ref, back_ref, d_logits_ref, rows_ref, dret_ref, hidden_ref, d_pre_ref = refs[4:11]
    prob_s, prod_s, back_s = refs[11:]
    capacity = piece_refs[0].shape[0]
    step = pl.program_id(0)
    me = info[2]
    lane = lax.broadcasted_iota(jnp.int32, prob_s.shape, 1)

    @pl.when(step == 0)
    def _():
        for m, ref in enumerate(piece_refs):
            start = pl.multiple_of((me ^ m) * capacity, capacity)
            rows_ref[pl.ds(start, capacity), :] = ref[...]
        logits = dot(rows_ref[...], router_ref[...], NN)
        logits = jnp.where(lane < experts, logits, MASKED)
        expo = jnp.exp(logits - jnp.max(logits, axis=1, keepdims=True))
        probs = expo / jnp.sum(expo, axis=1, keepdims=True)
        prob_s[...] = probs
        gate = jnp.sum(jnp.where(lane == me, probs, 0.0), axis=1, keepdims=True)
        dret_ref[...] = (gate * dz_ref[...].astype(F32)).astype(BF16)
        prod_s[...] = jnp.zeros_like(prod_s)
        back_s[...] = jnp.zeros_like(back_s)

    w1 = w1_ref[...]
    w2 = w2_ref[...]
    pre = dot(rows_ref[...], w1, NN)
    cumulative = 0.5 * (1.0 + lax.erf(pre * (1.0 / math.sqrt(2.0))))
    density = jnp.exp(-0.5 * pre * pre) * (1.0 / math.sqrt(2.0 * math.pi))
    hidden = (pre * cumulative).astype(BF16)
    d_hidden = dot(dret_ref[...], w2, NT)
    d_pre = (d_hidden * (cumulative + pre * density)).astype(BF16)
    hidden_ref[...] = hidden
    d_pre_ref[...] = d_pre
    prod_s[...] += dot(hidden, w2, NN)
    back_s[...] += dot(d_pre, w1, NT)

    @pl.when(step == pl.num_programs(0) - 1)
    def _():
        probs = prob_s[...]
        gate = jnp.sum(jnp.where(lane == me, probs, 0.0), axis=1, keepdims=True)
        chosen = jnp.where(lane == me, 1.0, 0.0)
        produced = prod_s[...].astype(BF16)
        prod_ref[...] = produced
        d_gate = jnp.sum(
            dz_ref[...].astype(F32) * produced.astype(F32), axis=1, keepdims=True
        )
        d_logits = (d_gate * probs * (chosen - gate)).astype(BF16)
        back = back_s[...].astype(BF16).astype(F32) + dot(d_logits, router_ref[...], NT)
        back_ref[...] = back.astype(BF16)
        d_logits_ref[...] = d_logits


def expert_layer(pieces, dz, w_both, w1, w2, ring):
    batch = len(pieces)
    capacity, width = pieces[0].shape
    slots = batch * capacity
    lanes = 128
    hidden = w1.shape[1]
    cut = width
    fixed = lambda j: (0, 0)
    whole = pl.BlockSpec((slots, width), fixed)
    return pl.pallas_call(
        functools.partial(expert_kernel, experts=batch, ring=ring, batch=batch),
        grid=(hidden // cut,),
        in_specs=[pl.BlockSpec((capacity, width), fixed)] * batch
        + [
            whole,
            pl.BlockSpec((width, lanes), lambda j: (0, width // lanes)),
            pl.BlockSpec((width, cut), lambda j: (0, j)),
            pl.BlockSpec((cut, width), lambda j: (j, 0)),
        ],
        out_specs=[
            whole,
            whole,
            pl.BlockSpec((slots, lanes), fixed),
            whole,
            whole,
            pl.BlockSpec((slots, cut), lambda j: (0, j)),
            pl.BlockSpec((slots, cut), lambda j: (0, j)),
        ],
        scratch_shapes=[
            pltpu.VMEM((slots, lanes), F32),
            pltpu.VMEM((slots, width), F32),
            pltpu.VMEM((slots, width), F32),
        ],
        out_shape=(
            jax.ShapeDtypeStruct((slots, width), BF16),
            jax.ShapeDtypeStruct((slots, width), BF16),
            jax.ShapeDtypeStruct((slots, lanes), BF16),
            jax.ShapeDtypeStruct((slots, width), BF16),
            jax.ShapeDtypeStruct((slots, width), BF16),
            jax.ShapeDtypeStruct((slots, hidden), BF16),
            jax.ShapeDtypeStruct((slots, hidden), BF16),
        ),
        compiler_params=pltpu.CompilerParams(
            dimension_semantics=("arbitrary",), vmem_limit_bytes=56 << 20
        ),
        name="experts",
    )(*pieces, dz, w_both, w1, w2)


def expert_grad_kernel(
    d_logits_ref, rows_ref, dret_ref, hidden_ref, d_pre_ref, *refs, groups, ring
):
    info = place(ring)
    router_ref, g1_refs, g2_refs, rows_t = refs[0], refs[1 : 1 + ring], refs[1 + ring : -1], refs[-1]

    @pl.when(pl.program_id(0) == 0)
    def _():
        rows_t[...] = rows_ref[...].astype(F32).T.astype(BF16)
        router_ref[...] = dot(rows_t[...], d_logits_ref[...], NN)

    g2 = dot(hidden_ref[...], dret_ref[...], TN).astype(BF16)
    share = g2.shape[0] // ring
    parts = [g2[c * share : (c + 1) * share, :] for c in range(ring)]
    for ref, rows in zip(g2_refs, xor_order(parts, info[1])):
        ref[pl.program_id(0) ^ info[0]] = rows
    g1 = dot(rows_t[...], d_pre_ref[...], NN).astype(BF16)
    tall = g1.shape[0] // (groups * ring)
    for g in range(groups):
        parts = [
            g1[(g * ring + c) * tall : (g * ring + c + 1) * tall, :] for c in range(ring)
        ]
        for ref, rows in zip(g1_refs, xor_order(parts, info[1])):
            ref[g ^ info[0]] = rows


def expert_grads(d_logits, rows, d_ret, hidden, d_pre, groups, ring):
    slots, width = rows.shape
    lanes = d_logits.shape[1]
    devices = groups * ring
    share = hidden.shape[1] // devices
    cut = share * ring
    tall = width // devices
    tiles = hidden.shape[1] // cut
    return pl.pallas_call(
        functools.partial(expert_grad_kernel, groups=groups, ring=ring),
        grid=(tiles,),
        in_specs=[
            pl.BlockSpec((slots, lanes), lambda j: (0, 0)),
            pl.BlockSpec((slots, width), lambda j: (0, 0)),
            pl.BlockSpec((slots, width), lambda j: (0, 0)),
            pl.BlockSpec((slots, cut), lambda j: (0, j)),
            pl.BlockSpec((slots, cut), lambda j: (0, j)),
        ],
        out_specs=[pl.BlockSpec((width, lanes), lambda j: (0, 0))]
        + [pl.BlockSpec((groups, tall, cut), lambda j: (0, j, 0))] * ring
        + [pl.BlockSpec((groups, share, width), lambda j: (0, 0, 0))] * ring,
        scratch_shapes=[pltpu.VMEM((width, slots), BF16)],
        out_shape=(jax.ShapeDtypeStruct((width, lanes), F32),)
        + (jax.ShapeDtypeStruct((groups, tiles * tall, cut), BF16),) * ring
        + (jax.ShapeDtypeStruct((groups, share, width), BF16),) * ring,
        compiler_params=pltpu.CompilerParams(
            dimension_semantics=("arbitrary",), vmem_limit_bytes=56 << 20
        ),
        name="expert_grads",
    )(d_logits, rows, d_ret, hidden, d_pre)


def body(
    tokens,
    seg_ids,
    routes,
    attn_gain,
    query_key_value_weight,
    attention_output_weight,
    bias_table,
    ffn_gain,
    router_weight,
    expert_in,
    expert_out,
    out_grad,
):
    n_ctx = lax.axis_size("ctx")
    n_batch = lax.axis_size("batch")
    per, width = tokens.shape[1:]
    head_count = bias_table.shape[1]
    groups = math.gcd(head_count, n_ctx)
    ring = n_ctx // groups
    heads = head_count // groups
    part = heads * 64
    tall = query_key_value_weight.shape[0]
    lanes = 128
    wide = 256
    rows_own = groups * per
    capacity = max(2, 2 * per // n_batch)
    slots = n_batch * capacity
    fine = tall % 8 == 0
    ctx = lax.axis_index("ctx").astype(jnp.int32)
    zed = lax.axis_index("batch").astype(jnp.int32)
    group, own = ctx // ring, ctx % ring

    def over_groups(parts):
        return [
            parts[m] if m == 0 else swap(parts[m], "ctx", n_ctx, ring * m) for m in range(groups)
        ]

    def over_ring(parts):
        return [parts[m] if m == 0 else swap(parts[m], "ctx", n_ctx, m) for m in range(ring)]

    def over_batch(parts):
        return [
            parts[m] if m == 0 else swap(parts[m], "batch", n_batch, m) for m in range(n_batch)
        ]

    def turn_batch(rows):
        rows = rows.reshape(n_batch, capacity, width)
        rows = lax.all_to_all(rows, "batch", split_axis=0, concat_axis=0, tiled=True)
        return rows.reshape(slots, width)

    def natural(pieces, columns):
        pieces = [p.reshape(n_batch, groups, tall, columns) for p in pieces]
        pieces = xor_order(pieces, own)
        pieces = [xor_order([c[z] for z in range(n_batch)], zed) for c in pieces]
        pieces = [[xor_order([b[g] for g in range(groups)], group) for b in c] for c in pieces]
        order = [(g, r, z) for g in range(groups) for r in range(ring) for z in range(n_batch)]
        return [jnp.concatenate([pieces[r][z][g] for g, r, z in order], axis=0)]

    first = kernel_call(
        functools.partial(first_kernel, part=part, ring=ring),
        "first",
        [tokens[0], seg_ids, attn_gain, query_key_value_weight],
        [((per + 16, width), BF16)] + [((tall, 3 * part), BF16)] * groups,
    )
    message, cuts = first[0], list(first[1:])
    cuts = over_groups(cuts)
    message, cuts = lax.optimization_barrier((message, cuts))
    arrived = over_groups([message] * groups)
    both = jnp.concatenate(
        [attention_output_weight, jnp.pad(router_weight, ((0, 0), (0, lanes - n_batch)))], axis=1
    )
    cuts = jnp.concatenate(cuts, axis=0)
    step = 1
    while step < n_batch:
        cuts = jnp.concatenate([cuts, swap(cuts, "batch", n_batch, step)], axis=0)
        cuts, both = lax.optimization_barrier((cuts, both)) if step == 1 else (cuts, both)
        step = step * 2
    step = 1
    while step < n_batch:
        both = jnp.concatenate([both, swap(both, "batch", n_batch, step)], axis=0)
        step = step * 2

    route_row = routes.reshape(1, per)
    d_result = out_grad[0]
    pick, pick_t, dz_sent = kernel_call(
        functools.partial(dispatch_kernel, capacity=capacity),
        "dispatch",
        [route_row, d_result],
        [((slots, per), BF16), ((per, slots), BF16), ((slots, width), BF16)],
    )
    table = sum(
        jnp.where(group == g, bias_table[:, g * heads : (g + 1) * heads], 0) for g in range(groups)
    )
    band = jnp.einsum(
        "dbc,bh->hdc",
        jnp.asarray(band_onehot(per), BF16),
        table,
        preferred_element_type=F32,
    )
    band = jnp.pad(band, ((0, 0), (0, 3), (0, 0)))
    arrived, cuts, dz_sent, band, both = lax.optimization_barrier(
        (arrived, cuts, dz_sent, band, both)
    )
    cuts = over_ring([cuts] * ring)
    dz_there = turn_batch(dz_sent)
    if not fine:
        cuts = natural(cuts, 3 * part)
    kv_rows = rows_own + 16
    q, kv_own, w_head = kernel_call(
        functools.partial(
            project_kernel,
            groups=groups,
            ring=ring,
            batch=n_batch,
            tall=tall,
            part=part,
            per=per,
            pieces=len(cuts),
        ),
        "project",
        [*arrived, *cuts],
        [
            ((rows_own, wide), BF16),
            ((kv_rows, 2 * wide), BF16),
            ((width, 3 * wide), BF16),
        ],
        [((width, 3 * part), F32)],
    )
    kv_own, both = lax.optimization_barrier((kv_own, both))
    kv_all = over_ring([kv_own] * ring)
    both = over_groups([both] * groups)

    out_t, lse, *mixed = attend(q, kv_all, band, heads, groups, ring, per)

    mixed, dz_there, both = lax.optimization_barrier((mixed, dz_there, both))
    both = jnp.stack([b.reshape(n_batch, tall, width + lanes) for b in both], axis=1)
    both = over_ring([both.reshape(n_batch * groups * tall, width + lanes)] * ring)
    if fine:
        both = kernel_call(
            functools.partial(gather_kernel, groups=groups, ring=ring, batch=n_batch, tall=tall),
            "gather",
            both,
            [((width, width + lanes), BF16)],
            [((width, width + lanes), F32)],
        )[0]
    else:
        both = natural(both, width + lanes)[0]
    mixed = over_groups(mixed)
    mixed, both = lax.optimization_barrier((mixed, both))
    middle, gate, *rows_sent = kernel_call(
        functools.partial(
            middle_kernel, groups=groups, ring=ring, batch=n_batch, part=part, capacity=capacity
        ),
        "middle",
        [*mixed, both, tokens[0], ffn_gain, pick, route_row],
        [((per, width), F32), ((per, 1), F32)] + [((capacity, width), BF16)] * n_batch,
    )
    rows_there = over_batch(rows_sent)
    produced, back, *saved = expert_layer(
        rows_there, dz_there, both, expert_in[0], expert_out[0], ring
    )
    back = turn_batch(back)
    router_part, *grads = expert_grads(*saved, groups, ring)
    g1, g2 = grads[:ring], grads[ring:]

    back, g1, g2 = lax.optimization_barrier((back, g1, g2))
    g1, g2 = over_ring(g1), over_ring(g2)
    kept, kept_left, kept_right, grads_one, grads_two = merge(g1, g2)
    sums_shape = (n_batch, groups, tall, width + lanes)
    sums_shape = (
        [(sums_shape, F32)] + [(sums_shape, BF16)] * (ring - 1)
        if fine
        else [((width, width + lanes), F32)]
    )
    d_middle, ffn_gain_part, *rest = kernel_call(
        functools.partial(
            branch_kernel,
            groups=groups,
            ring=ring,
            batch=n_batch,
            tall=tall,
            part=part,
        ),
        "branch",
        [back, *mixed, pick_t, middle, d_result, ffn_gain, both, router_part],
        [((per, width), F32), ((1, width), F32)] + [((per, part), BF16)] * groups + sums_shape,
    )
    d_mix, out_parts = rest[:groups], rest[groups:]

    def by_place(parts):
        if fine:
            return parts
        grad = parts[0].reshape(groups, ring, n_batch, tall, parts[0].shape[1])
        parts = xor_order([grad[:, r] for r in range(ring)], own)
        parts = [xor_order([p[:, z] for z in range(n_batch)], zed) for p in parts]
        parts = [[xor_order([z[g] for g in range(groups)], group) for z in p] for p in parts]
        parts = [jnp.stack([jnp.stack(z) for z in p]) for p in parts]
        return [parts[0]] + [p.astype(BF16) for p in parts[1:]]

    d_mix = over_groups(d_mix)
    out_parts = over_ring(by_place(out_parts))
    d_mix, grads_one, grads_two, out_parts = lax.optimization_barrier(
        (d_mix, grads_one, grads_two, out_parts)
    )
    shape = out_parts[0].shape[1:]
    out_parts = kernel_call(
        functools.partial(half_kernel, ring=ring),
        "half_out",
        out_parts,
        [(shape, F32)] + [(shape, BF16)] * (n_batch - 1),
    )
    out_parts = over_batch(out_parts)
    grads_one = swap(grads_one, "ctx", n_ctx, ring)
    grads_two = swap(grads_two, "ctx", n_ctx, 2 * ring)

    dq, dkv_own, *rest = attend_back(
        q, kv_all, band, d_mix, out_t, lse, heads, groups, ring, per
    )
    dkv_other, table_part = rest[: ring - 1], rest[ring - 1]
    dkv_other, grads_one, grads_two, out_parts, produced = lax.optimization_barrier(
        (dkv_other, grads_one, grads_two, out_parts, produced)
    )
    dkv_got = over_ring([dkv_own] + dkv_other)[1:]
    returned = turn_batch(produced)
    last_left, last_right = fold(kept_left, kept_right, grads_one, grads_two)
    last_left = swap(last_left, "ctx", n_ctx, 2 * ring)
    last_right = swap(last_right, "ctx", n_ctx, ring)

    grads_shape = (
        [((n_batch, groups, tall, 3 * part), F32)]
        + [((n_batch, groups, tall, 3 * part), BF16)] * (ring - 1)
        if fine
        else [((width, 3 * part), F32)]
    )
    d_packed, *packed_parts = kernel_call(
        functools.partial(
            weight_kernel,
            groups=groups,
            ring=ring,
            batch=n_batch,
            tall=tall,
            part=part,
            per=per,
        ),
        "weight",
        [dq, dkv_own, *dkv_got, *arrived],
        [((rows_own, 3 * wide), BF16)] + grads_shape,
        [((rows_own, width), BF16)],
    )
    late_rows = -(-(2 * width // lanes + head_count) // 8) * 8
    *d_normed, late = kernel_call(
        functools.partial(unproject_kernel, per=per, ring=ring, heads=heads, groups=groups),
        "unproject",
        [d_packed, w_head, attn_gain, ffn_gain_part, table_part, *arrived],
        [((per, width), F32)]
        + [((per, width), BF16)] * (groups - 1)
        + [((n_ctx * n_batch, late_rows, lanes), F32)],
    )
    packed_parts = over_ring(by_place(packed_parts))
    packed_parts, d_normed, last_left, last_right, returned = lax.optimization_barrier(
        (packed_parts, d_normed, last_left, last_right, returned)
    )
    got = over_groups(d_normed)
    shape = packed_parts[0].shape[1:]
    packed_parts = kernel_call(
        functools.partial(half_kernel, ring=ring),
        "half_packed",
        packed_parts,
        [(shape, F32)] + [(shape, BF16)] * (n_batch - 1),
    )
    packed_parts = list(packed_parts)
    layer_out = kernel_call(
        combine_kernel,
        "combine",
        [returned, pick_t, middle, gate],
        [((per, width), BF16)],
    )[0][None]
    expert_in_grad, expert_out_grad = kernel_call(
        finish_kernel,
        "finish",
        [kept, grads_one, grads_two, last_left, last_right],
        [
            ((width // n_ctx, expert_in.shape[2]), F32),
            ((expert_out.shape[1] // n_ctx, width), F32),
        ],
    )
    packed_parts[-1], layer_out, expert_in_grad, expert_out_grad = lax.optimization_barrier(
        (packed_parts[-1], layer_out, expert_in_grad, expert_out_grad)
    )
    packed_parts = over_batch(packed_parts)
    tokens_grad = kernel_call(
        functools.partial(tokens_kernel, groups=groups),
        "tokens",
        [*got, tokens[0], attn_gain, d_middle],
        [((per, width), BF16)],
    )[0][None]
    packed_parts, layer_out, expert_in_grad, expert_out_grad, tokens_grad = (
        lax.optimization_barrier(
            (packed_parts, layer_out, expert_in_grad, expert_out_grad, tokens_grad)
        )
    )
    parts = kernel_call(
        functools.partial(quarter_kernel, batch=n_batch),
        "quarter",
        [*packed_parts, *out_parts],
        [((tall, 3 * part + width + lanes), BF16)] * groups,
    )

    late = lax.all_to_all(late, ("ctx", "batch"), split_axis=0, concat_axis=0, tiled=True)
    attn_gain_grad, ffn_gain_grad, d_table = kernel_call(
        late_kernel,
        "late",
        [late],
        [((width // lanes, lanes), F32)] * 2 + [((head_count, lanes), F32)],
    )
    attn_gain_grad = attn_gain_grad.reshape(width)
    ffn_gain_grad = ffn_gain_grad.reshape(width)
    bias_grad = d_table[:, : bias_table.shape[0]].T
    qkv_grad, out_weight_grad, router_grad = kernel_call(
        functools.partial(columns_kernel, groups=groups, ring=ring, part=part),
        "columns",
        over_groups(parts),
        [((tall, 3 * width), F32), ((tall, width), F32), ((tall, lanes), F32)],
    )
    router_grad = router_grad[:, :n_batch]
    return (
        layer_out,
        tokens_grad,
        attn_gain_grad,
        qkv_grad,
        out_weight_grad,
        bias_grad,
        ffn_gain_grad,
        router_grad,
        expert_in_grad[None],
        expert_out_grad[None],
    )


def solution(mesh):
    return jax.shard_map(
        body,
        mesh=mesh,
        in_specs=(
            P("batch", "ctx", None),
            P("batch", "ctx"),
            P("ctx", "batch", None, None),
            P(),
            P(("ctx", "batch"), None),
            P(("ctx", "batch"), None),
            P(),
            P(),
            P(("ctx", "batch"), None),
            P("batch", None, None),
            P("batch", None, None),
            P("batch", "ctx", None),
        ),
        out_specs=(
            P("batch", "ctx", None),
            P("batch", "ctx", None),
            P(),
            P(("ctx", "batch"), None),
            P(("ctx", "batch"), None),
            P(),
            P(),
            P(("ctx", "batch"), None),
            P("batch", "ctx", None),
            P("batch", "ctx", None),
        ),
        check_vma=False,
    )
```

```python
import functools
import math

import jax
import jax.numpy as jnp
import numpy as np
from jax import lax
from jax.experimental import pallas as pl
from jax.experimental.pallas import tpu as pltpu
from jax.sharding import PartitionSpec as P

BUCKETS = 32
MAX_DIST = 128
EPSILON = 1e-06
MASKED = -1e30
F32 = jnp.float32
BF16 = jnp.bfloat16


def bucket_limits():
    half_span = BUCKETS // 2
    exact_span = half_span // 2
    log_levels = half_span - exact_span
    limits = []
    for level_at in range(1, log_levels):
        bound_row = exact_span
        while (
            bound_row**log_levels * exact_span**level_at
            < MAX_DIST**level_at * exact_span**log_levels
        ):
            bound_row = bound_row + 1
        limits.append(bound_row)
    return limits


def relative_bucket(offsets):
    half_span = BUCKETS // 2
    exact_span = half_span // 2
    distance = np.abs(offsets)
    far = np.full(distance.shape, exact_span, np.int32)
    for bound_row in bucket_limits():
        far = far + (distance >= bound_row).astype(np.int32)
    near = np.where(distance < exact_span, distance, far)
    return near + np.where(offsets > 0, half_span, 0)


def band_buckets(block):
    column = np.arange(2 * block)
    rows = []
    for d in range(5):
        if d in (0, 4):
            offsets = np.full((2 * block,), (d - 2) * max(block, MAX_DIST), np.int64)
        else:
            offsets = (d - 2) * block + block - column
        rows.append(relative_bucket(offsets))
    return np.stack(rows)


def band_onehot(block):
    return band_buckets(block)[:, None, :] == np.arange(BUCKETS)[None, :, None]


def dot(a, b, dims, precision=None):
    return lax.dot_general(a, b, (dims, ((), ())), preferred_element_type=F32, precision=precision)


NN = ((1,), (0,))
NT = ((1,), (1,))
TN = ((0,), (0,))


def xor_order(parts, index):
    parts = list(parts)
    step = 1
    while step < len(parts):
        odd = (index // step) % 2 == 1
        parts = [jnp.where(odd, parts[i ^ step], parts[i]) for i in range(len(parts))]
        step = step * 2
    return parts


def vmem(count):
    return [pl.BlockSpec(memory_space=pltpu.VMEM)] * count


def place(ring):
    ctx = lax.axis_index("ctx").astype(jnp.int32)
    return ctx // ring, ctx % ring, lax.axis_index("batch").astype(jnp.int32)


def kernel_call(kernel, name, arrays, out_shape, scratch=()):
    return pl.pallas_call(
        kernel,
        out_shape=tuple(jax.ShapeDtypeStruct(shape, kind) for shape, kind in out_shape),
        in_specs=vmem(len(arrays)),
        out_specs=vmem(len(out_shape)),
        scratch_shapes=[
            pltpu.SMEM(shape, kind) if kind == jnp.int32 else pltpu.VMEM(shape, kind)
            for shape, kind in scratch
        ],
        compiler_params=pltpu.CompilerParams(vmem_limit_bytes=56 << 20),
        name=name,
    )(*arrays)


def swap(value, axis, size, mask):
    return lax.ppermute(value, axis, [(i, i ^ mask) for i in range(size)])


def column(row, size):
    return jnp.broadcast_to(row, (size, row.shape[1])).T


def first_kernel(tokens_ref, seg_ref, gain_ref, row_ref, message_ref, *cut_refs, part, ring):
    info = place(ring)
    tokens = tokens_ref[...].astype(F32)
    per, width = tokens.shape
    scale = lax.rsqrt(jnp.mean(tokens * tokens, axis=1, keepdims=True) + EPSILON)
    message_ref[:per, :] = (tokens * scale * gain_ref[...].astype(F32)[None, :]).astype(BF16)
    message_ref[per:, :] = jnp.zeros((message_ref.shape[0] - per, width), BF16)
    message_ref[per:, :per] = jnp.broadcast_to(
        seg_ref[...].astype(F32), (message_ref.shape[0] - per, per)
    ).astype(BF16)
    rows = row_ref[...].astype(F32)
    groups = len(cut_refs)
    cuts = [
        jnp.concatenate(
            [rows[:, k * width + g * part : k * width + (g + 1) * part] for k in range(3)], axis=1
        )
        for g in range(groups)
    ]
    for ref, cut in zip(cut_refs, xor_order(cuts, info[0])):
        ref[...] = cut.astype(BF16)


def row_place(info, g, r, z, ring, batch):
    return ((g ^ info[0]) * ring + (r ^ info[1])) * batch + (z ^ info[2])


def assemble(info, piece_refs, dest_ref, groups, batch, tall):
    ring = len(piece_refs)
    for r in range(ring):
        for z in range(batch):
            for g in range(groups):
                block = row_place(info, g, r, z, ring, batch)
                at = (z * groups + g) * tall
                dest_ref[pl.ds(pl.multiple_of(block * tall, 8), tall), :] = piece_refs[r][
                    at : at + tall, :
                ].astype(F32)


def project_kernel(*refs, groups, ring, batch, tall, part, per, pieces):
    x_refs, refs = refs[:groups], refs[groups:]
    w_refs, refs = refs[:pieces], refs[pieces:]
    q_ref, kv_ref, w_out, w_s = refs
    wide = 256
    if tall % 8 == 0:
        assemble(place(ring), w_refs, w_s, groups, batch, tall)
    else:
        w_s[...] = w_refs[0][...].astype(F32)
    gap = jnp.zeros((w_s.shape[0], wide - part), BF16)
    w = jnp.concatenate(
        [x for k in range(3) for x in (w_s[:, k * part : (k + 1) * part].astype(BF16), gap)],
        axis=1,
    )
    w_out[...] = w
    kv_ref[groups * per :, :] = jnp.zeros((kv_ref.shape[0] - groups * per, 2 * wide), BF16)
    seg = jnp.concatenate([x_ref[per : per + 1, :wide].astype(F32) for x_ref in x_refs], axis=0)
    seg = jnp.concatenate(
        [seg, jnp.zeros((kv_ref.shape[0] - groups * per - groups, wide), F32)], axis=0
    )
    kv_ref[groups * per :, :wide] = seg.astype(BF16)
    for m in range(groups):
        packed = dot(x_refs[m][:per, :], w_out[...], NN).astype(BF16)
        q_ref[m * per : (m + 1) * per, :] = packed[:, :wide]
        kv_ref[m * per : (m + 1) * per, :] = packed[:, wide:]


def slot_row(route, capacity):
    per = route.shape[1]
    earlier = lax.broadcasted_iota(jnp.int32, (per, per), 0) < lax.broadcasted_iota(
        jnp.int32, (per, per), 1
    )
    same = jnp.where((column(route, per) == route) & earlier, 1.0, 0.0)
    return route * capacity + jnp.sum(same, axis=0, keepdims=True)


def dispatch_kernel(route_ref, dz_ref, pick_ref, pick_t_ref, sent_ref, *, capacity):
    target = slot_row(route_ref[...].astype(F32), capacity).astype(jnp.int32)
    slots, per = pick_ref.shape
    slot = lax.broadcasted_iota(jnp.int32, (slots, per), 0)
    pick = jnp.where(slot == target, 1.0, 0.0)
    pick_ref[...] = pick.astype(BF16)
    pick_t_ref[...] = pick.T.astype(BF16)
    sent_ref[...] = dot(pick.astype(BF16), dz_ref[...], NN).astype(BF16)


def gather_kernel(*refs, groups, ring, batch, tall):
    w_refs, w_ref, w_s = refs[:-2], refs[-2], refs[-1]
    assemble(place(ring), w_refs, w_s, groups, batch, tall)
    w_ref[...] = w_s[...].astype(BF16)


def middle_kernel(*refs, groups, ring, batch, part, capacity):
    info = place(ring)
    mixed_refs, refs = refs[:groups], refs[groups:]
    w_ref, tokens_ref, gain_ref, pick_ref, route_ref, middle_ref, gate_ref = refs[:7]
    sent_refs = refs[7:]
    width = tokens_ref.shape[1]
    middle = tokens_ref[...].astype(F32)
    for m in range(groups):
        start = pl.multiple_of((info[0] ^ m) * part, 16)
        middle += dot(mixed_refs[m][...], w_ref[pl.ds(start, part), :width], NN)
    middle_ref[...] = middle
    scale = lax.rsqrt(jnp.mean(middle * middle, axis=1, keepdims=True) + EPSILON)
    normed = (middle * scale * gain_ref[...].astype(F32)[None, :]).astype(BF16)
    for m, ref in enumerate(sent_refs):
        start = pl.multiple_of((info[2] ^ m) * capacity, capacity)
        ref[...] = dot(pick_ref[pl.ds(start, capacity), :], normed, NN).astype(BF16)
    logits = dot(normed, w_ref[:, width:], NN)
    lane = lax.broadcasted_iota(jnp.int32, logits.shape, 1)
    logits = jnp.where(lane < batch, logits, MASKED)
    expo = jnp.exp(logits - jnp.max(logits, axis=1, keepdims=True))
    probs = expo / jnp.sum(expo, axis=1, keepdims=True)
    route = column(route_ref[...].astype(F32), logits.shape[1]).astype(jnp.int32)
    gate_ref[...] = jnp.sum(jnp.where(lane == route, probs, 0.0), axis=1, keepdims=True)


def branch_kernel(back_ref, *refs, groups, ring, batch, tall, part):
    info = place(ring)
    mixed_refs, refs = refs[:groups], refs[groups:]
    pick_t_ref, middle_ref, dz_ref, gain_ref, w_ref, rpart_ref = refs[:6]
    d_middle_ref, gain_part_ref = refs[6:8]
    d_mixed_refs, grad_refs = refs[8 : 8 + groups], refs[8 + groups :]
    width = middle_ref.shape[1]
    d_normed = dot(pick_t_ref[...], back_ref[...], NN)
    middle = middle_ref[...]
    scale = lax.rsqrt(jnp.mean(middle * middle, axis=1, keepdims=True) + EPSILON)
    gain_part_ref[...] = jnp.sum(d_normed * middle * scale, axis=0, keepdims=True)
    scaled = gain_ref[...].astype(F32)[None, :] * d_normed
    d_middle = (
        dz_ref[...].astype(F32)
        + scale * scaled
        - middle
        * (scale * scale * scale)
        * jnp.mean(scaled * middle, axis=1, keepdims=True)
    )
    d_middle_ref[...] = d_middle
    d_branch = d_middle.astype(BF16)
    for m in range(groups):
        start = pl.multiple_of((info[0] ^ m) * part, 16)
        d_mixed_refs[m][...] = dot(d_branch, w_ref[pl.ds(start, part), :width], NT).astype(BF16)
    for m in range(groups):
        start = pl.multiple_of((info[0] ^ m) * part, 16)
        grad = dot(mixed_refs[m][...], d_branch, TN)
        grad = jnp.concatenate([grad, rpart_ref[pl.ds(start, part), :]], axis=1)
        if tall % 8 == 0:
            scatter_rows(info, grad, m, grad_refs, ring, batch, tall, 0)
        else:
            grad_refs[0][pl.ds(start, part), :] = grad


def scatter_rows(info, grad, g, grad_refs, ring, batch, tall, turn):
    for z in range(batch):
        rows = [
            grad[(r * batch + z) * tall : (r * batch + z + 1) * tall, :] for r in range(ring)
        ]
        for ref, row in zip(grad_refs, xor_order(rows, info[1])):
            ref[z ^ turn, g] = row.astype(ref.dtype)


def weight_kernel(dq_ref, *refs, groups, ring, batch, tall, part, per):
    info = place(ring)
    got_refs, refs = refs[:ring], refs[ring:]
    x_refs, dp_ref, grad_refs, x_s = refs[:groups], refs[groups], refs[groups + 1 : -1], refs[-1]
    wide = 256
    for m in range(groups):
        rows = slice(m * per, (m + 1) * per)
        dkv = got_refs[0][rows, :]
        for ref in got_refs[1:]:
            dkv += ref[rows, :].astype(F32)
        dp_ref[rows, :wide] = dq_ref[rows, :]
        dp_ref[rows, wide:] = dkv.astype(BF16)
        x_s[rows, :] = x_refs[m][:per, :]
    share = ring * batch * tall
    for g in range(groups):
        grad = dot(x_s[:, g * share : (g + 1) * share], dp_ref[...], TN)
        grad = jnp.concatenate([grad[:, k * wide : k * wide + part] for k in range(3)], axis=1)
        if tall % 8 == 0:
            scatter_rows(info, grad, g ^ info[0], grad_refs, ring, batch, tall, info[2])
        else:
            grad_refs[0][g * share : (g + 1) * share, :] = grad


def unproject_kernel(
    dp_ref, w_ref, gain_ref, gain2_ref, table_ref, *refs, per, ring, heads, groups
):
    x_refs, d_refs, late_ref = refs[:groups], refs[groups : 2 * groups], refs[-1]
    width = gain2_ref.shape[1]
    total = jnp.zeros((1, width), F32)
    for m, ref in enumerate(d_refs):
        rows = slice(m * per, (m + 1) * per)
        d_normed = dot(dp_ref[rows, :], w_ref[...], NT)
        ref[...] = d_normed.astype(ref.dtype)
        total += jnp.sum(d_normed * x_refs[m][:per, :].astype(F32), axis=0, keepdims=True)
    total = total / gain_ref[...].astype(F32)[None, :]
    late_ref[0] = jnp.zeros(late_ref.shape[1:], F32)
    count = width // 128
    for k in range(count):
        late_ref[0, k : k + 1, :] = total[:, k * 128 : (k + 1) * 128]
        late_ref[0, count + k : count + k + 1, :] = gain2_ref[:, k * 128 : (k + 1) * 128]
    group = place(ring)[0]
    for h in range(heads):
        late_ref[0, pl.ds(2 * count + group * heads + h, 1), :] = table_ref[h : h + 1, :]
    whole = late_ref[0]

    @pl.loop(1, late_ref.shape[0])
    def _(k):
        late_ref[k] = whole


def late_kernel(got_ref, gain1_ref, gain2_ref, table_ref):
    total = jnp.sum(got_ref[...], axis=0)
    count, heads = gain1_ref.shape[0], table_ref.shape[0]
    gain1_ref[...] = total[:count, :]
    gain2_ref[...] = total[count : 2 * count, :]
    table_ref[...] = total[2 * count : 2 * count + heads, :]


def half_kernel(*refs, ring):
    total = refs[0][...]
    for ref in refs[1:ring]:
        total += ref[...].astype(F32)
    if len(refs) == ring + 1:
        refs[ring][...] = total.astype(BF16)
    else:
        for m, ref in enumerate(refs[ring:]):
            ref[...] = total[m].astype(ref.dtype)


def quarter_kernel(two_ref, *refs, batch):
    one = refs[0][...]
    for ref in refs[1:batch]:
        one += ref[...].astype(F32)
    two = jnp.sum(two_ref[...].astype(F32), axis=0)
    cut = one.shape[2]
    for m, ref in enumerate(refs[batch:]):
        ref[:, :cut] = one[m].astype(BF16)
        ref[:, cut:] = two[m].astype(BF16)


def columns_kernel(*refs, groups, ring, part):
    qkv_ref, out_ref, router_ref = refs[groups:]
    cut, width = 3 * part, out_ref.shape[1]
    parts = xor_order([ref[:, :cut].astype(F32) for ref in refs[:groups]], place(ring)[0])
    qkv_ref[...] = jnp.concatenate(
        [p[:, k * part : (k + 1) * part] for k in range(3) for p in parts], axis=1
    )
    total = sum(ref[:, cut:].astype(F32) for ref in refs[:groups])
    out_ref[...] = total[:, :width]
    router = total[:, width:]
    spare = jnp.zeros((router.shape[1] - router.shape[0], router.shape[1]), F32)
    router = jnp.concatenate([router, spare], axis=0).T
    router_ref[...] = router[: router_ref.shape[0], : router_ref.shape[1]]


def tokens_kernel(*refs, groups):
    tokens_ref, gain_ref, d_middle_ref, out_ref = refs[groups:]
    d_normed = refs[0][...]
    for ref in refs[1:groups]:
        d_normed += ref[...].astype(F32)
    tokens = tokens_ref[...].astype(F32)
    scale = lax.rsqrt(jnp.mean(tokens * tokens, axis=1, keepdims=True) + EPSILON)
    scaled = gain_ref[...].astype(F32)[None, :] * d_normed
    out_ref[...] = (
        d_middle_ref[...]
        + scale * scaled
        - tokens
        * (scale * scale * scale)
        * jnp.mean(scaled * tokens, axis=1, keepdims=True)
    ).astype(BF16)


def combine_kernel(got_ref, pick_t_ref, middle_ref, gate_ref, out_ref):
    returned = dot(pick_t_ref[...], got_ref[...], NN)
    out_ref[...] = (middle_ref[...] + gate_ref[...] * returned).astype(BF16)


def merge_kernel(*refs, ring):
    g1_refs, g2_refs = refs[:ring], refs[ring : 2 * ring]
    own_ref, left_ref, right_ref, one_ref, two_ref = refs[2 * ring :]
    step = pl.program_id(0)
    g1 = sum(ref[...].astype(F32) for ref in g1_refs).astype(BF16)
    g2 = sum(ref[...].astype(F32) for ref in g2_refs).astype(BF16)
    rows, half = g1.shape[0], g1.shape[1] // 2

    def put(ref, cut):
        ref[:rows, :] = g1[:, cut]
        ref[rows:, :] = g2[:, cut]

    left, right = slice(0, half), slice(half, 2 * half)
    pl.when(step <= 1)(lambda: put(one_ref, left))
    pl.when((step == 1) | (step == 2))(lambda: put(two_ref, right))
    pl.when(step == 0)(lambda: put(right_ref, right))
    pl.when(step == 2)(lambda: put(left_ref, left))
    pl.when(step == 3)(lambda: put(own_ref, slice(0, 2 * half)))


def merge(g1, g2):
    groups, rows, width = g1[0].shape
    assert groups == 4
    ring = len(g1)
    tall, half = 2 * rows, width // 2
    order = lambda s: (jnp.where(s == 0, 1, jnp.where(s == 1, 3, jnp.where(s == 2, 2, 0))), 0, 0)
    block = lambda columns: pl.BlockSpec((tall, columns), lambda s: (0, 0))
    return pl.pallas_call(
        functools.partial(merge_kernel, ring=ring),
        grid=(groups,),
        out_shape=(
            jax.ShapeDtypeStruct((tall, width), BF16),
            jax.ShapeDtypeStruct((tall, half), BF16),
            jax.ShapeDtypeStruct((tall, half), BF16),
            jax.ShapeDtypeStruct((2, tall, half), BF16),
            jax.ShapeDtypeStruct((2, tall, half), BF16),
        ),
        in_specs=[pl.BlockSpec((None, rows, width), order)] * (2 * ring),
        out_specs=[
            block(width),
            block(half),
            block(half),
            pl.BlockSpec((None, tall, half), lambda s: (jnp.minimum(s, 1), 0, 0)),
            pl.BlockSpec((None, tall, half), lambda s: (jnp.where(s <= 1, 1, 0), 0, 0)),
        ],
        compiler_params=pltpu.CompilerParams(
            dimension_semantics=("arbitrary",), vmem_limit_bytes=56 << 20
        ),
        name="merge",
    )(*g1, *g2)


def fold_kernel(left_ref, right_ref, one_ref, two_ref, left_out, right_out):
    left_out[...] = (left_ref[...].astype(F32) + one_ref[...].astype(F32)).astype(BF16)
    right_out[...] = (right_ref[...].astype(F32) + two_ref[...].astype(F32)).astype(BF16)


def fold(left, right, one, two):
    tall, half = left.shape
    steps = 2
    plain = pl.BlockSpec((tall // steps, half), lambda s: (s, 0))
    second = pl.BlockSpec((None, tall // steps, half), lambda s: (1, s, 0))
    return pl.pallas_call(
        fold_kernel,
        grid=(steps,),
        out_shape=(jax.ShapeDtypeStruct((tall, half), BF16),) * 2,
        in_specs=[plain, plain, second, second],
        out_specs=[plain, plain],
        compiler_params=pltpu.CompilerParams(dimension_semantics=("arbitrary",)),
        name="fold",
    )(left, right, one, two)


def finish_kernel(own_ref, one_ref, two_ref, left_ref, right_ref, in_ref, out_ref):
    tall, width = in_ref.shape[0], out_ref.shape[1]
    half, rows = width // 2, out_ref.shape[0]
    for at, first_ref, last_ref in ((0, one_ref, left_ref), (half, two_ref, right_ref)):
        cut = slice(at, at + half)
        total = own_ref[:, cut].astype(F32) + first_ref[0].astype(F32) + last_ref[...].astype(F32)
        for j in range(in_ref.shape[1] // width):
            in_ref[:, j * width + at : j * width + at + half] = total[j * tall : (j + 1) * tall, :]
        out_ref[:, cut] = total[rows:, :]


SEGMENTS = 8


def set_bias(band_ref, bias_s, heads, block):
    @pl.loop(0, heads)
    def _(h):
        @pl.loop(0, 5)
        def _(d):
            row = jnp.broadcast_to(band_ref[h, pl.ds(d, 1), :], (block, 2 * block))
            bias_s[h, d] = pltpu.roll(row, block, 1, stride=1, stride_axis=0)[:, :block]


def key_at(kb, info, ring, groups):
    return ((kb % ring) ^ info[1]) * groups + ((kb // ring) ^ info[0])


def set_spans(info, kv_refs, seg_s, span_s, groups, ring, block):
    rows = [ref[groups * block : groups * block + groups, :block].astype(F32) for ref in kv_refs]
    seg = jnp.concatenate(rows, axis=0)
    seg_s[...] = seg
    blocks = groups * ring
    low, high = seg[:, 0:1], seg[:, block - 1 : block]
    at = lax.broadcasted_iota(jnp.int32, (blocks, 1), 0)
    natural = (((at % groups) ^ info[0]) * ring + ((at // groups) ^ info[1])).astype(F32)
    for i in range(groups):
        meets = (low <= high[i : i + 1, :]) & (high >= low[i : i + 1, :])
        first = jnp.min(jnp.where(meets, natural, float(blocks)))
        last = jnp.max(jnp.where(meets, natural, -1.0))
        span_s[i, 0] = first.astype(jnp.int32)
        span_s[i, 1] = last.astype(jnp.int32) + 1


def with_extras(pair, half, extras):
    lane = lax.broadcasted_iota(jnp.int32, pair.shape, 1)
    kept = jnp.where(lane // 64 == half, pair, 0.0)
    spot = lane - (1 - half) * 64
    for at, extra in extras:
        if at is None:
            kept = jnp.where((spot >= 0) & (spot < SEGMENTS), extra(spot), kept)
        else:
            kept = jnp.where(spot == at, extra, kept)
    return kept


def key_extras(seg_col):
    return (None, lambda spot: jnp.where(spot.astype(F32) == seg_col, 0.0, MASKED))


def query_extras(seg_col):
    return (None, lambda spot: jnp.where(spot.astype(F32) == seg_col, 1.0, 0.0))


def three_parts(value):
    high = value.astype(BF16).astype(F32)
    middle = (value - high).astype(BF16).astype(F32)
    return high, middle, value - high - middle


def set_keys(kv_refs, seg_s, heads, groups, block, ones, key_s, turned_s, turn, value_s=None):
    wide = 256
    for r, ref in enumerate(kv_refs):

        @pl.loop(0, groups)
        def _(g):
            at, rows = r * groups + g, pl.ds(pl.multiple_of(g * block, block), block)
            seg_col = column(seg_s[pl.ds(at, 1), :], 128)
            turned_s[at] = ref[rows, turn : turn + wide].astype(F32).T.astype(BF16)
            for h in range(heads):
                lane = (h // 2) * 128
                extras = [key_extras(seg_col)] + [(SEGMENTS + n, 1.0) for n in range(ones)]
                key = with_extras(ref[rows, lane : lane + 128].astype(F32), h % 2, extras)
                key_s[at, h] = key.astype(BF16)
                if value_s is not None:
                    lane = wide + lane
                    extras = [(n, 1.0) for n in range(ones)]
                    value = with_extras(ref[rows, lane : lane + 128].astype(F32), h % 2, extras)
                    value_s[at, h] = value.astype(BF16)


def two_step(first, last, start, finish, even, odd):
    start(first, even)

    @pl.loop(0, (last - first + 1) // 2)
    def _(j):
        kb = first + 2 * j
        start(jnp.minimum(kb + 1, last - 1), odd)
        finish(kb, even)

        @pl.when(kb + 1 < last)
        def _():
            start(jnp.minimum(kb + 2, last - 1), even)
            finish(kb + 1, odd)


def attend_kernel(q_ref, *refs, heads, groups, ring, block):
    info = place(ring)
    kv_refs, refs = refs[:ring], refs[ring:]
    band_ref, ot_ref, lse_ref = refs[:3]
    mixed_refs, refs = refs[3 : 3 + groups], refs[3 + groups :]
    bias_s, seg_s, span_s, key_s, vt_s, query_s, stat_s, acc_s, even_s, odd_s = refs
    set_bias(band_ref, bias_s, heads, block)
    set_spans(info, kv_refs, seg_s, span_s, groups, ring, block)
    set_keys(kv_refs, seg_s, heads, groups, block, 0, key_s, vt_s, 256)

    @pl.loop(0, groups)
    def _(i):
        qb = (i ^ info[0]) * ring + info[1]
        rows = pl.ds(pl.multiple_of(i * block, block), block)
        seg_col = column(seg_s[pl.ds(i, 1), :], 128)
        for h in range(heads):
            lane = (h // 2) * 128
            query = q_ref[rows, lane : lane + 128].astype(F32) * 0.125
            query_s[h] = with_extras(query, h % 2, [query_extras(seg_col)]).astype(BF16)
        stat_s[0:heads] = jnp.full((heads, 1, block), MASKED, F32)
        stat_s[heads : 2 * heads] = jnp.zeros((heads, 1, block), F32)
        acc_s[...] = jnp.zeros_like(acc_s)

        def start(kb, score_s):
            at = key_at(kb, info, ring, groups)
            d = jnp.clip(kb - qb, -2, 2) + 2
            for h in range(heads):
                score_s[h] = dot(key_s[at, h], query_s[h], NT) + bias_s[h, d]

        def finish(kb, score_s):
            at = key_at(kb, info, ring, groups)
            tops = [
                jnp.maximum(stat_s[h], jnp.max(score_s[h], axis=0, keepdims=True))
                for h in range(heads)
            ]
            expos = [jnp.exp(score_s[h] - tops[h]) for h in range(heads)]
            for h in range(heads):
                decay = jnp.exp(stat_s[h] - tops[h])
                stat_s[h] = tops[h]
                stat_s[heads + h] = stat_s[heads + h] * decay + jnp.sum(
                    expos[h], axis=0, keepdims=True
                )
                value_t = vt_s[at, h * 64 : (h + 1) * 64, :]
                acc_s[h] = acc_s[h] * decay + dot(value_t, expos[h].astype(BF16), NN)

        two_step(span_s[i, 0], span_s[i, 1], start, finish, even_s, odd_s)

        for h in range(heads):
            total = stat_s[heads + h]
            ot_ref[i, h * 64 : (h + 1) * 64, :] = acc_s[h] / total
            lse_ref[i, h : h + 1, :] = stat_s[h] + jnp.log(total)

    for i in range(groups):
        mixed_refs[i][...] = ot_ref[i].T.astype(BF16)


def attend(q, kv_all, band, heads, groups, ring, block):
    width = heads * 64
    return kernel_call(
        functools.partial(attend_kernel, heads=heads, groups=groups, ring=ring, block=block),
        "attend",
        [q, *kv_all, band],
        [((groups, width, block), F32), ((groups, 8, block), F32)]
        + [((block, width), BF16)] * groups,
        [
            ((heads, 5, block, block), F32),
            ((groups * ring, block), F32),
            ((groups, 2), jnp.int32),
            ((groups * ring, heads, block, 128), BF16),
            ((groups * ring, 256, block), BF16),
            ((heads, block, 128), BF16),
            ((2 * heads, 1, block), F32),
            ((heads, 64, block), F32),
            ((heads, block, block), F32),
            ((heads, block, block), F32),
        ],
    )


def attend_back_kernel(q_ref, *refs, heads, groups, ring, block):
    info = place(ring)
    kv_refs, refs = refs[:ring], refs[ring:]
    band_ref, refs = refs[0], refs[1:]
    dmix_refs, refs = refs[:groups], refs[groups:]
    ot_ref, lse_ref, dq_ref, own_ref = refs[:4]
    other_refs, refs = refs[4 : 3 + ring], refs[3 + ring :]
    dband_ref, bias_s, seg_s, span_s, key_s, value_s, kt_s, query_s, plain_s, dout_s = refs[:10]
    dplain_s, dqt_s, dkv_s, dbias_s, dmix_s = refs[10:]
    wide = 256
    blocks = groups * ring
    set_bias(band_ref, bias_s, heads, block)
    set_spans(info, kv_refs, seg_s, span_s, groups, ring, block)
    set_keys(kv_refs, seg_s, heads, groups, block, 3, key_s, kt_s, 0, value_s)
    for i in range(groups):
        dmix_s[i, :, : heads * 64] = dmix_refs[i][...].astype(F32)
        dmix_s[i, :, heads * 64 :] = jnp.zeros((block, wide - heads * 64), F32)

    @pl.loop(0, blocks)
    def _(at):
        dkv_s[at] = jnp.zeros(dkv_s.shape[1:], F32)

    @pl.loop(0, heads)
    def _(h):
        dbias_s[h] = jnp.zeros(dbias_s.shape[1:], F32)

    @pl.loop(0, groups)
    def _(i):
        qb = (i ^ info[0]) * ring + info[1]
        rows = pl.ds(pl.multiple_of(i * block, block), block)
        seg_col = column(seg_s[pl.ds(i, 1), :], 128)
        dmix = dmix_s[i]
        dmix_t = dmix.T
        for h in range(heads):
            cut, lane = slice(h * 64, (h + 1) * 64), (h // 2) * 128
            delta = jnp.sum(dmix_t[cut, :] * ot_ref[i, cut, :], axis=0, keepdims=True)
            delta = three_parts(column(-delta, 128))
            lse = three_parts(column(-lse_ref[i, h : h + 1, :], 128))
            query = q_ref[rows, lane : lane + 128].astype(F32) * 0.125
            extras = [query_extras(seg_col)] + [(SEGMENTS + n, lse[n]) for n in range(3)]
            query_s[h] = with_extras(query, h % 2, extras).astype(BF16)
            plain_s[h] = with_extras(query, h % 2, []).astype(BF16)
            d_out = dmix[:, lane : lane + 128]
            extras = [(n, delta[n]) for n in range(3)]
            dout_s[h] = with_extras(d_out, h % 2, extras).astype(BF16)
            dplain_s[h] = with_extras(d_out, h % 2, []).astype(BF16)
        dqt_s[...] = jnp.zeros_like(dqt_s)

        @pl.loop(span_s[i, 0], span_s[i, 1])
        def _(kb):
            at = key_at(kb, info, ring, groups)
            d = jnp.clip(kb - qb, -2, 2) + 2
            softs = [
                jnp.exp(dot(key_s[at, h], query_s[h], NT) + bias_s[h, d]) for h in range(heads)
            ]
            d_scores = [
                (softs[h] * dot(value_s[at, h], dout_s[h], NT)).astype(BF16) for h in range(heads)
            ]
            for h in range(heads):
                lane = (h // 2) * 128
                dkv_s[at, :, wide + lane : wide + lane + 128] += dot(
                    softs[h].astype(BF16), dplain_s[h], NN
                )
                dkv_s[at, :, lane : lane + 128] += dot(d_scores[h], plain_s[h], NN)
                dqt_s[h * 64 : (h + 1) * 64, :] += dot(
                    kt_s[at, h * 64 : (h + 1) * 64, :], d_scores[h], NN
                )
                dbias_s[h, d] += d_scores[h].astype(F32)

        pad = jnp.zeros((wide - heads * 64, block), F32)
        dq_ref[rows, :] = (jnp.concatenate([dqt_s[...], pad], axis=0) * 0.125).T.astype(BF16)

    for r in range(ring):

        @pl.loop(0, groups)
        def _(g):
            at, rows = r * groups + g, pl.ds(pl.multiple_of(g * block, block), block)
            if r == 0:
                own_ref[rows, :] = dkv_s[at]
            else:
                other_refs[r - 1][rows, :] = dkv_s[at].astype(BF16)

    buckets = band_buckets(block)
    zero = jnp.zeros((block, block), F32)
    lane = lax.broadcasted_iota(jnp.int32, (1, 128), 1)
    column_at = lax.broadcasted_iota(jnp.int32, (1, 2 * block), 1)
    dband_ref[...] = jnp.zeros_like(dband_ref)

    @pl.loop(0, heads)
    def _(h):
        table = jnp.zeros((1, 128), F32)
        for d in range(5):
            if d in (0, 4):
                tile = jnp.sum(dbias_s[h, d], axis=0, keepdims=True)
                tile = jnp.concatenate([tile, zero[:1]], axis=1)
            else:
                tile = jnp.concatenate([zero, dbias_s[h, d]], axis=1)
                tall = block
                while tall > 1:
                    tall = tall // 2
                    tile = tile[:tall] + pltpu.roll(tile[tall:], 2 * block - tall, 1)
            for bucket in sorted(set(buckets[d].tolist())):
                held = np.nonzero(buckets[d] == bucket)[0]
                keep = (column_at >= int(held[0])) & (column_at <= int(held[-1]))
                held_sum = jnp.sum(jnp.where(keep, tile, 0.0), axis=1, keepdims=True)
                table += jnp.where(lane == bucket, held_sum, 0.0)
        dband_ref[pl.ds(h, 1), :] = table


def attend_back(q, kv_all, band, d_mix, out_t, lse, heads, groups, ring, block):
    own = groups * block
    blocks = groups * ring
    return kernel_call(
        functools.partial(attend_back_kernel, heads=heads, groups=groups, ring=ring, block=block),
        "attend_back",
        [q, *kv_all, band, *d_mix, out_t, lse],
        [((own, 256), BF16), ((own, 512), F32)]
        + [((own, 512), BF16)] * (ring - 1)
        + [((8, 128), F32)],
        [((heads, 5, block, block), F32), ((blocks, block), F32), ((groups, 2), jnp.int32)]
        + [((blocks, heads, block, 128), BF16)] * 2
        + [((blocks, 256, block), BF16)]
        + [((heads, block, 128), BF16)] * 4
        + [
            ((heads * 64, block), F32),
            ((blocks, block, 512), F32),
            ((heads, 5, block, block), F32),
            ((groups, block, 256), F32),
        ],
    )


def expert_kernel(*refs, experts, ring, batch):
    info = place(ring)
    piece_refs, refs = refs[:batch], refs[batch:]
    dz_ref, router_ref, w1_ref, w2_ref = refs[:4]
    prod_ref, back_ref, d_logits_ref, rows_ref, dret_ref, hidden_ref, d_pre_ref = refs[4:11]
    prob_s, prod_s, back_s = refs[11:]
    capacity = piece_refs[0].shape[0]
    step = pl.program_id(0)
    me = info[2]
    lane = lax.broadcasted_iota(jnp.int32, prob_s.shape, 1)

    @pl.when(step == 0)
    def _():
        for m, ref in enumerate(piece_refs):
            start = pl.multiple_of((me ^ m) * capacity, capacity)
            rows_ref[pl.ds(start, capacity), :] = ref[...]
        logits = dot(rows_ref[...], router_ref[...], NN)
        logits = jnp.where(lane < experts, logits, MASKED)
        expo = jnp.exp(logits - jnp.max(logits, axis=1, keepdims=True))
        probs = expo / jnp.sum(expo, axis=1, keepdims=True)
        prob_s[...] = probs
        gate = jnp.sum(jnp.where(lane == me, probs, 0.0), axis=1, keepdims=True)
        dret_ref[...] = (gate * dz_ref[...].astype(F32)).astype(BF16)
        prod_s[...] = jnp.zeros_like(prod_s)
        back_s[...] = jnp.zeros_like(back_s)

    w1 = w1_ref[...]
    w2 = w2_ref[...]
    pre = dot(rows_ref[...], w1, NN)
    cumulative = 0.5 * (1.0 + lax.erf(pre * (1.0 / math.sqrt(2.0))))
    density = jnp.exp(-0.5 * pre * pre) * (1.0 / math.sqrt(2.0 * math.pi))
    hidden = (pre * cumulative).astype(BF16)
    d_hidden = dot(dret_ref[...], w2, NT)
    d_pre = (d_hidden * (cumulative + pre * density)).astype(BF16)
    hidden_ref[...] = hidden
    d_pre_ref[...] = d_pre
    prod_s[...] += dot(hidden, w2, NN)
    back_s[...] += dot(d_pre, w1, NT)

    @pl.when(step == pl.num_programs(0) - 1)
    def _():
        probs = prob_s[...]
        gate = jnp.sum(jnp.where(lane == me, probs, 0.0), axis=1, keepdims=True)
        chosen = jnp.where(lane == me, 1.0, 0.0)
        produced = prod_s[...].astype(BF16)
        prod_ref[...] = produced
        d_gate = jnp.sum(
            dz_ref[...].astype(F32) * produced.astype(F32), axis=1, keepdims=True
        )
        d_logits = (d_gate * probs * (chosen - gate)).astype(BF16)
        back = back_s[...].astype(BF16).astype(F32) + dot(d_logits, router_ref[...], NT)
        back_ref[...] = back.astype(BF16)
        d_logits_ref[...] = d_logits


def expert_layer(pieces, dz, w_both, w1, w2, ring):
    batch = len(pieces)
    capacity, width = pieces[0].shape
    slots = batch * capacity
    lanes = 128
    hidden = w1.shape[1]
    cut = width
    fixed = lambda j: (0, 0)
    whole = pl.BlockSpec((slots, width), fixed)
    return pl.pallas_call(
        functools.partial(expert_kernel, experts=batch, ring=ring, batch=batch),
        grid=(hidden // cut,),
        in_specs=[pl.BlockSpec((capacity, width), fixed)] * batch
        + [
            whole,
            pl.BlockSpec((width, lanes), lambda j: (0, width // lanes)),
            pl.BlockSpec((width, cut), lambda j: (0, j)),
            pl.BlockSpec((cut, width), lambda j: (j, 0)),
        ],
        out_specs=[
            whole,
            whole,
            pl.BlockSpec((slots, lanes), fixed),
            whole,
            whole,
            pl.BlockSpec((slots, cut), lambda j: (0, j)),
            pl.BlockSpec((slots, cut), lambda j: (0, j)),
        ],
        scratch_shapes=[
            pltpu.VMEM((slots, lanes), F32),
            pltpu.VMEM((slots, width), F32),
            pltpu.VMEM((slots, width), F32),
        ],
        out_shape=(
            jax.ShapeDtypeStruct((slots, width), BF16),
            jax.ShapeDtypeStruct((slots, width), BF16),
            jax.ShapeDtypeStruct((slots, lanes), BF16),
            jax.ShapeDtypeStruct((slots, width), BF16),
            jax.ShapeDtypeStruct((slots, width), BF16),
            jax.ShapeDtypeStruct((slots, hidden), BF16),
            jax.ShapeDtypeStruct((slots, hidden), BF16),
        ),
        compiler_params=pltpu.CompilerParams(
            dimension_semantics=("arbitrary",), vmem_limit_bytes=56 << 20
        ),
        name="experts",
    )(*pieces, dz, w_both, w1, w2)


def expert_grad_kernel(
    d_logits_ref, rows_ref, dret_ref, hidden_ref, d_pre_ref, *refs, groups, ring
):
    info = place(ring)
    router_ref, g1_refs, g2_refs, rows_t = refs[0], refs[1 : 1 + ring], refs[1 + ring : -1], refs[-1]

    @pl.when(pl.program_id(0) == 0)
    def _():
        rows_t[...] = rows_ref[...].astype(F32).T.astype(BF16)
        router_ref[...] = dot(rows_t[...], d_logits_ref[...], NN)

    g2 = dot(hidden_ref[...], dret_ref[...], TN).astype(BF16)
    share = g2.shape[0] // ring
    parts = [g2[c * share : (c + 1) * share, :] for c in range(ring)]
    for ref, rows in zip(g2_refs, xor_order(parts, info[1])):
        ref[pl.program_id(0) ^ info[0]] = rows
    g1 = dot(rows_t[...], d_pre_ref[...], NN).astype(BF16)
    tall = g1.shape[0] // (groups * ring)
    for g in range(groups):
        parts = [
            g1[(g * ring + c) * tall : (g * ring + c + 1) * tall, :] for c in range(ring)
        ]
        for ref, rows in zip(g1_refs, xor_order(parts, info[1])):
            ref[g ^ info[0]] = rows


def expert_grads(d_logits, rows, d_ret, hidden, d_pre, groups, ring):
    slots, width = rows.shape
    lanes = d_logits.shape[1]
    devices = groups * ring
    share = hidden.shape[1] // devices
    cut = share * ring
    tall = width // devices
    tiles = hidden.shape[1] // cut
    return pl.pallas_call(
        functools.partial(expert_grad_kernel, groups=groups, ring=ring),
        grid=(tiles,),
        in_specs=[
            pl.BlockSpec((slots, lanes), lambda j: (0, 0)),
            pl.BlockSpec((slots, width), lambda j: (0, 0)),
            pl.BlockSpec((slots, width), lambda j: (0, 0)),
            pl.BlockSpec((slots, cut), lambda j: (0, j)),
            pl.BlockSpec((slots, cut), lambda j: (0, j)),
        ],
        out_specs=[pl.BlockSpec((width, lanes), lambda j: (0, 0))]
        + [pl.BlockSpec((groups, tall, cut), lambda j: (0, j, 0))] * ring
        + [pl.BlockSpec((groups, share, width), lambda j: (0, 0, 0))] * ring,
        scratch_shapes=[pltpu.VMEM((width, slots), BF16)],
        out_shape=(jax.ShapeDtypeStruct((width, lanes), F32),)
        + (jax.ShapeDtypeStruct((groups, tiles * tall, cut), BF16),) * ring
        + (jax.ShapeDtypeStruct((groups, share, width), BF16),) * ring,
        compiler_params=pltpu.CompilerParams(
            dimension_semantics=("arbitrary",), vmem_limit_bytes=56 << 20
        ),
        name="expert_grads",
    )(d_logits, rows, d_ret, hidden, d_pre)


def body(
    tokens,
    seg_ids,
    routes,
    attn_gain,
    query_key_value_weight,
    attention_output_weight,
    bias_table,
    ffn_gain,
    router_weight,
    expert_in,
    expert_out,
    out_grad,
):
    n_ctx = lax.axis_size("ctx")
    n_batch = lax.axis_size("batch")
    per, width = tokens.shape[1:]
    head_count = bias_table.shape[1]
    groups = math.gcd(head_count, n_ctx)
    ring = n_ctx // groups
    heads = head_count // groups
    part = heads * 64
    tall = query_key_value_weight.shape[0]
    lanes = 128
    wide = 256
    rows_own = groups * per
    capacity = max(2, 2 * per // n_batch)
    slots = n_batch * capacity
    fine = tall % 8 == 0
    ctx = lax.axis_index("ctx").astype(jnp.int32)
    zed = lax.axis_index("batch").astype(jnp.int32)
    group, own = ctx // ring, ctx % ring

    def over_groups(parts):
        return [
            parts[m] if m == 0 else swap(parts[m], "ctx", n_ctx, ring * m) for m in range(groups)
        ]

    def over_ring(parts):
        return [parts[m] if m == 0 else swap(parts[m], "ctx", n_ctx, m) for m in range(ring)]

    def over_batch(parts):
        return [
            parts[m] if m == 0 else swap(parts[m], "batch", n_batch, m) for m in range(n_batch)
        ]

    def turn_batch(rows):
        rows = rows.reshape(n_batch, capacity, width)
        rows = lax.all_to_all(rows, "batch", split_axis=0, concat_axis=0, tiled=True)
        return rows.reshape(slots, width)

    def natural(pieces, columns):
        pieces = [p.reshape(n_batch, groups, tall, columns) for p in pieces]
        pieces = xor_order(pieces, own)
        pieces = [xor_order([c[z] for z in range(n_batch)], zed) for c in pieces]
        pieces = [[xor_order([b[g] for g in range(groups)], group) for b in c] for c in pieces]
        order = [(g, r, z) for g in range(groups) for r in range(ring) for z in range(n_batch)]
        return [jnp.concatenate([pieces[r][z][g] for g, r, z in order], axis=0)]

    first = kernel_call(
        functools.partial(first_kernel, part=part, ring=ring),
        "first",
        [tokens[0], seg_ids, attn_gain, query_key_value_weight],
        [((per + 16, width), BF16)] + [((tall, 3 * part), BF16)] * groups,
    )
    message, cuts = first[0], list(first[1:])
    cuts = over_groups(cuts)
    message, cuts = lax.optimization_barrier((message, cuts))
    arrived = over_groups([message] * groups)
    both = jnp.concatenate(
        [attention_output_weight, jnp.pad(router_weight, ((0, 0), (0, lanes - n_batch)))], axis=1
    )
    cuts = jnp.concatenate(cuts, axis=0)
    step = 1
    while step < n_batch:
        cuts = jnp.concatenate([cuts, swap(cuts, "batch", n_batch, step)], axis=0)
        cuts, both = lax.optimization_barrier((cuts, both)) if step == 1 else (cuts, both)
        step = step * 2
    step = 1
    while step < n_batch:
        both = jnp.concatenate([both, swap(both, "batch", n_batch, step)], axis=0)
        step = step * 2

    route_row = routes.reshape(1, per)
    d_result = out_grad[0]
    pick, pick_t, dz_sent = kernel_call(
        functools.partial(dispatch_kernel, capacity=capacity),
        "dispatch",
        [route_row, d_result],
        [((slots, per), BF16), ((per, slots), BF16), ((slots, width), BF16)],
    )
    table = sum(
        jnp.where(group == g, bias_table[:, g * heads : (g + 1) * heads], 0) for g in range(groups)
    )
    band = jnp.einsum(
        "dbc,bh->hdc",
        jnp.asarray(band_onehot(per), BF16),
        table,
        preferred_element_type=F32,
    )
    band = jnp.pad(band, ((0, 0), (0, 3), (0, 0)))
    arrived, cuts, dz_sent, band, both = lax.optimization_barrier(
        (arrived, cuts, dz_sent, band, both)
    )
    cuts = over_ring([cuts] * ring)
    dz_there = turn_batch(dz_sent)
    if not fine:
        cuts = natural(cuts, 3 * part)
    kv_rows = rows_own + 16
    q, kv_own, w_head = kernel_call(
        functools.partial(
            project_kernel,
            groups=groups,
            ring=ring,
            batch=n_batch,
            tall=tall,
            part=part,
            per=per,
            pieces=len(cuts),
        ),
        "project",
        [*arrived, *cuts],
        [
            ((rows_own, wide), BF16),
            ((kv_rows, 2 * wide), BF16),
            ((width, 3 * wide), BF16),
        ],
        [((width, 3 * part), F32)],
    )
    kv_own, both = lax.optimization_barrier((kv_own, both))
    kv_all = over_ring([kv_own] * ring)
    both = over_groups([both] * groups)

    out_t, lse, *mixed = attend(q, kv_all, band, heads, groups, ring, per)

    mixed, dz_there, both = lax.optimization_barrier((mixed, dz_there, both))
    both = jnp.stack([b.reshape(n_batch, tall, width + lanes) for b in both], axis=1)
    both = over_ring([both.reshape(n_batch * groups * tall, width + lanes)] * ring)
    if fine:
        both = kernel_call(
            functools.partial(gather_kernel, groups=groups, ring=ring, batch=n_batch, tall=tall),
            "gather",
            both,
            [((width, width + lanes), BF16)],
            [((width, width + lanes), F32)],
        )[0]
    else:
        both = natural(both, width + lanes)[0]
    mixed = over_groups(mixed)
    mixed, both = lax.optimization_barrier((mixed, both))
    middle, gate, *rows_sent = kernel_call(
        functools.partial(
            middle_kernel, groups=groups, ring=ring, batch=n_batch, part=part, capacity=capacity
        ),
        "middle",
        [*mixed, both, tokens[0], ffn_gain, pick, route_row],
        [((per, width), F32), ((per, 1), F32)] + [((capacity, width), BF16)] * n_batch,
    )
    rows_there = over_batch(rows_sent)
    produced, back, *saved = expert_layer(
        rows_there, dz_there, both, expert_in[0], expert_out[0], ring
    )
    back = turn_batch(back)
    router_part, *grads = expert_grads(*saved, groups, ring)
    g1, g2 = grads[:ring], grads[ring:]

    back, g1, g2 = lax.optimization_barrier((back, g1, g2))
    g1, g2 = over_ring(g1), over_ring(g2)
    kept, kept_left, kept_right, grads_one, grads_two = merge(g1, g2)
    sums_shape = (n_batch, groups, tall, width + lanes)
    sums_shape = (
        [(sums_shape, F32)] + [(sums_shape, BF16)] * (ring - 1)
        if fine
        else [((width, width + lanes), F32)]
    )
    d_middle, ffn_gain_part, *rest = kernel_call(
        functools.partial(
            branch_kernel,
            groups=groups,
            ring=ring,
            batch=n_batch,
            tall=tall,
            part=part,
        ),
        "branch",
        [back, *mixed, pick_t, middle, d_result, ffn_gain, both, router_part],
        [((per, width), F32), ((1, width), F32)] + [((per, part), BF16)] * groups + sums_shape,
    )
    d_mix, out_parts = rest[:groups], rest[groups:]

    def by_place(parts, turn):
        if fine:
            return parts
        grad = parts[0].reshape(groups, ring, n_batch, tall, parts[0].shape[1])
        parts = xor_order([grad[:, r] for r in range(ring)], own)
        parts = [xor_order([p[:, z] for z in range(n_batch)], turn) for p in parts]
        parts = [[xor_order([z[g] for g in range(groups)], group) for z in p] for p in parts]
        parts = [jnp.stack([jnp.stack(z) for z in p]) for p in parts]
        return [parts[0]] + [p.astype(BF16) for p in parts[1:]]

    d_mix = over_groups(d_mix)
    out_parts = over_ring(by_place(out_parts, zed * 0))
    d_mix, grads_one, grads_two, out_parts = lax.optimization_barrier(
        (d_mix, grads_one, grads_two, out_parts)
    )
    out_part = kernel_call(
        functools.partial(half_kernel, ring=ring),
        "half_out",
        out_parts,
        [(out_parts[0].shape, BF16)],
    )[0]
    returned = turn_batch(produced)
    grads_one = swap(grads_one, "ctx", n_ctx, ring)
    grads_two = swap(grads_two, "ctx", n_ctx, 2 * ring)

    dq, dkv_own, *rest = attend_back(
        q, kv_all, band, d_mix, out_t, lse, heads, groups, ring, per
    )
    dkv_other, table_part = rest[: ring - 1], rest[ring - 1]
    dkv_other, grads_one, grads_two, out_part, returned = lax.optimization_barrier(
        (dkv_other, grads_one, grads_two, out_part, returned)
    )
    dkv_got = over_ring([dkv_own] + dkv_other)[1:]
    out_part = lax.all_to_all(out_part, "batch", split_axis=0, concat_axis=0, tiled=True)
    last_left, last_right = fold(kept_left, kept_right, grads_one, grads_two)
    last_left = swap(last_left, "ctx", n_ctx, 2 * ring)
    last_right = swap(last_right, "ctx", n_ctx, ring)

    grads_shape = (
        [((n_batch, groups, tall, 3 * part), F32)]
        + [((n_batch, groups, tall, 3 * part), BF16)] * (ring - 1)
        if fine
        else [((width, 3 * part), F32)]
    )
    d_packed, *packed_parts = kernel_call(
        functools.partial(
            weight_kernel,
            groups=groups,
            ring=ring,
            batch=n_batch,
            tall=tall,
            part=part,
            per=per,
        ),
        "weight",
        [dq, dkv_own, *dkv_got, *arrived],
        [((rows_own, 3 * wide), BF16)] + grads_shape,
        [((rows_own, width), BF16)],
    )
    late_rows = -(-(2 * width // lanes + head_count) // 8) * 8
    *d_normed, late = kernel_call(
        functools.partial(unproject_kernel, per=per, ring=ring, heads=heads, groups=groups),
        "unproject",
        [d_packed, w_head, attn_gain, ffn_gain_part, table_part, *arrived],
        [((per, width), F32)]
        + [((per, width), BF16)] * (groups - 1)
        + [((n_ctx * n_batch, late_rows, lanes), F32)],
    )
    packed_parts = over_ring(by_place(packed_parts, zed))
    packed_parts, d_normed, last_left, last_right, out_part = lax.optimization_barrier(
        (packed_parts, d_normed, last_left, last_right, out_part)
    )
    got = over_groups(d_normed)
    shape = packed_parts[0].shape[1:]
    packed_parts = kernel_call(
        functools.partial(half_kernel, ring=ring),
        "half_packed",
        packed_parts,
        [(shape, F32)] + [(shape, BF16)] * (n_batch - 1),
    )
    packed_parts = list(packed_parts)
    layer_out = kernel_call(
        combine_kernel,
        "combine",
        [returned, pick_t, middle, gate],
        [((per, width), BF16)],
    )[0][None]
    expert_in_grad, expert_out_grad = kernel_call(
        finish_kernel,
        "finish",
        [kept, grads_one, grads_two, last_left, last_right],
        [
            ((width // n_ctx, expert_in.shape[2]), F32),
            ((expert_out.shape[1] // n_ctx, width), F32),
        ],
    )
    packed_parts[-1], layer_out, expert_in_grad, expert_out_grad = lax.optimization_barrier(
        (packed_parts[-1], layer_out, expert_in_grad, expert_out_grad)
    )
    packed_parts = over_batch(packed_parts)
    tokens_grad = kernel_call(
        functools.partial(tokens_kernel, groups=groups),
        "tokens",
        [*got, tokens[0], attn_gain, d_middle],
        [((per, width), BF16)],
    )[0][None]
    packed_parts, layer_out, expert_in_grad, expert_out_grad, tokens_grad = (
        lax.optimization_barrier(
            (packed_parts, layer_out, expert_in_grad, expert_out_grad, tokens_grad)
        )
    )
    parts = kernel_call(
        functools.partial(quarter_kernel, batch=n_batch),
        "quarter",
        [out_part, *packed_parts],
        [((tall, 3 * part + width + lanes), BF16)] * groups,
    )

    late = lax.all_to_all(late, ("ctx", "batch"), split_axis=0, concat_axis=0, tiled=True)
    attn_gain_grad, ffn_gain_grad, d_table = kernel_call(
        late_kernel,
        "late",
        [late],
        [((width // lanes, lanes), F32)] * 2 + [((head_count, lanes), F32)],
    )
    attn_gain_grad = attn_gain_grad.reshape(width)
    ffn_gain_grad = ffn_gain_grad.reshape(width)
    bias_grad = d_table[:, : bias_table.shape[0]].T
    qkv_grad, out_weight_grad, router_grad = kernel_call(
        functools.partial(columns_kernel, groups=groups, ring=ring, part=part),
        "columns",
        over_groups(parts),
        [((tall, 3 * width), F32), ((tall, width), F32), ((n_batch, tall), F32)],
    )
    router_grad = router_grad.T
    return (
        layer_out,
        tokens_grad,
        attn_gain_grad,
        qkv_grad,
        out_weight_grad,
        bias_grad,
        ffn_gain_grad,
        router_grad,
        expert_in_grad[None],
        expert_out_grad[None],
    )


def solution(mesh):
    return jax.shard_map(
        body,
        mesh=mesh,
        in_specs=(
            P("batch", "ctx", None),
            P("batch", "ctx"),
            P("ctx", "batch", None, None),
            P(),
            P(("ctx", "batch"), None),
            P(("ctx", "batch"), None),
            P(),
            P(),
            P(("ctx", "batch"), None),
            P("batch", None, None),
            P("batch", None, None),
            P("batch", "ctx", None),
        ),
        out_specs=(
            P("batch", "ctx", None),
            P("batch", "ctx", None),
            P(),
            P(("ctx", "batch"), None),
            P(("ctx", "batch"), None),
            P(),
            P(),
            P(("ctx", "batch"), None),
            P("batch", "ctx", None),
            P("batch", "ctx", None),
        ),
        check_vma=False,
    )
```

```python
import functools
import math

import jax
import jax.numpy as jnp
import numpy as np
from jax import lax
from jax.experimental import pallas as pl
from jax.experimental.pallas import tpu as pltpu
from jax.sharding import PartitionSpec as P

BUCKETS = 32
MAX_DIST = 128
EPSILON = 1e-06
MASKED = -1e30
F32 = jnp.float32
BF16 = jnp.bfloat16


def bucket_limits():
    half_span = BUCKETS // 2
    exact_span = half_span // 2
    log_levels = half_span - exact_span
    limits = []
    for level_at in range(1, log_levels):
        bound_row = exact_span
        while (
            bound_row**log_levels * exact_span**level_at
            < MAX_DIST**level_at * exact_span**log_levels
        ):
            bound_row = bound_row + 1
        limits.append(bound_row)
    return limits


def relative_bucket(offsets):
    half_span = BUCKETS // 2
    exact_span = half_span // 2
    distance = np.abs(offsets)
    far = np.full(distance.shape, exact_span, np.int32)
    for bound_row in bucket_limits():
        far = far + (distance >= bound_row).astype(np.int32)
    near = np.where(distance < exact_span, distance, far)
    return near + np.where(offsets > 0, half_span, 0)


def band_buckets(block):
    column = np.arange(2 * block)
    rows = []
    for d in range(5):
        if d in (0, 4):
            offsets = np.full((2 * block,), (d - 2) * max(block, MAX_DIST), np.int64)
        else:
            offsets = (d - 2) * block + block - column
        rows.append(relative_bucket(offsets))
    return np.stack(rows)


def band_onehot(block):
    return band_buckets(block)[:, None, :] == np.arange(BUCKETS)[None, :, None]


def dot(a, b, dims, precision=None):
    return lax.dot_general(a, b, (dims, ((), ())), preferred_element_type=F32, precision=precision)


NN = ((1,), (0,))
NT = ((1,), (1,))
TN = ((0,), (0,))


def xor_order(parts, index):
    parts = list(parts)
    step = 1
    while step < len(parts):
        odd = (index // step) % 2 == 1
        parts = [jnp.where(odd, parts[i ^ step], parts[i]) for i in range(len(parts))]
        step = step * 2
    return parts


def vmem(count):
    return [pl.BlockSpec(memory_space=pltpu.VMEM)] * count


def place(ring):
    ctx = lax.axis_index("ctx").astype(jnp.int32)
    return ctx // ring, ctx % ring, lax.axis_index("batch").astype(jnp.int32)


def kernel_call(kernel, name, arrays, out_shape, scratch=()):
    return pl.pallas_call(
        kernel,
        out_shape=tuple(jax.ShapeDtypeStruct(shape, kind) for shape, kind in out_shape),
        in_specs=vmem(len(arrays)),
        out_specs=vmem(len(out_shape)),
        scratch_shapes=[
            pltpu.SMEM(shape, kind) if kind == jnp.int32 else pltpu.VMEM(shape, kind)
            for shape, kind in scratch
        ],
        compiler_params=pltpu.CompilerParams(vmem_limit_bytes=56 << 20),
        name=name,
    )(*arrays)


def swap(value, axis, size, mask):
    return lax.ppermute(value, axis, [(i, i ^ mask) for i in range(size)])


def column(row, size):
    return jnp.broadcast_to(row, (size, row.shape[1])).T


def first_kernel(tokens_ref, seg_ref, gain_ref, row_ref, message_ref, *cut_refs, part, ring):
    info = place(ring)
    tokens = tokens_ref[...].astype(F32)
    per, width = tokens.shape
    scale = lax.rsqrt(jnp.mean(tokens * tokens, axis=1, keepdims=True) + EPSILON)
    message_ref[:per, :] = (tokens * scale * gain_ref[...].astype(F32)[None, :]).astype(BF16)
    message_ref[per:, :] = jnp.zeros((message_ref.shape[0] - per, width), BF16)
    message_ref[per:, :per] = jnp.broadcast_to(
        seg_ref[...].astype(F32), (message_ref.shape[0] - per, per)
    ).astype(BF16)
    rows = row_ref[...].astype(F32)
    groups = len(cut_refs)
    cuts = [
        jnp.concatenate(
            [rows[:, k * width + g * part : k * width + (g + 1) * part] for k in range(3)], axis=1
        )
        for g in range(groups)
    ]
    for ref, cut in zip(cut_refs, xor_order(cuts, info[0])):
        ref[...] = cut.astype(BF16)


def row_place(info, g, r, z, ring, batch):
    return ((g ^ info[0]) * ring + (r ^ info[1])) * batch + (z ^ info[2])


def assemble(info, piece_refs, dest_ref, groups, batch, tall):
    ring = len(piece_refs)
    for r in range(ring):
        for z in range(batch):
            for g in range(groups):
                block = row_place(info, g, r, z, ring, batch)
                at = (z * groups + g) * tall
                dest_ref[pl.ds(pl.multiple_of(block * tall, 8), tall), :] = piece_refs[r][
                    at : at + tall, :
                ].astype(F32)


def project_kernel(*refs, groups, ring, batch, tall, part, per, pieces):
    x_refs, refs = refs[:groups], refs[groups:]
    w_refs, refs = refs[:pieces], refs[pieces:]
    q_ref, kv_ref, w_out, w_s = refs
    wide = 256
    if tall % 8 == 0:
        assemble(place(ring), w_refs, w_s, groups, batch, tall)
    else:
        w_s[...] = w_refs[0][...].astype(F32)
    gap = jnp.zeros((w_s.shape[0], wide - part), BF16)
    w = jnp.concatenate(
        [x for k in range(3) for x in (w_s[:, k * part : (k + 1) * part].astype(BF16), gap)],
        axis=1,
    )
    w_out[...] = w
    kv_ref[groups * per :, :] = jnp.zeros((kv_ref.shape[0] - groups * per, 2 * wide), BF16)
    seg = jnp.concatenate([x_ref[per : per + 1, :wide].astype(F32) for x_ref in x_refs], axis=0)
    seg = jnp.concatenate(
        [seg, jnp.zeros((kv_ref.shape[0] - groups * per - groups, wide), F32)], axis=0
    )
    kv_ref[groups * per :, :wide] = seg.astype(BF16)
    for m in range(groups):
        packed = dot(x_refs[m][:per, :], w_out[...], NN).astype(BF16)
        q_ref[m * per : (m + 1) * per, :] = packed[:, :wide]
        kv_ref[m * per : (m + 1) * per, :] = packed[:, wide:]


def slot_row(route, capacity):
    per = route.shape[1]
    earlier = lax.broadcasted_iota(jnp.int32, (per, per), 0) < lax.broadcasted_iota(
        jnp.int32, (per, per), 1
    )
    same = jnp.where((column(route, per) == route) & earlier, 1.0, 0.0)
    return route * capacity + jnp.sum(same, axis=0, keepdims=True)


def dispatch_kernel(route_ref, dz_ref, pick_ref, pick_t_ref, sent_ref, *, capacity):
    target = slot_row(route_ref[...].astype(F32), capacity).astype(jnp.int32)
    slots, per = pick_ref.shape
    slot = lax.broadcasted_iota(jnp.int32, (slots, per), 0)
    pick = jnp.where(slot == target, 1.0, 0.0)
    pick_ref[...] = pick.astype(BF16)
    pick_t_ref[...] = pick.T.astype(BF16)
    sent_ref[...] = dot(pick.astype(BF16), dz_ref[...], NN).astype(BF16)


def gather_kernel(*refs, groups, ring, batch, tall):
    w_refs, w_ref, w_s = refs[:-2], refs[-2], refs[-1]
    assemble(place(ring), w_refs, w_s, groups, batch, tall)
    w_ref[...] = w_s[...].astype(BF16)


def middle_kernel(*refs, groups, ring, batch, part, capacity):
    info = place(ring)
    mixed_refs, refs = refs[:groups], refs[groups:]
    w_ref, tokens_ref, gain_ref, pick_ref, route_ref, middle_ref, gate_ref = refs[:7]
    sent_refs = refs[7:]
    width = tokens_ref.shape[1]
    middle = tokens_ref[...].astype(F32)
    for m in range(groups):
        start = pl.multiple_of((info[0] ^ m) * part, 16)
        middle += dot(mixed_refs[m][...], w_ref[pl.ds(start, part), :width], NN)
    middle_ref[...] = middle
    scale = lax.rsqrt(jnp.mean(middle * middle, axis=1, keepdims=True) + EPSILON)
    normed = (middle * scale * gain_ref[...].astype(F32)[None, :]).astype(BF16)
    for m, ref in enumerate(sent_refs):
        start = pl.multiple_of((info[2] ^ m) * capacity, capacity)
        ref[...] = dot(pick_ref[pl.ds(start, capacity), :], normed, NN).astype(BF16)
    logits = dot(normed, w_ref[:, width:], NN)
    lane = lax.broadcasted_iota(jnp.int32, logits.shape, 1)
    logits = jnp.where(lane < batch, logits, MASKED)
    expo = jnp.exp(logits - jnp.max(logits, axis=1, keepdims=True))
    probs = expo / jnp.sum(expo, axis=1, keepdims=True)
    route = column(route_ref[...].astype(F32), logits.shape[1]).astype(jnp.int32)
    gate_ref[...] = jnp.sum(jnp.where(lane == route, probs, 0.0), axis=1, keepdims=True)


def branch_kernel(back_ref, *refs, groups, ring, batch, tall, part):
    info = place(ring)
    mixed_refs, refs = refs[:groups], refs[groups:]
    pick_t_ref, middle_ref, dz_ref, gain_ref, w_ref, rpart_ref = refs[:6]
    d_middle_ref, gain_part_ref = refs[6:8]
    d_mixed_refs, grad_refs = refs[8 : 8 + groups], refs[8 + groups :]
    width = middle_ref.shape[1]
    d_normed = dot(pick_t_ref[...], back_ref[...], NN)
    middle = middle_ref[...]
    scale = lax.rsqrt(jnp.mean(middle * middle, axis=1, keepdims=True) + EPSILON)
    gain_part_ref[...] = jnp.sum(d_normed * middle * scale, axis=0, keepdims=True)
    scaled = gain_ref[...].astype(F32)[None, :] * d_normed
    d_middle = (
        dz_ref[...].astype(F32)
        + scale * scaled
        - middle
        * (scale * scale * scale)
        * jnp.mean(scaled * middle, axis=1, keepdims=True)
    )
    d_middle_ref[...] = d_middle
    d_branch = d_middle.astype(BF16)
    for m in range(groups):
        start = pl.multiple_of((info[0] ^ m) * part, 16)
        d_mixed_refs[m][...] = dot(d_branch, w_ref[pl.ds(start, part), :width], NT).astype(BF16)
    for m in range(groups):
        start = pl.multiple_of((info[0] ^ m) * part, 16)
        grad = dot(mixed_refs[m][...], d_branch, TN)
        grad = jnp.concatenate([grad, rpart_ref[pl.ds(start, part), :]], axis=1)
        if tall % 8 == 0:
            scatter_rows(info, grad, m, grad_refs, ring, batch, tall, 0)
        else:
            grad_refs[0][pl.ds(start, part), :] = grad


def scatter_rows(info, grad, g, grad_refs, ring, batch, tall, turn):
    for z in range(batch):
        rows = [
            grad[(r * batch + z) * tall : (r * batch + z + 1) * tall, :] for r in range(ring)
        ]
        for ref, row in zip(grad_refs, xor_order(rows, info[1])):
            ref[z ^ turn, g] = row.astype(ref.dtype)


def weight_kernel(dq_ref, *refs, groups, ring, batch, tall, part, per):
    info = place(ring)
    got_refs, refs = refs[:ring], refs[ring:]
    x_refs, dp_ref, grad_refs, x_s = refs[:groups], refs[groups], refs[groups + 1 : -1], refs[-1]
    wide = 256
    for m in range(groups):
        rows = slice(m * per, (m + 1) * per)
        dkv = got_refs[0][rows, :]
        for ref in got_refs[1:]:
            dkv += ref[rows, :].astype(F32)
        dp_ref[rows, :wide] = dq_ref[rows, :]
        dp_ref[rows, wide:] = dkv.astype(BF16)
        x_s[rows, :] = x_refs[m][:per, :]
    share = ring * batch * tall
    for g in range(groups):
        grad = dot(x_s[:, g * share : (g + 1) * share], dp_ref[...], TN)
        grad = jnp.concatenate([grad[:, k * wide : k * wide + part] for k in range(3)], axis=1)
        if tall % 8 == 0:
            scatter_rows(info, grad, g ^ info[0], grad_refs, ring, batch, tall, info[2])
        else:
            grad_refs[0][g * share : (g + 1) * share, :] = grad


def unproject_kernel(
    dp_ref, w_ref, gain_ref, gain2_ref, table_ref, *refs, per, ring, heads, groups
):
    x_refs, d_refs, late_ref = refs[:groups], refs[groups : 2 * groups], refs[-1]
    width = gain2_ref.shape[1]
    total = jnp.zeros((1, width), F32)
    for m, ref in enumerate(d_refs):
        rows = slice(m * per, (m + 1) * per)
        d_normed = dot(dp_ref[rows, :], w_ref[...], NT)
        ref[...] = d_normed.astype(ref.dtype)
        total += jnp.sum(d_normed * x_refs[m][:per, :].astype(F32), axis=0, keepdims=True)
    total = total / gain_ref[...].astype(F32)[None, :]
    late_ref[0] = jnp.zeros(late_ref.shape[1:], F32)
    count = width // 128
    for k in range(count):
        late_ref[0, k : k + 1, :] = total[:, k * 128 : (k + 1) * 128]
        late_ref[0, count + k : count + k + 1, :] = gain2_ref[:, k * 128 : (k + 1) * 128]
    group = place(ring)[0]
    for h in range(heads):
        late_ref[0, pl.ds(2 * count + group * heads + h, 1), :] = table_ref[h : h + 1, :]
    whole = late_ref[0]

    @pl.loop(1, late_ref.shape[0])
    def _(k):
        late_ref[k] = whole


def late_kernel(got_ref, gain1_ref, gain2_ref, table_ref):
    total = jnp.sum(got_ref[...], axis=0)
    count, heads = gain1_ref.shape[0], table_ref.shape[0]
    gain1_ref[...] = total[:count, :]
    gain2_ref[...] = total[count : 2 * count, :]
    table_ref[...] = total[2 * count : 2 * count + heads, :]


def half_kernel(*refs, ring):
    total = refs[0][...]
    for ref in refs[1:ring]:
        total += ref[...].astype(F32)
    if len(refs) == ring + 1:
        refs[ring][...] = total.astype(BF16)
    else:
        for m, ref in enumerate(refs[ring:]):
            ref[...] = total[m].astype(ref.dtype)


def quarter_kernel(two_ref, *refs, batch):
    one = refs[0][...]
    for ref in refs[1:batch]:
        one += ref[...].astype(F32)
    two = jnp.sum(two_ref[...].astype(F32), axis=0)
    cut = one.shape[2]
    for m, ref in enumerate(refs[batch:]):
        ref[:, :cut] = one[m].astype(BF16)
        ref[:, cut:] = two[m].astype(BF16)


def columns_kernel(*refs, groups, ring, part):
    qkv_ref, out_ref, router_ref = refs[groups:]
    cut, width = 3 * part, out_ref.shape[1]
    parts = xor_order([ref[:, :cut].astype(F32) for ref in refs[:groups]], place(ring)[0])
    qkv_ref[...] = jnp.concatenate(
        [p[:, k * part : (k + 1) * part] for k in range(3) for p in parts], axis=1
    )
    total = sum(ref[:, cut:].astype(F32) for ref in refs[:groups])
    out_ref[...] = total[:, :width]
    router = total[:, width:]
    spare = jnp.zeros((router.shape[1] - router.shape[0], router.shape[1]), F32)
    router = jnp.concatenate([router, spare], axis=0).T
    router_ref[...] = router[: router_ref.shape[0], : router_ref.shape[1]]


def tokens_kernel(*refs, groups):
    tokens_ref, gain_ref, d_middle_ref, out_ref = refs[groups:]
    d_normed = refs[0][...]
    for ref in refs[1:groups]:
        d_normed += ref[...].astype(F32)
    tokens = tokens_ref[...].astype(F32)
    scale = lax.rsqrt(jnp.mean(tokens * tokens, axis=1, keepdims=True) + EPSILON)
    scaled = gain_ref[...].astype(F32)[None, :] * d_normed
    out_ref[...] = (
        d_middle_ref[...]
        + scale * scaled
        - tokens
        * (scale * scale * scale)
        * jnp.mean(scaled * tokens, axis=1, keepdims=True)
    ).astype(BF16)


def combine_kernel(got_ref, pick_t_ref, middle_ref, gate_ref, out_ref):
    returned = dot(pick_t_ref[...], got_ref[...], NN)
    out_ref[...] = (middle_ref[...] + gate_ref[...] * returned).astype(BF16)


def ring_total(refs):
    return sum(ref[...].astype(F32) for ref in refs)


def merge_kernel(*refs, ring):
    one_ref, two_ref = refs[2 * ring :]
    g1, g2 = ring_total(refs[:ring]).astype(BF16), ring_total(refs[ring : 2 * ring]).astype(BF16)
    rows = g1.shape[0]

    def put(ref):
        ref[:rows, :] = g1
        ref[rows:, :] = g2

    pl.when(pl.program_id(0) <= 1)(lambda: put(one_ref))
    pl.when(pl.program_id(0) >= 2)(lambda: put(two_ref))


def merge(g1, g2):
    groups, rows, width = g1[0].shape
    assert groups == 4
    ring = len(g1)
    half = width // 2
    order = lambda s: (jnp.where(s == 0, 1, jnp.where(s == 3, 2, 3)), 0, jnp.where(s >= 2, 1, 0))
    message = jax.ShapeDtypeStruct((2, 2 * rows, half), BF16)
    return pl.pallas_call(
        functools.partial(merge_kernel, ring=ring),
        grid=(groups,),
        out_shape=(message, message),
        in_specs=[pl.BlockSpec((None, rows, half), order)] * (2 * ring),
        out_specs=[
            pl.BlockSpec((None, 2 * rows, half), lambda s: (jnp.minimum(s, 1), 0, 0)),
            pl.BlockSpec((None, 2 * rows, half), lambda s: (jnp.where(s <= 2, 1, 0), 0, 0)),
        ],
        compiler_params=pltpu.CompilerParams(
            dimension_semantics=("arbitrary",), vmem_limit_bytes=56 << 20
        ),
        name="merge",
    )(*g1, *g2)


def fold_kernel(*refs, ring):
    one_ref, two_ref, left_out, right_out = refs[4 * ring :]
    rows = refs[0].shape[0]
    for k, (add_ref, ref) in enumerate(((one_ref, left_out), (two_ref, right_out))):
        for part in range(2):
            at = (2 * k + part) * ring
            cut = slice(part * rows, (part + 1) * rows)
            ref[cut, :] = (ring_total(refs[at : at + ring]) + add_ref[cut, :].astype(F32)).astype(BF16)


def fold(g1, g2, one, two):
    rows, half = g1[0].shape[1], one.shape[2]
    ring = len(g1)
    left = pl.BlockSpec((None, rows, half), lambda s: (2, 0, 0))
    right = pl.BlockSpec((None, rows, half), lambda s: (1, 0, 1))
    second = pl.BlockSpec((None, 2 * rows, half), lambda s: (1, 0, 0))
    whole = pl.BlockSpec((2 * rows, half), lambda s: (0, 0))
    return pl.pallas_call(
        functools.partial(fold_kernel, ring=ring),
        grid=(1,),
        out_shape=(jax.ShapeDtypeStruct((2 * rows, half), BF16),) * 2,
        in_specs=[left] * (2 * ring) + [right] * (2 * ring) + [second] * 2,
        out_specs=[whole] * 2,
        compiler_params=pltpu.CompilerParams(vmem_limit_bytes=56 << 20),
        name="fold",
    )(*g1, *g2, *g1, *g2, one, two)


def finish_kernel(*refs, ring):
    one_ref, two_ref, left_ref, right_ref, in_ref, out_ref = refs[2 * ring :]
    tall, width = in_ref.shape[0], out_ref.shape[1]
    half, rows = width // 2, out_ref.shape[0]
    g1, g2 = ring_total(refs[:ring]), ring_total(refs[ring : 2 * ring])
    for at, first_ref, last_ref in ((0, one_ref, left_ref), (half, two_ref, right_ref)):
        cut = slice(at, at + half)
        more = first_ref[...].astype(F32) + last_ref[...].astype(F32)
        total = g1[:, cut] + more[:rows, :]
        for j in range(in_ref.shape[1] // width):
            in_ref[:, j * width + at : j * width + at + half] = total[j * tall : (j + 1) * tall, :]
        out_ref[:, cut] = g2[:, cut] + more[rows:, :]


def finish(g1, g2, one, two, left, right, tall, hidden):
    rows, width = g1[0].shape[1:]
    ring, half = len(g1), width // 2
    mine = pl.BlockSpec((None, rows, width), lambda s: (0, 0, 0))
    first = pl.BlockSpec((None, 2 * rows, half), lambda s: (0, 0, 0))
    whole = pl.BlockSpec((2 * rows, half), lambda s: (0, 0))
    return pl.pallas_call(
        functools.partial(finish_kernel, ring=ring),
        grid=(1,),
        out_shape=(
            jax.ShapeDtypeStruct((tall, hidden), F32),
            jax.ShapeDtypeStruct((rows, width), F32),
        ),
        in_specs=[mine] * (2 * ring) + [first] * 2 + [whole] * 2,
        out_specs=[
            pl.BlockSpec((tall, hidden), lambda s: (0, 0)),
            pl.BlockSpec((rows, width), lambda s: (0, 0)),
        ],
        compiler_params=pltpu.CompilerParams(vmem_limit_bytes=56 << 20),
        name="finish",
    )(*g1, *g2, one, two, left, right)


SEGMENTS = 8


def set_bias(band_ref, bias_s, heads, block):
    @pl.loop(0, heads)
    def _(h):
        @pl.loop(0, 5)
        def _(d):
            row = jnp.broadcast_to(band_ref[h, pl.ds(d, 1), :], (block, 2 * block))
            bias_s[h, d] = pltpu.roll(row, block, 1, stride=1, stride_axis=0)[:, :block]


def key_at(kb, info, ring, groups):
    return ((kb % ring) ^ info[1]) * groups + ((kb // ring) ^ info[0])


def set_spans(info, kv_refs, seg_s, span_s, groups, ring, block):
    rows = [ref[groups * block : groups * block + groups, :block].astype(F32) for ref in kv_refs]
    seg = jnp.concatenate(rows, axis=0)
    seg_s[...] = seg
    blocks = groups * ring
    low, high = seg[:, 0:1], seg[:, block - 1 : block]
    at = lax.broadcasted_iota(jnp.int32, (blocks, 1), 0)
    natural = (((at % groups) ^ info[0]) * ring + ((at // groups) ^ info[1])).astype(F32)
    for i in range(groups):
        meets = (low <= high[i : i + 1, :]) & (high >= low[i : i + 1, :])
        first = jnp.min(jnp.where(meets, natural, float(blocks)))
        last = jnp.max(jnp.where(meets, natural, -1.0))
        span_s[i, 0] = first.astype(jnp.int32)
        span_s[i, 1] = last.astype(jnp.int32) + 1


def with_extras(pair, half, extras):
    lane = lax.broadcasted_iota(jnp.int32, pair.shape, 1)
    kept = jnp.where(lane // 64 == half, pair, 0.0)
    spot = lane - (1 - half) * 64
    for at, extra in extras:
        if at is None:
            kept = jnp.where((spot >= 0) & (spot < SEGMENTS), extra(spot), kept)
        else:
            kept = jnp.where(spot == at, extra, kept)
    return kept


def key_extras(seg_col):
    return (None, lambda spot: jnp.where(spot.astype(F32) == seg_col, 0.0, MASKED))


def query_extras(seg_col):
    return (None, lambda spot: jnp.where(spot.astype(F32) == seg_col, 1.0, 0.0))


def three_parts(value):
    high = value.astype(BF16).astype(F32)
    middle = (value - high).astype(BF16).astype(F32)
    return high, middle, value - high - middle


def set_keys(kv_refs, seg_s, heads, groups, block, ones, key_s, turned_s, turn, value_s=None):
    wide = 256
    for r, ref in enumerate(kv_refs):

        @pl.loop(0, groups)
        def _(g):
            at, rows = r * groups + g, pl.ds(pl.multiple_of(g * block, block), block)
            seg_col = column(seg_s[pl.ds(at, 1), :], 128)
            turned_s[at] = ref[rows, turn : turn + wide].astype(F32).T.astype(BF16)
            for h in range(heads):
                lane = (h // 2) * 128
                extras = [key_extras(seg_col)] + [(SEGMENTS + n, 1.0) for n in range(ones)]
                key = with_extras(ref[rows, lane : lane + 128].astype(F32), h % 2, extras)
                key_s[at, h] = key.astype(BF16)
                if value_s is not None:
                    lane = wide + lane
                    extras = [(n, 1.0) for n in range(ones)]
                    value = with_extras(ref[rows, lane : lane + 128].astype(F32), h % 2, extras)
                    value_s[at, h] = value.astype(BF16)


def two_step(first, last, start, finish, even, odd):
    start(first, even)

    @pl.loop(0, (last - first + 1) // 2)
    def _(j):
        kb = first + 2 * j
        start(jnp.minimum(kb + 1, last - 1), odd)
        finish(kb, even)

        @pl.when(kb + 1 < last)
        def _():
            start(jnp.minimum(kb + 2, last - 1), even)
            finish(kb + 1, odd)


def attend_kernel(q_ref, *refs, heads, groups, ring, block):
    info = place(ring)
    kv_refs, refs = refs[:ring], refs[ring:]
    band_ref, ot_ref, lse_ref = refs[:3]
    mixed_refs, refs = refs[3 : 3 + groups], refs[3 + groups :]
    bias_s, seg_s, span_s, key_s, vt_s, query_s, stat_s, acc_s, even_s, odd_s = refs
    set_bias(band_ref, bias_s, heads, block)
    set_spans(info, kv_refs, seg_s, span_s, groups, ring, block)
    set_keys(kv_refs, seg_s, heads, groups, block, 0, key_s, vt_s, 256)

    @pl.loop(0, groups)
    def _(i):
        qb = (i ^ info[0]) * ring + info[1]
        rows = pl.ds(pl.multiple_of(i * block, block), block)
        seg_col = column(seg_s[pl.ds(i, 1), :], 128)
        for h in range(heads):
            lane = (h // 2) * 128
            query = q_ref[rows, lane : lane + 128].astype(F32) * 0.125
            query_s[h] = with_extras(query, h % 2, [query_extras(seg_col)]).astype(BF16)
        stat_s[0:heads] = jnp.full((heads, 1, block), MASKED, F32)
        stat_s[heads : 2 * heads] = jnp.zeros((heads, 1, block), F32)
        acc_s[...] = jnp.zeros_like(acc_s)

        def start(kb, score_s):
            at = key_at(kb, info, ring, groups)
            d = jnp.clip(kb - qb, -2, 2) + 2
            for h in range(heads):
                score_s[h] = dot(key_s[at, h], query_s[h], NT) + bias_s[h, d]

        def finish(kb, score_s):
            at = key_at(kb, info, ring, groups)
            tops = [
                jnp.maximum(stat_s[h], jnp.max(score_s[h], axis=0, keepdims=True))
                for h in range(heads)
            ]
            expos = [jnp.exp(score_s[h] - tops[h]) for h in range(heads)]
            for h in range(heads):
                decay = jnp.exp(stat_s[h] - tops[h])
                stat_s[h] = tops[h]
                stat_s[heads + h] = stat_s[heads + h] * decay + jnp.sum(
                    expos[h], axis=0, keepdims=True
                )
                value_t = vt_s[at, h * 64 : (h + 1) * 64, :]
                acc_s[h] = acc_s[h] * decay + dot(value_t, expos[h].astype(BF16), NN)

        two_step(span_s[i, 0], span_s[i, 1], start, finish, even_s, odd_s)

        for h in range(heads):
            total = stat_s[heads + h]
            ot_ref[i, h * 64 : (h + 1) * 64, :] = acc_s[h] / total
            lse_ref[i, h : h + 1, :] = stat_s[h] + jnp.log(total)

    for i in range(groups):
        mixed_refs[i][...] = ot_ref[i].T.astype(BF16)


def attend(q, kv_all, band, heads, groups, ring, block):
    width = heads * 64
    return kernel_call(
        functools.partial(attend_kernel, heads=heads, groups=groups, ring=ring, block=block),
        "attend",
        [q, *kv_all, band],
        [((groups, width, block), F32), ((groups, 8, block), F32)]
        + [((block, width), BF16)] * groups,
        [
            ((heads, 5, block, block), F32),
            ((groups * ring, block), F32),
            ((groups, 2), jnp.int32),
            ((groups * ring, heads, block, 128), BF16),
            ((groups * ring, 256, block), BF16),
            ((heads, block, 128), BF16),
            ((2 * heads, 1, block), F32),
            ((heads, 64, block), F32),
            ((heads, block, block), F32),
            ((heads, block, block), F32),
        ],
    )


def attend_back_kernel(q_ref, *refs, heads, groups, ring, block):
    info = place(ring)
    kv_refs, refs = refs[:ring], refs[ring:]
    band_ref, refs = refs[0], refs[1:]
    dmix_refs, refs = refs[:groups], refs[groups:]
    ot_ref, lse_ref, dq_ref, own_ref = refs[:4]
    other_refs, refs = refs[4 : 3 + ring], refs[3 + ring :]
    dband_ref, bias_s, seg_s, span_s, key_s, value_s, kt_s, query_s, plain_s, dout_s = refs[:10]
    dplain_s, dqt_s, dkv_s, dbias_s, dmix_s = refs[10:]
    wide = 256
    blocks = groups * ring
    set_bias(band_ref, bias_s, heads, block)
    set_spans(info, kv_refs, seg_s, span_s, groups, ring, block)
    set_keys(kv_refs, seg_s, heads, groups, block, 3, key_s, kt_s, 0, value_s)
    for i in range(groups):
        dmix_s[i, :, : heads * 64] = dmix_refs[i][...].astype(F32)
        dmix_s[i, :, heads * 64 :] = jnp.zeros((block, wide - heads * 64), F32)

    @pl.loop(0, blocks)
    def _(at):
        dkv_s[at] = jnp.zeros(dkv_s.shape[1:], F32)

    @pl.loop(0, heads)
    def _(h):
        dbias_s[h] = jnp.zeros(dbias_s.shape[1:], F32)

    @pl.loop(0, groups)
    def _(i):
        qb = (i ^ info[0]) * ring + info[1]
        rows = pl.ds(pl.multiple_of(i * block, block), block)
        seg_col = column(seg_s[pl.ds(i, 1), :], 128)
        dmix = dmix_s[i]
        dmix_t = dmix.T
        for h in range(heads):
            cut, lane = slice(h * 64, (h + 1) * 64), (h // 2) * 128
            delta = jnp.sum(dmix_t[cut, :] * ot_ref[i, cut, :], axis=0, keepdims=True)
            delta = three_parts(column(-delta, 128))
            lse = three_parts(column(-lse_ref[i, h : h + 1, :], 128))
            query = q_ref[rows, lane : lane + 128].astype(F32) * 0.125
            extras = [query_extras(seg_col)] + [(SEGMENTS + n, lse[n]) for n in range(3)]
            query_s[h] = with_extras(query, h % 2, extras).astype(BF16)
            plain_s[h] = with_extras(query, h % 2, []).astype(BF16)
            d_out = dmix[:, lane : lane + 128]
            extras = [(n, delta[n]) for n in range(3)]
            dout_s[h] = with_extras(d_out, h % 2, extras).astype(BF16)
            dplain_s[h] = with_extras(d_out, h % 2, []).astype(BF16)
        dqt_s[...] = jnp.zeros_like(dqt_s)

        @pl.loop(span_s[i, 0], span_s[i, 1])
        def _(kb):
            at = key_at(kb, info, ring, groups)
            d = jnp.clip(kb - qb, -2, 2) + 2
            softs = [
                jnp.exp(dot(key_s[at, h], query_s[h], NT) + bias_s[h, d]) for h in range(heads)
            ]
            d_scores = [
                (softs[h] * dot(value_s[at, h], dout_s[h], NT)).astype(BF16) for h in range(heads)
            ]
            for h in range(heads):
                lane = (h // 2) * 128
                dkv_s[at, :, wide + lane : wide + lane + 128] += dot(
                    softs[h].astype(BF16), dplain_s[h], NN
                )
                dkv_s[at, :, lane : lane + 128] += dot(d_scores[h], plain_s[h], NN)
                dqt_s[h * 64 : (h + 1) * 64, :] += dot(
                    kt_s[at, h * 64 : (h + 1) * 64, :], d_scores[h], NN
                )
                dbias_s[h, d] += d_scores[h].astype(F32)

        pad = jnp.zeros((wide - heads * 64, block), F32)
        dq_ref[rows, :] = (jnp.concatenate([dqt_s[...], pad], axis=0) * 0.125).T.astype(BF16)

    for r in range(ring):

        @pl.loop(0, groups)
        def _(g):
            at, rows = r * groups + g, pl.ds(pl.multiple_of(g * block, block), block)
            if r == 0:
                own_ref[rows, :] = dkv_s[at]
            else:
                other_refs[r - 1][rows, :] = dkv_s[at].astype(BF16)

    buckets = band_buckets(block)
    zero = jnp.zeros((block, block), F32)
    lane = lax.broadcasted_iota(jnp.int32, (1, 128), 1)
    column_at = lax.broadcasted_iota(jnp.int32, (1, 2 * block), 1)
    dband_ref[...] = jnp.zeros_like(dband_ref)

    @pl.loop(0, heads)
    def _(h):
        table = jnp.zeros((1, 128), F32)
        for d in range(5):
            if d in (0, 4):
                tile = jnp.sum(dbias_s[h, d], axis=0, keepdims=True)
                tile = jnp.concatenate([tile, zero[:1]], axis=1)
            else:
                tile = jnp.concatenate([zero, dbias_s[h, d]], axis=1)
                tall = block
                while tall > 1:
                    tall = tall // 2
                    tile = tile[:tall] + pltpu.roll(tile[tall:], 2 * block - tall, 1)
            for bucket in sorted(set(buckets[d].tolist())):
                held = np.nonzero(buckets[d] == bucket)[0]
                keep = (column_at >= int(held[0])) & (column_at <= int(held[-1]))
                held_sum = jnp.sum(jnp.where(keep, tile, 0.0), axis=1, keepdims=True)
                table += jnp.where(lane == bucket, held_sum, 0.0)
        dband_ref[pl.ds(h, 1), :] = table


def attend_back(q, kv_all, band, d_mix, out_t, lse, heads, groups, ring, block):
    own = groups * block
    blocks = groups * ring
    return kernel_call(
        functools.partial(attend_back_kernel, heads=heads, groups=groups, ring=ring, block=block),
        "attend_back",
        [q, *kv_all, band, *d_mix, out_t, lse],
        [((own, 256), BF16), ((own, 512), F32)]
        + [((own, 512), BF16)] * (ring - 1)
        + [((8, 128), F32)],
        [((heads, 5, block, block), F32), ((blocks, block), F32), ((groups, 2), jnp.int32)]
        + [((blocks, heads, block, 128), BF16)] * 2
        + [((blocks, 256, block), BF16)]
        + [((heads, block, 128), BF16)] * 4
        + [
            ((heads * 64, block), F32),
            ((blocks, block, 512), F32),
            ((heads, 5, block, block), F32),
            ((groups, block, 256), F32),
        ],
    )


def expert_kernel(*refs, experts, ring, batch):
    info = place(ring)
    piece_refs, refs = refs[:batch], refs[batch:]
    dz_ref, router_ref, w1_ref, w2_ref = refs[:4]
    prod_ref, back_ref, d_logits_ref, rows_ref, dret_ref, hidden_ref, d_pre_ref = refs[4:11]
    prob_s, prod_s, back_s = refs[11:]
    capacity = piece_refs[0].shape[0]
    step = pl.program_id(0)
    me = info[2]
    lane = lax.broadcasted_iota(jnp.int32, prob_s.shape, 1)

    @pl.when(step == 0)
    def _():
        for m, ref in enumerate(piece_refs):
            start = pl.multiple_of((me ^ m) * capacity, capacity)
            rows_ref[pl.ds(start, capacity), :] = ref[...]
        logits = dot(rows_ref[...], router_ref[...], NN)
        logits = jnp.where(lane < experts, logits, MASKED)
        expo = jnp.exp(logits - jnp.max(logits, axis=1, keepdims=True))
        probs = expo / jnp.sum(expo, axis=1, keepdims=True)
        prob_s[...] = probs
        gate = jnp.sum(jnp.where(lane == me, probs, 0.0), axis=1, keepdims=True)
        dret_ref[...] = (gate * dz_ref[...].astype(F32)).astype(BF16)
        prod_s[...] = jnp.zeros_like(prod_s)
        back_s[...] = jnp.zeros_like(back_s)

    w1 = w1_ref[...]
    w2 = w2_ref[...]
    pre = dot(rows_ref[...], w1, NN)
    cumulative = 0.5 * (1.0 + lax.erf(pre * (1.0 / math.sqrt(2.0))))
    density = jnp.exp(-0.5 * pre * pre) * (1.0 / math.sqrt(2.0 * math.pi))
    hidden = (pre * cumulative).astype(BF16)
    d_hidden = dot(dret_ref[...], w2, NT)
    d_pre = (d_hidden * (cumulative + pre * density)).astype(BF16)
    hidden_ref[...] = hidden
    d_pre_ref[...] = d_pre
    prod_s[...] += dot(hidden, w2, NN)
    back_s[...] += dot(d_pre, w1, NT)

    @pl.when(step == pl.num_programs(0) - 1)
    def _():
        probs = prob_s[...]
        gate = jnp.sum(jnp.where(lane == me, probs, 0.0), axis=1, keepdims=True)
        chosen = jnp.where(lane == me, 1.0, 0.0)
        produced = prod_s[...].astype(BF16)
        prod_ref[...] = produced
        d_gate = jnp.sum(
            dz_ref[...].astype(F32) * produced.astype(F32), axis=1, keepdims=True
        )
        d_logits = (d_gate * probs * (chosen - gate)).astype(BF16)
        back = back_s[...].astype(BF16).astype(F32) + dot(d_logits, router_ref[...], NT)
        back_ref[...] = back.astype(BF16)
        d_logits_ref[...] = d_logits


def expert_layer(pieces, dz, w_both, w1, w2, ring):
    batch = len(pieces)
    capacity, width = pieces[0].shape
    slots = batch * capacity
    lanes = 128
    hidden = w1.shape[1]
    cut = width
    fixed = lambda j: (0, 0)
    whole = pl.BlockSpec((slots, width), fixed)
    return pl.pallas_call(
        functools.partial(expert_kernel, experts=batch, ring=ring, batch=batch),
        grid=(hidden // cut,),
        in_specs=[pl.BlockSpec((capacity, width), fixed)] * batch
        + [
            whole,
            pl.BlockSpec((width, lanes), lambda j: (0, width // lanes)),
            pl.BlockSpec((width, cut), lambda j: (0, j)),
            pl.BlockSpec((cut, width), lambda j: (j, 0)),
        ],
        out_specs=[
            whole,
            whole,
            pl.BlockSpec((slots, lanes), fixed),
            whole,
            whole,
            pl.BlockSpec((slots, cut), lambda j: (0, j)),
            pl.BlockSpec((slots, cut), lambda j: (0, j)),
        ],
        scratch_shapes=[
            pltpu.VMEM((slots, lanes), F32),
            pltpu.VMEM((slots, width), F32),
            pltpu.VMEM((slots, width), F32),
        ],
        out_shape=(
            jax.ShapeDtypeStruct((slots, width), BF16),
            jax.ShapeDtypeStruct((slots, width), BF16),
            jax.ShapeDtypeStruct((slots, lanes), BF16),
            jax.ShapeDtypeStruct((slots, width), BF16),
            jax.ShapeDtypeStruct((slots, width), BF16),
            jax.ShapeDtypeStruct((slots, hidden), BF16),
            jax.ShapeDtypeStruct((slots, hidden), BF16),
        ),
        compiler_params=pltpu.CompilerParams(
            dimension_semantics=("arbitrary",), vmem_limit_bytes=56 << 20
        ),
        name="experts",
    )(*pieces, dz, w_both, w1, w2)


def expert_grad_kernel(
    d_logits_ref, rows_ref, dret_ref, hidden_ref, d_pre_ref, *refs, groups, ring
):
    info = place(ring)
    router_ref, g1_refs, g2_refs, rows_t = refs[0], refs[1 : 1 + ring], refs[1 + ring : -1], refs[-1]

    @pl.when(pl.program_id(0) == 0)
    def _():
        rows_t[...] = rows_ref[...].astype(F32).T.astype(BF16)
        router_ref[...] = dot(rows_t[...], d_logits_ref[...], NN)

    g2 = dot(hidden_ref[...], dret_ref[...], TN).astype(BF16)
    share = g2.shape[0] // ring
    parts = [g2[c * share : (c + 1) * share, :] for c in range(ring)]
    for ref, rows in zip(g2_refs, xor_order(parts, info[1])):
        ref[pl.program_id(0) ^ info[0]] = rows
    g1 = dot(rows_t[...], d_pre_ref[...], NN).astype(BF16)
    tall = g1.shape[0] // (groups * ring)
    for g in range(groups):
        parts = [
            g1[(g * ring + c) * tall : (g * ring + c + 1) * tall, :] for c in range(ring)
        ]
        for ref, rows in zip(g1_refs, xor_order(parts, info[1])):
            ref[g ^ info[0]] = rows


def expert_grads(d_logits, rows, d_ret, hidden, d_pre, groups, ring):
    slots, width = rows.shape
    lanes = d_logits.shape[1]
    devices = groups * ring
    share = hidden.shape[1] // devices
    cut = share * ring
    tall = width // devices
    tiles = hidden.shape[1] // cut
    return pl.pallas_call(
        functools.partial(expert_grad_kernel, groups=groups, ring=ring),
        grid=(tiles,),
        in_specs=[
            pl.BlockSpec((slots, lanes), lambda j: (0, 0)),
            pl.BlockSpec((slots, width), lambda j: (0, 0)),
            pl.BlockSpec((slots, width), lambda j: (0, 0)),
            pl.BlockSpec((slots, cut), lambda j: (0, j)),
            pl.BlockSpec((slots, cut), lambda j: (0, j)),
        ],
        out_specs=[pl.BlockSpec((width, lanes), lambda j: (0, 0))]
        + [pl.BlockSpec((groups, tall, cut), lambda j: (0, j, 0))] * ring
        + [pl.BlockSpec((groups, share, width), lambda j: (0, 0, 0))] * ring,
        scratch_shapes=[pltpu.VMEM((width, slots), BF16)],
        out_shape=(jax.ShapeDtypeStruct((width, lanes), F32),)
        + (jax.ShapeDtypeStruct((groups, tiles * tall, cut), BF16),) * ring
        + (jax.ShapeDtypeStruct((groups, share, width), BF16),) * ring,
        compiler_params=pltpu.CompilerParams(
            dimension_semantics=("arbitrary",), vmem_limit_bytes=56 << 20
        ),
        name="expert_grads",
    )(d_logits, rows, d_ret, hidden, d_pre)


def body(
    tokens,
    seg_ids,
    routes,
    attn_gain,
    query_key_value_weight,
    attention_output_weight,
    bias_table,
    ffn_gain,
    router_weight,
    expert_in,
    expert_out,
    out_grad,
):
    n_ctx = lax.axis_size("ctx")
    n_batch = lax.axis_size("batch")
    per, width = tokens.shape[1:]
    head_count = bias_table.shape[1]
    groups = math.gcd(head_count, n_ctx)
    ring = n_ctx // groups
    heads = head_count // groups
    part = heads * 64
    tall = query_key_value_weight.shape[0]
    lanes = 128
    wide = 256
    rows_own = groups * per
    capacity = max(2, 2 * per // n_batch)
    slots = n_batch * capacity
    fine = tall % 8 == 0
    ctx = lax.axis_index("ctx").astype(jnp.int32)
    zed = lax.axis_index("batch").astype(jnp.int32)
    group, own = ctx // ring, ctx % ring

    def over_groups(parts):
        return [
            parts[m] if m == 0 else swap(parts[m], "ctx", n_ctx, ring * m) for m in range(groups)
        ]

    def over_ring(parts):
        return [parts[m] if m == 0 else swap(parts[m], "ctx", n_ctx, m) for m in range(ring)]

    def over_batch(parts):
        return [
            parts[m] if m == 0 else swap(parts[m], "batch", n_batch, m) for m in range(n_batch)
        ]

    def turn_batch(rows):
        rows = rows.reshape(n_batch, capacity, width)
        rows = lax.all_to_all(rows, "batch", split_axis=0, concat_axis=0, tiled=True)
        return rows.reshape(slots, width)

    def natural(pieces, columns):
        pieces = [p.reshape(n_batch, groups, tall, columns) for p in pieces]
        pieces = xor_order(pieces, own)
        pieces = [xor_order([c[z] for z in range(n_batch)], zed) for c in pieces]
        pieces = [[xor_order([b[g] for g in range(groups)], group) for b in c] for c in pieces]
        order = [(g, r, z) for g in range(groups) for r in range(ring) for z in range(n_batch)]
        return [jnp.concatenate([pieces[r][z][g] for g, r, z in order], axis=0)]

    first = kernel_call(
        functools.partial(first_kernel, part=part, ring=ring),
        "first",
        [tokens[0], seg_ids, attn_gain, query_key_value_weight],
        [((per + 16, width), BF16)] + [((tall, 3 * part), BF16)] * groups,
    )
    message, cuts = first[0], list(first[1:])
    cuts = over_groups(cuts)
    message, cuts = lax.optimization_barrier((message, cuts))
    arrived = over_groups([message] * groups)
    both = jnp.concatenate(
        [attention_output_weight, jnp.pad(router_weight, ((0, 0), (0, lanes - n_batch)))], axis=1
    )
    cuts = jnp.concatenate(cuts, axis=0)
    step = 1
    while step < n_batch:
        cuts = jnp.concatenate([cuts, swap(cuts, "batch", n_batch, step)], axis=0)
        cuts, both = lax.optimization_barrier((cuts, both)) if step == 1 else (cuts, both)
        step = step * 2
    step = 1
    while step < n_batch:
        both = jnp.concatenate([both, swap(both, "batch", n_batch, step)], axis=0)
        step = step * 2

    route_row = routes.reshape(1, per)
    d_result = out_grad[0]
    pick, pick_t, dz_sent = kernel_call(
        functools.partial(dispatch_kernel, capacity=capacity),
        "dispatch",
        [route_row, d_result],
        [((slots, per), BF16), ((per, slots), BF16), ((slots, width), BF16)],
    )
    table = sum(
        jnp.where(group == g, bias_table[:, g * heads : (g + 1) * heads], 0) for g in range(groups)
    )
    band = jnp.einsum(
        "dbc,bh->hdc",
        jnp.asarray(band_onehot(per), BF16),
        table,
        preferred_element_type=F32,
    )
    band = jnp.pad(band, ((0, 0), (0, 3), (0, 0)))
    arrived, cuts, dz_sent, band, both = lax.optimization_barrier(
        (arrived, cuts, dz_sent, band, both)
    )
    cuts = over_ring([cuts] * ring)
    dz_there = turn_batch(dz_sent)
    if not fine:
        cuts = natural(cuts, 3 * part)
    kv_rows = rows_own + 16
    q, kv_own, w_head = kernel_call(
        functools.partial(
            project_kernel,
            groups=groups,
            ring=ring,
            batch=n_batch,
            tall=tall,
            part=part,
            per=per,
            pieces=len(cuts),
        ),
        "project",
        [*arrived, *cuts],
        [
            ((rows_own, wide), BF16),
            ((kv_rows, 2 * wide), BF16),
            ((width, 3 * wide), BF16),
        ],
        [((width, 3 * part), F32)],
    )
    kv_own, both = lax.optimization_barrier((kv_own, both))
    kv_all = over_ring([kv_own] * ring)
    both = over_groups([both] * groups)

    out_t, lse, *mixed = attend(q, kv_all, band, heads, groups, ring, per)

    mixed, dz_there, both = lax.optimization_barrier((mixed, dz_there, both))
    both = jnp.stack([b.reshape(n_batch, tall, width + lanes) for b in both], axis=1)
    both = over_ring([both.reshape(n_batch * groups * tall, width + lanes)] * ring)
    if fine:
        both = kernel_call(
            functools.partial(gather_kernel, groups=groups, ring=ring, batch=n_batch, tall=tall),
            "gather",
            both,
            [((width, width + lanes), BF16)],
            [((width, width + lanes), F32)],
        )[0]
    else:
        both = natural(both, width + lanes)[0]
    mixed = over_groups(mixed)
    mixed, both = lax.optimization_barrier((mixed, both))
    middle, gate, *rows_sent = kernel_call(
        functools.partial(
            middle_kernel, groups=groups, ring=ring, batch=n_batch, part=part, capacity=capacity
        ),
        "middle",
        [*mixed, both, tokens[0], ffn_gain, pick, route_row],
        [((per, width), F32), ((per, 1), F32)] + [((capacity, width), BF16)] * n_batch,
    )
    rows_there = over_batch(rows_sent)
    produced, back, *saved = expert_layer(
        rows_there, dz_there, both, expert_in[0], expert_out[0], ring
    )
    back = turn_batch(back)
    router_part, *grads = expert_grads(*saved, groups, ring)
    g1, g2 = grads[:ring], grads[ring:]

    back, g1, g2 = lax.optimization_barrier((back, g1, g2))
    g1, g2 = over_ring(g1), over_ring(g2)
    grads_one, grads_two = merge(g1, g2)
    sums_shape = (n_batch, groups, tall, width + lanes)
    sums_shape = (
        [(sums_shape, F32)] + [(sums_shape, BF16)] * (ring - 1)
        if fine
        else [((width, width + lanes), F32)]
    )
    d_middle, ffn_gain_part, *rest = kernel_call(
        functools.partial(
            branch_kernel,
            groups=groups,
            ring=ring,
            batch=n_batch,
            tall=tall,
            part=part,
        ),
        "branch",
        [back, *mixed, pick_t, middle, d_result, ffn_gain, both, router_part],
        [((per, width), F32), ((1, width), F32)] + [((per, part), BF16)] * groups + sums_shape,
    )
    d_mix, out_parts = rest[:groups], rest[groups:]

    def by_place(parts, turn):
        if fine:
            return parts
        grad = parts[0].reshape(groups, ring, n_batch, tall, parts[0].shape[1])
        parts = xor_order([grad[:, r] for r in range(ring)], own)
        parts = [xor_order([p[:, z] for z in range(n_batch)], turn) for p in parts]
        parts = [[xor_order([z[g] for g in range(groups)], group) for z in p] for p in parts]
        parts = [jnp.stack([jnp.stack(z) for z in p]) for p in parts]
        return [parts[0]] + [p.astype(BF16) for p in parts[1:]]

    d_mix = over_groups(d_mix)
    out_parts = over_ring(by_place(out_parts, zed * 0))
    d_mix, grads_one, grads_two, out_parts = lax.optimization_barrier(
        (d_mix, grads_one, grads_two, out_parts)
    )
    out_part = kernel_call(
        functools.partial(half_kernel, ring=ring),
        "half_out",
        out_parts,
        [(out_parts[0].shape, BF16)],
    )[0]
    returned = turn_batch(produced)
    grads_one = swap(grads_one, "ctx", n_ctx, ring)
    grads_two = swap(grads_two, "ctx", n_ctx, 2 * ring)

    dq, dkv_own, *rest = attend_back(
        q, kv_all, band, d_mix, out_t, lse, heads, groups, ring, per
    )
    dkv_other, table_part = rest[: ring - 1], rest[ring - 1]
    dkv_other, grads_one, grads_two, out_part, returned = lax.optimization_barrier(
        (dkv_other, grads_one, grads_two, out_part, returned)
    )
    dkv_got = over_ring([dkv_own] + dkv_other)[1:]
    out_part = lax.all_to_all(out_part, "batch", split_axis=0, concat_axis=0, tiled=True)
    last_left, last_right = fold(g1, g2, grads_one, grads_two)
    last_left = swap(last_left, "ctx", n_ctx, 2 * ring)
    last_right = swap(last_right, "ctx", n_ctx, ring)

    grads_shape = (
        [((n_batch, groups, tall, 3 * part), F32)]
        + [((n_batch, groups, tall, 3 * part), BF16)] * (ring - 1)
        if fine
        else [((width, 3 * part), F32)]
    )
    d_packed, *packed_parts = kernel_call(
        functools.partial(
            weight_kernel,
            groups=groups,
            ring=ring,
            batch=n_batch,
            tall=tall,
            part=part,
            per=per,
        ),
        "weight",
        [dq, dkv_own, *dkv_got, *arrived],
        [((rows_own, 3 * wide), BF16)] + grads_shape,
        [((rows_own, width), BF16)],
    )
    late_rows = -(-(2 * width // lanes + head_count) // 8) * 8
    *d_normed, late = kernel_call(
        functools.partial(unproject_kernel, per=per, ring=ring, heads=heads, groups=groups),
        "unproject",
        [d_packed, w_head, attn_gain, ffn_gain_part, table_part, *arrived],
        [((per, width), F32)]
        + [((per, width), BF16)] * (groups - 1)
        + [((n_ctx * n_batch, late_rows, lanes), F32)],
    )
    packed_parts = over_ring(by_place(packed_parts, zed))
    packed_parts, d_normed, last_left, last_right, out_part = lax.optimization_barrier(
        (packed_parts, d_normed, last_left, last_right, out_part)
    )
    got = over_groups(d_normed)
    shape = packed_parts[0].shape[1:]
    packed_parts = kernel_call(
        functools.partial(half_kernel, ring=ring),
        "half_packed",
        packed_parts,
        [(shape, F32)] + [(shape, BF16)] * (n_batch - 1),
    )
    packed_parts = list(packed_parts)
    layer_out = kernel_call(
        combine_kernel,
        "combine",
        [returned, pick_t, middle, gate],
        [((per, width), BF16)],
    )[0][None]
    expert_in_grad, expert_out_grad = finish(
        g1,
        g2,
        grads_one,
        grads_two,
        last_left,
        last_right,
        width // n_ctx,
        expert_in.shape[2],
    )
    packed_parts[1], layer_out, expert_in_grad, expert_out_grad = lax.optimization_barrier(
        (packed_parts[1], layer_out, expert_in_grad, expert_out_grad)
    )
    packed_parts = over_batch(packed_parts)
    packed_parts, got = lax.optimization_barrier((packed_parts, got))
    tokens_grad = kernel_call(
        functools.partial(tokens_kernel, groups=groups),
        "tokens",
        [*got, tokens[0], attn_gain, d_middle],
        [((per, width), BF16)],
    )[0][None]
    parts = kernel_call(
        functools.partial(quarter_kernel, batch=n_batch),
        "quarter",
        [out_part, *packed_parts],
        [((tall, 3 * part + width + lanes), BF16)] * groups,
    )

    late = lax.all_to_all(late, ("ctx", "batch"), split_axis=0, concat_axis=0, tiled=True)
    attn_gain_grad, ffn_gain_grad, d_table = kernel_call(
        late_kernel,
        "late",
        [late],
        [((width // lanes, lanes), F32)] * 2 + [((head_count, lanes), F32)],
    )
    attn_gain_grad = attn_gain_grad.reshape(width)
    ffn_gain_grad = ffn_gain_grad.reshape(width)
    bias_grad = d_table[:, : bias_table.shape[0]].T
    qkv_grad, out_weight_grad, router_grad = kernel_call(
        functools.partial(columns_kernel, groups=groups, ring=ring, part=part),
        "columns",
        over_groups(parts),
        [((tall, 3 * width), F32), ((tall, width), F32), ((n_batch, tall), F32)],
    )
    router_grad = router_grad.T
    return (
        layer_out,
        tokens_grad,
        attn_gain_grad,
        qkv_grad,
        out_weight_grad,
        bias_grad,
        ffn_gain_grad,
        router_grad,
        expert_in_grad[None],
        expert_out_grad[None],
    )


def solution(mesh):
    return jax.shard_map(
        body,
        mesh=mesh,
        in_specs=(
            P("batch", "ctx", None),
            P("batch", "ctx"),
            P("ctx", "batch", None, None),
            P(),
            P(("ctx", "batch"), None),
            P(("ctx", "batch"), None),
            P(),
            P(),
            P(("ctx", "batch"), None),
            P("batch", None, None),
            P("batch", None, None),
            P("batch", "ctx", None),
        ),
        out_specs=(
            P("batch", "ctx", None),
            P("batch", "ctx", None),
            P(),
            P(("ctx", "batch"), None),
            P(("ctx", "batch"), None),
            P(),
            P(),
            P(("ctx", "batch"), None),
            P("batch", "ctx", None),
            P("batch", "ctx", None),
        ),
        check_vma=False,
    )
```

```python
import functools
import math

import jax
import jax.numpy as jnp
import numpy as np
from jax import lax
from jax.experimental import pallas as pl
from jax.experimental.pallas import tpu as pltpu
from jax.sharding import PartitionSpec as P

BUCKETS = 32
MAX_DIST = 128
EPSILON = 1e-06
MASKED = -1e30
F32 = jnp.float32
BF16 = jnp.bfloat16


def bucket_limits():
    half_span = BUCKETS // 2
    exact_span = half_span // 2
    log_levels = half_span - exact_span
    limits = []
    for level_at in range(1, log_levels):
        bound_row = exact_span
        while (
            bound_row**log_levels * exact_span**level_at
            < MAX_DIST**level_at * exact_span**log_levels
        ):
            bound_row = bound_row + 1
        limits.append(bound_row)
    return limits


def relative_bucket(offsets):
    half_span = BUCKETS // 2
    exact_span = half_span // 2
    distance = np.abs(offsets)
    far = np.full(distance.shape, exact_span, np.int32)
    for bound_row in bucket_limits():
        far = far + (distance >= bound_row).astype(np.int32)
    near = np.where(distance < exact_span, distance, far)
    return near + np.where(offsets > 0, half_span, 0)


def band_buckets(block):
    column = np.arange(2 * block)
    rows = []
    for d in range(5):
        if d in (0, 4):
            offsets = np.full((2 * block,), (d - 2) * max(block, MAX_DIST), np.int64)
        else:
            offsets = (d - 2) * block + block - column
        rows.append(relative_bucket(offsets))
    return np.stack(rows)


def band_onehot(block):
    return band_buckets(block)[:, None, :] == np.arange(BUCKETS)[None, :, None]


def dot(a, b, dims, precision=None):
    return lax.dot_general(a, b, (dims, ((), ())), preferred_element_type=F32, precision=precision)


NN = ((1,), (0,))
NT = ((1,), (1,))
TN = ((0,), (0,))


def xor_order(parts, index):
    parts = list(parts)
    step = 1
    while step < len(parts):
        odd = (index // step) % 2 == 1
        parts = [jnp.where(odd, parts[i ^ step], parts[i]) for i in range(len(parts))]
        step = step * 2
    return parts


def vmem(count):
    return [pl.BlockSpec(memory_space=pltpu.VMEM)] * count


def place(ring):
    ctx = lax.axis_index("ctx").astype(jnp.int32)
    return ctx // ring, ctx % ring, lax.axis_index("batch").astype(jnp.int32)


def kernel_call(kernel, name, arrays, out_shape, scratch=()):
    return pl.pallas_call(
        kernel,
        out_shape=tuple(jax.ShapeDtypeStruct(shape, kind) for shape, kind in out_shape),
        in_specs=vmem(len(arrays)),
        out_specs=vmem(len(out_shape)),
        scratch_shapes=[
            pltpu.SMEM(shape, kind) if kind == jnp.int32 else pltpu.VMEM(shape, kind)
            for shape, kind in scratch
        ],
        compiler_params=pltpu.CompilerParams(vmem_limit_bytes=56 << 20),
        name=name,
    )(*arrays)


def swap(value, axis, size, mask):
    return lax.ppermute(value, axis, [(i, i ^ mask) for i in range(size)])


def column(row, size):
    return jnp.broadcast_to(row, (size, row.shape[1])).T


def first_kernel(tokens_ref, seg_ref, gain_ref, row_ref, message_ref, *cut_refs, part, ring):
    info = place(ring)
    tokens = tokens_ref[...].astype(F32)
    per, width = tokens.shape
    scale = lax.rsqrt(jnp.mean(tokens * tokens, axis=1, keepdims=True) + EPSILON)
    message_ref[:per, :] = (tokens * scale * gain_ref[...].astype(F32)[None, :]).astype(BF16)
    message_ref[per:, :] = jnp.zeros((message_ref.shape[0] - per, width), BF16)
    message_ref[per:, :per] = jnp.broadcast_to(
        seg_ref[...].astype(F32), (message_ref.shape[0] - per, per)
    ).astype(BF16)
    rows = row_ref[...].astype(F32)
    groups = len(cut_refs)
    cuts = [
        jnp.concatenate(
            [rows[:, k * width + g * part : k * width + (g + 1) * part] for k in range(3)], axis=1
        )
        for g in range(groups)
    ]
    for ref, cut in zip(cut_refs, xor_order(cuts, info[0])):
        ref[...] = cut.astype(BF16)


def row_place(info, g, r, z, ring, batch):
    return ((g ^ info[0]) * ring + (r ^ info[1])) * batch + (z ^ info[2])


def assemble(info, piece_refs, dest_ref, groups, batch, tall):
    ring = len(piece_refs)
    for r in range(ring):
        for z in range(batch):
            for g in range(groups):
                block = row_place(info, g, r, z, ring, batch)
                at = (z * groups + g) * tall
                dest_ref[pl.ds(pl.multiple_of(block * tall, 8), tall), :] = piece_refs[r][
                    at : at + tall, :
                ].astype(F32)


def project_kernel(*refs, groups, ring, batch, tall, part, per, pieces):
    x_refs, refs = refs[:groups], refs[groups:]
    w_refs, refs = refs[:pieces], refs[pieces:]
    q_ref, kv_ref, w_out, w_s = refs
    wide = 256
    if tall % 8 == 0:
        assemble(place(ring), w_refs, w_s, groups, batch, tall)
    else:
        w_s[...] = w_refs[0][...].astype(F32)
    gap = jnp.zeros((w_s.shape[0], wide - part), BF16)
    w = jnp.concatenate(
        [x for k in range(3) for x in (w_s[:, k * part : (k + 1) * part].astype(BF16), gap)],
        axis=1,
    )
    w_out[...] = w
    kv_ref[groups * per :, :] = jnp.zeros((kv_ref.shape[0] - groups * per, 2 * wide), BF16)
    seg = jnp.concatenate([x_ref[per : per + 1, :wide].astype(F32) for x_ref in x_refs], axis=0)
    seg = jnp.concatenate(
        [seg, jnp.zeros((kv_ref.shape[0] - groups * per - groups, wide), F32)], axis=0
    )
    kv_ref[groups * per :, :wide] = seg.astype(BF16)
    for m in range(groups):
        packed = dot(x_refs[m][:per, :], w_out[...], NN).astype(BF16)
        q_ref[m * per : (m + 1) * per, :] = packed[:, :wide]
        kv_ref[m * per : (m + 1) * per, :] = packed[:, wide:]


def slot_row(route, capacity):
    per = route.shape[1]
    earlier = lax.broadcasted_iota(jnp.int32, (per, per), 0) < lax.broadcasted_iota(
        jnp.int32, (per, per), 1
    )
    same = jnp.where((column(route, per) == route) & earlier, 1.0, 0.0)
    return route * capacity + jnp.sum(same, axis=0, keepdims=True)


def dispatch_kernel(route_ref, dz_ref, pick_ref, pick_t_ref, sent_ref, *, capacity):
    target = slot_row(route_ref[...].astype(F32), capacity).astype(jnp.int32)
    slots, per = pick_ref.shape
    slot = lax.broadcasted_iota(jnp.int32, (slots, per), 0)
    pick = jnp.where(slot == target, 1.0, 0.0)
    pick_ref[...] = pick.astype(BF16)
    pick_t_ref[...] = pick.T.astype(BF16)
    sent_ref[...] = dot(pick.astype(BF16), dz_ref[...], NN).astype(BF16)


def gather_kernel(*refs, groups, ring, batch, tall):
    w_refs, w_ref, w_s = refs[:-2], refs[-2], refs[-1]
    assemble(place(ring), w_refs, w_s, groups, batch, tall)
    w_ref[...] = w_s[...].astype(BF16)


def middle_kernel(*refs, groups, ring, batch, part, capacity):
    info = place(ring)
    mixed_refs, refs = refs[:groups], refs[groups:]
    w_ref, tokens_ref, gain_ref, pick_ref, route_ref, middle_ref, gate_ref = refs[:7]
    sent_refs = refs[7:]
    width = tokens_ref.shape[1]
    middle = tokens_ref[...].astype(F32)
    for m in range(groups):
        start = pl.multiple_of((info[0] ^ m) * part, 16)
        middle += dot(mixed_refs[m][...], w_ref[pl.ds(start, part), :width], NN)
    middle_ref[...] = middle
    scale = lax.rsqrt(jnp.mean(middle * middle, axis=1, keepdims=True) + EPSILON)
    normed = (middle * scale * gain_ref[...].astype(F32)[None, :]).astype(BF16)
    for m, ref in enumerate(sent_refs):
        start = pl.multiple_of((info[2] ^ m) * capacity, capacity)
        ref[...] = dot(pick_ref[pl.ds(start, capacity), :], normed, NN).astype(BF16)
    logits = dot(normed, w_ref[:, width:], NN)
    lane = lax.broadcasted_iota(jnp.int32, logits.shape, 1)
    logits = jnp.where(lane < batch, logits, MASKED)
    expo = jnp.exp(logits - jnp.max(logits, axis=1, keepdims=True))
    probs = expo / jnp.sum(expo, axis=1, keepdims=True)
    route = column(route_ref[...].astype(F32), logits.shape[1]).astype(jnp.int32)
    gate_ref[...] = jnp.sum(jnp.where(lane == route, probs, 0.0), axis=1, keepdims=True)


def branch_kernel(back_ref, *refs, groups, ring, batch, tall, part):
    info = place(ring)
    mixed_refs, refs = refs[:groups], refs[groups:]
    pick_t_ref, middle_ref, dz_ref, gain_ref, w_ref, rpart_ref = refs[:6]
    d_middle_ref, gain_part_ref = refs[6:8]
    d_mixed_refs, grad_refs = refs[8 : 8 + groups], refs[8 + groups :]
    width = middle_ref.shape[1]
    d_normed = dot(pick_t_ref[...], back_ref[...], NN)
    middle = middle_ref[...]
    scale = lax.rsqrt(jnp.mean(middle * middle, axis=1, keepdims=True) + EPSILON)
    gain_part_ref[...] = jnp.sum(d_normed * middle * scale, axis=0, keepdims=True)
    scaled = gain_ref[...].astype(F32)[None, :] * d_normed
    d_middle = (
        dz_ref[...].astype(F32)
        + scale * scaled
        - middle
        * (scale * scale * scale)
        * jnp.mean(scaled * middle, axis=1, keepdims=True)
    )
    d_middle_ref[...] = d_middle
    d_branch = d_middle.astype(BF16)
    for m in range(groups):
        start = pl.multiple_of((info[0] ^ m) * part, 16)
        d_mixed_refs[m][...] = dot(d_branch, w_ref[pl.ds(start, part), :width], NT).astype(BF16)
    for m in range(groups):
        start = pl.multiple_of((info[0] ^ m) * part, 16)
        grad = dot(mixed_refs[m][...], d_branch, TN)
        grad = jnp.concatenate([grad, rpart_ref[pl.ds(start, part), :]], axis=1)
        if tall % 8 == 0:
            scatter_rows(info, grad, m, grad_refs, ring, batch, tall, 0)
        else:
            grad_refs[0][pl.ds(start, part), :] = grad


def scatter_rows(info, grad, g, grad_refs, ring, batch, tall, turn):
    for z in range(batch):
        rows = [
            grad[(r * batch + z) * tall : (r * batch + z + 1) * tall, :] for r in range(ring)
        ]
        for ref, row in zip(grad_refs, xor_order(rows, info[1])):
            ref[z ^ turn, g] = row.astype(ref.dtype)


def weight_kernel(dq_ref, *refs, groups, ring, batch, tall, part, per):
    info = place(ring)
    got_refs, refs = refs[:ring], refs[ring:]
    x_refs, dp_ref, grad_refs, x_s = refs[:groups], refs[groups], refs[groups + 1 : -1], refs[-1]
    wide = 256
    for m in range(groups):
        rows = slice(m * per, (m + 1) * per)
        dkv = got_refs[0][rows, :]
        for ref in got_refs[1:]:
            dkv += ref[rows, :].astype(F32)
        dp_ref[rows, :wide] = dq_ref[rows, :]
        dp_ref[rows, wide:] = dkv.astype(BF16)
        x_s[rows, :] = x_refs[m][:per, :]
    share = ring * batch * tall
    for g in range(groups):
        grad = dot(x_s[:, g * share : (g + 1) * share], dp_ref[...], TN)
        grad = jnp.concatenate([grad[:, k * wide : k * wide + part] for k in range(3)], axis=1)
        if tall % 8 == 0:
            scatter_rows(info, grad, g ^ info[0], grad_refs, ring, batch, tall, info[2])
        else:
            grad_refs[0][g * share : (g + 1) * share, :] = grad


def unproject_kernel(
    dp_ref, w_ref, gain_ref, gain2_ref, table_ref, *refs, per, ring, heads, groups
):
    x_refs, d_refs, late_ref = refs[:groups], refs[groups : 2 * groups], refs[-1]
    width = gain2_ref.shape[1]
    total = jnp.zeros((1, width), F32)
    for m, ref in enumerate(d_refs):
        rows = slice(m * per, (m + 1) * per)
        d_normed = dot(dp_ref[rows, :], w_ref[...], NT)
        ref[...] = d_normed.astype(ref.dtype)
        total += jnp.sum(d_normed * x_refs[m][:per, :].astype(F32), axis=0, keepdims=True)
    total = total / gain_ref[...].astype(F32)[None, :]
    late_ref[0] = jnp.zeros(late_ref.shape[1:], F32)
    count = width // 128
    for k in range(count):
        late_ref[0, k : k + 1, :] = total[:, k * 128 : (k + 1) * 128]
        late_ref[0, count + k : count + k + 1, :] = gain2_ref[:, k * 128 : (k + 1) * 128]
    group = place(ring)[0]
    for h in range(heads):
        late_ref[0, pl.ds(2 * count + group * heads + h, 1), :] = table_ref[h : h + 1, :]
    whole = late_ref[0]

    @pl.loop(1, late_ref.shape[0])
    def _(k):
        late_ref[k] = whole


def late_kernel(got_ref, gain1_ref, gain2_ref, table_ref):
    total = jnp.sum(got_ref[...], axis=0)
    count, heads = gain1_ref.shape[0], table_ref.shape[0]
    gain1_ref[...] = total[:count, :]
    gain2_ref[...] = total[count : 2 * count, :]
    table_ref[...] = total[2 * count : 2 * count + heads, :]


def half_kernel(*refs, ring):
    total = refs[0][...]
    for ref in refs[1:ring]:
        total += ref[...].astype(F32)
    if len(refs) == ring + 1:
        refs[ring][...] = total.astype(BF16)
    else:
        for m, ref in enumerate(refs[ring:]):
            ref[...] = total[m].astype(ref.dtype)


def quarter_kernel(two_ref, *refs, batch):
    one = refs[0][...]
    for ref in refs[1:batch]:
        one += ref[...].astype(F32)
    two = jnp.sum(two_ref[...].astype(F32), axis=0)
    cut = one.shape[2]
    for m, ref in enumerate(refs[batch:]):
        ref[:, :cut] = one[m].astype(BF16)
        ref[:, cut:] = two[m].astype(BF16)


def columns_kernel(*refs, groups, ring, part):
    qkv_ref, out_ref, router_ref = refs[groups:]
    cut, width = 3 * part, out_ref.shape[1]
    parts = xor_order([ref[:, :cut].astype(F32) for ref in refs[:groups]], place(ring)[0])
    qkv_ref[...] = jnp.concatenate(
        [p[:, k * part : (k + 1) * part] for k in range(3) for p in parts], axis=1
    )
    total = sum(ref[:, cut:].astype(F32) for ref in refs[:groups])
    out_ref[...] = total[:, :width]
    router = total[:, width:]
    spare = jnp.zeros((router.shape[1] - router.shape[0], router.shape[1]), F32)
    router = jnp.concatenate([router, spare], axis=0).T
    router_ref[...] = router[: router_ref.shape[0], : router_ref.shape[1]]


def tokens_kernel(*refs, groups):
    tokens_ref, gain_ref, d_middle_ref, out_ref = refs[groups:]
    d_normed = refs[0][...]
    for ref in refs[1:groups]:
        d_normed += ref[...].astype(F32)
    tokens = tokens_ref[...].astype(F32)
    scale = lax.rsqrt(jnp.mean(tokens * tokens, axis=1, keepdims=True) + EPSILON)
    scaled = gain_ref[...].astype(F32)[None, :] * d_normed
    out_ref[...] = (
        d_middle_ref[...]
        + scale * scaled
        - tokens
        * (scale * scale * scale)
        * jnp.mean(scaled * tokens, axis=1, keepdims=True)
    ).astype(BF16)


def combine_kernel(got_ref, pick_t_ref, middle_ref, gate_ref, out_ref):
    returned = dot(pick_t_ref[...], got_ref[...], NN)
    out_ref[...] = (middle_ref[...] + gate_ref[...] * returned).astype(BF16)


def ring_total(refs):
    return sum(ref[...].astype(F32) for ref in refs)


def merge_kernel(*refs, ring):
    one_ref, two_ref = refs[2 * ring :]
    g1, g2 = ring_total(refs[:ring]).astype(BF16), ring_total(refs[ring : 2 * ring]).astype(BF16)
    rows = g1.shape[0]

    def put(ref):
        ref[:rows, :] = g1
        ref[rows:, :] = g2

    pl.when(pl.program_id(0) <= 1)(lambda: put(one_ref))
    pl.when(pl.program_id(0) >= 2)(lambda: put(two_ref))


def merge(g1, g2):
    groups, rows, width = g1[0].shape
    assert groups == 4
    ring = len(g1)
    half = width // 2
    order = lambda s: (jnp.where(s == 0, 1, jnp.where(s == 3, 2, 3)), 0, jnp.where(s >= 2, 1, 0))
    message = jax.ShapeDtypeStruct((2, 2 * rows, half), BF16)
    return pl.pallas_call(
        functools.partial(merge_kernel, ring=ring),
        grid=(groups,),
        out_shape=(message, message),
        in_specs=[pl.BlockSpec((None, rows, half), order)] * (2 * ring),
        out_specs=[
            pl.BlockSpec((None, 2 * rows, half), lambda s: (jnp.minimum(s, 1), 0, 0)),
            pl.BlockSpec((None, 2 * rows, half), lambda s: (jnp.where(s <= 2, 1, 0), 0, 0)),
        ],
        compiler_params=pltpu.CompilerParams(
            dimension_semantics=("arbitrary",), vmem_limit_bytes=56 << 20
        ),
        name="merge",
    )(*g1, *g2)


def fold_kernel(*refs, ring):
    one_ref, two_ref, left_out, right_out = refs[4 * ring :]
    rows = refs[0].shape[0]
    for k, (add_ref, ref) in enumerate(((one_ref, left_out), (two_ref, right_out))):
        for part in range(2):
            at = (2 * k + part) * ring
            cut = slice(part * rows, (part + 1) * rows)
            ref[cut, :] = (ring_total(refs[at : at + ring]) + add_ref[cut, :].astype(F32)).astype(BF16)


def fold(g1, g2, one, two):
    rows, half = g1[0].shape[1], one.shape[2]
    ring = len(g1)
    left = pl.BlockSpec((None, rows, half), lambda s: (2, 0, 0))
    right = pl.BlockSpec((None, rows, half), lambda s: (1, 0, 1))
    second = pl.BlockSpec((None, 2 * rows, half), lambda s: (1, 0, 0))
    whole = pl.BlockSpec((2 * rows, half), lambda s: (0, 0))
    return pl.pallas_call(
        functools.partial(fold_kernel, ring=ring),
        grid=(1,),
        out_shape=(jax.ShapeDtypeStruct((2 * rows, half), BF16),) * 2,
        in_specs=[left] * (2 * ring) + [right] * (2 * ring) + [second] * 2,
        out_specs=[whole] * 2,
        compiler_params=pltpu.CompilerParams(vmem_limit_bytes=56 << 20),
        name="fold",
    )(*g1, *g2, *g1, *g2, one, two)


def finish_kernel(*refs, ring):
    one_ref, two_ref, left_ref, right_ref, in_ref, out_ref = refs[2 * ring :]
    tall, width = in_ref.shape[0], out_ref.shape[1]
    half, rows = width // 2, out_ref.shape[0]
    g1, g2 = ring_total(refs[:ring]), ring_total(refs[ring : 2 * ring])
    for at, first_ref, last_ref in ((0, one_ref, left_ref), (half, two_ref, right_ref)):
        cut = slice(at, at + half)
        more = first_ref[...].astype(F32) + last_ref[...].astype(F32)
        total = g1[:, cut] + more[:rows, :]
        for j in range(in_ref.shape[1] // width):
            in_ref[:, j * width + at : j * width + at + half] = total[j * tall : (j + 1) * tall, :]
        out_ref[:, cut] = g2[:, cut] + more[rows:, :]


def finish(g1, g2, one, two, left, right, tall, hidden):
    rows, width = g1[0].shape[1:]
    ring, half = len(g1), width // 2
    mine = pl.BlockSpec((None, rows, width), lambda s: (0, 0, 0))
    first = pl.BlockSpec((None, 2 * rows, half), lambda s: (0, 0, 0))
    whole = pl.BlockSpec((2 * rows, half), lambda s: (0, 0))
    return pl.pallas_call(
        functools.partial(finish_kernel, ring=ring),
        grid=(1,),
        out_shape=(
            jax.ShapeDtypeStruct((tall, hidden), F32),
            jax.ShapeDtypeStruct((rows, width), F32),
        ),
        in_specs=[mine] * (2 * ring) + [first] * 2 + [whole] * 2,
        out_specs=[
            pl.BlockSpec((tall, hidden), lambda s: (0, 0)),
            pl.BlockSpec((rows, width), lambda s: (0, 0)),
        ],
        compiler_params=pltpu.CompilerParams(vmem_limit_bytes=56 << 20),
        name="finish",
    )(*g1, *g2, one, two, left, right)


SEGMENTS = 8


def set_bias(band_ref, bias_s, heads, block):
    @pl.loop(0, heads)
    def _(h):
        @pl.loop(0, 5)
        def _(d):
            row = jnp.broadcast_to(band_ref[h, pl.ds(d, 1), :], (block, 2 * block))
            bias_s[h, d] = pltpu.roll(row, block, 1, stride=1, stride_axis=0)[:, :block]


def key_at(kb, info, ring, groups):
    return ((kb % ring) ^ info[1]) * groups + ((kb // ring) ^ info[0])


def set_spans(info, kv_refs, seg_s, span_s, groups, ring, block):
    rows = [ref[groups * block : groups * block + groups, :block].astype(F32) for ref in kv_refs]
    seg = jnp.concatenate(rows, axis=0)
    seg_s[...] = seg
    blocks = groups * ring
    low, high = seg[:, 0:1], seg[:, block - 1 : block]
    at = lax.broadcasted_iota(jnp.int32, (blocks, 1), 0)
    natural = (((at % groups) ^ info[0]) * ring + ((at // groups) ^ info[1])).astype(F32)
    for i in range(groups):
        meets = (low <= high[i : i + 1, :]) & (high >= low[i : i + 1, :])
        first = jnp.min(jnp.where(meets, natural, float(blocks)))
        last = jnp.max(jnp.where(meets, natural, -1.0))
        span_s[i, 0] = first.astype(jnp.int32)
        span_s[i, 1] = last.astype(jnp.int32) + 1


def with_extras(pair, half, extras):
    lane = lax.broadcasted_iota(jnp.int32, pair.shape, 1)
    kept = jnp.where(lane // 64 == half, pair, 0.0)
    spot = lane - (1 - half) * 64
    for at, extra in extras:
        if at is None:
            kept = jnp.where((spot >= 0) & (spot < SEGMENTS), extra(spot), kept)
        else:
            kept = jnp.where(spot == at, extra, kept)
    return kept


def key_extras(seg_col):
    return (None, lambda spot: jnp.where(spot.astype(F32) == seg_col, 0.0, MASKED))


def query_extras(seg_col):
    return (None, lambda spot: jnp.where(spot.astype(F32) == seg_col, 1.0, 0.0))


def three_parts(value):
    high = value.astype(BF16).astype(F32)
    middle = (value - high).astype(BF16).astype(F32)
    return high, middle, value - high - middle


def set_keys(kv_refs, seg_s, heads, groups, block, ones, key_s, turned_s, turn, value_s=None):
    wide = 256
    for r, ref in enumerate(kv_refs):

        @pl.loop(0, groups)
        def _(g):
            at, rows = r * groups + g, pl.ds(pl.multiple_of(g * block, block), block)
            seg_col = column(seg_s[pl.ds(at, 1), :], 128)
            turned_s[at] = ref[rows, turn : turn + wide].astype(F32).T.astype(BF16)
            for h in range(heads):
                lane = (h // 2) * 128
                extras = [key_extras(seg_col)] + [(SEGMENTS + n, 1.0) for n in range(ones)]
                key = with_extras(ref[rows, lane : lane + 128].astype(F32), h % 2, extras)
                key_s[at, h] = key.astype(BF16)
                if value_s is not None:
                    lane = wide + lane
                    extras = [(n, 1.0) for n in range(ones)]
                    value = with_extras(ref[rows, lane : lane + 128].astype(F32), h % 2, extras)
                    value_s[at, h] = value.astype(BF16)


def two_step(first, last, start, finish, even, odd):
    start(first, even)

    @pl.loop(0, (last - first + 1) // 2)
    def _(j):
        kb = first + 2 * j
        start(jnp.minimum(kb + 1, last - 1), odd)
        finish(kb, even)

        @pl.when(kb + 1 < last)
        def _():
            start(jnp.minimum(kb + 2, last - 1), even)
            finish(kb + 1, odd)


def attend_kernel(q_ref, *refs, heads, groups, ring, block):
    info = place(ring)
    kv_refs, refs = refs[:ring], refs[ring:]
    band_ref, ot_ref, lse_ref = refs[:3]
    mixed_refs, refs = refs[3 : 3 + groups], refs[3 + groups :]
    bias_s, seg_s, span_s, key_s, vt_s, query_s, stat_s, acc_s, even_s, odd_s = refs
    set_bias(band_ref, bias_s, heads, block)
    set_spans(info, kv_refs, seg_s, span_s, groups, ring, block)
    set_keys(kv_refs, seg_s, heads, groups, block, 0, key_s, vt_s, 256)

    @pl.loop(0, groups)
    def _(i):
        qb = (i ^ info[0]) * ring + info[1]
        rows = pl.ds(pl.multiple_of(i * block, block), block)
        seg_col = column(seg_s[pl.ds(i, 1), :], 128)
        for h in range(heads):
            lane = (h // 2) * 128
            query = q_ref[rows, lane : lane + 128].astype(F32) * 0.125
            query_s[h] = with_extras(query, h % 2, [query_extras(seg_col)]).astype(BF16)
        stat_s[0:heads] = jnp.full((heads, 1, block), MASKED, F32)
        stat_s[heads : 2 * heads] = jnp.zeros((heads, 1, block), F32)
        acc_s[...] = jnp.zeros_like(acc_s)

        def start(kb, score_s):
            at = key_at(kb, info, ring, groups)
            d = jnp.clip(kb - qb, -2, 2) + 2
            for h in range(heads):
                score_s[h] = dot(key_s[at, h], query_s[h], NT) + bias_s[h, d]

        def finish(kb, score_s):
            at = key_at(kb, info, ring, groups)
            tops = [
                jnp.maximum(stat_s[h], jnp.max(score_s[h], axis=0, keepdims=True))
                for h in range(heads)
            ]
            expos = [jnp.exp(score_s[h] - tops[h]) for h in range(heads)]
            for h in range(heads):
                decay = jnp.exp(stat_s[h] - tops[h])
                stat_s[h] = tops[h]
                stat_s[heads + h] = stat_s[heads + h] * decay + jnp.sum(
                    expos[h], axis=0, keepdims=True
                )
                value_t = vt_s[at, h * 64 : (h + 1) * 64, :]
                acc_s[h] = acc_s[h] * decay + dot(value_t, expos[h].astype(BF16), NN)

        two_step(span_s[i, 0], span_s[i, 1], start, finish, even_s, odd_s)

        for h in range(heads):
            total = stat_s[heads + h]
            ot_ref[i, h * 64 : (h + 1) * 64, :] = acc_s[h] / total
            lse_ref[i, h : h + 1, :] = stat_s[h] + jnp.log(total)

    for i in range(groups):
        mixed_refs[i][...] = ot_ref[i].T.astype(BF16)


def attend(q, kv_all, band, heads, groups, ring, block):
    width = heads * 64
    return kernel_call(
        functools.partial(attend_kernel, heads=heads, groups=groups, ring=ring, block=block),
        "attend",
        [q, *kv_all, band],
        [((groups, width, block), F32), ((groups, 8, block), F32)]
        + [((block, width), BF16)] * groups,
        [
            ((heads, 5, block, block), F32),
            ((groups * ring, block), F32),
            ((groups, 2), jnp.int32),
            ((groups * ring, heads, block, 128), BF16),
            ((groups * ring, 256, block), BF16),
            ((heads, block, 128), BF16),
            ((2 * heads, 1, block), F32),
            ((heads, 64, block), F32),
            ((heads, block, block), F32),
            ((heads, block, block), F32),
        ],
    )


def attend_back_kernel(q_ref, *refs, heads, groups, ring, block):
    info = place(ring)
    kv_refs, refs = refs[:ring], refs[ring:]
    band_ref, refs = refs[0], refs[1:]
    dmix_refs, refs = refs[:groups], refs[groups:]
    ot_ref, lse_ref, dq_ref, own_ref = refs[:4]
    other_refs, refs = refs[4 : 3 + ring], refs[3 + ring :]
    dband_ref, bias_s, seg_s, span_s, key_s, value_s, kt_s, query_s, plain_s, dout_s = refs[:10]
    dplain_s, dqt_s, dkv_s, dbias_s, dmix_s = refs[10:]
    wide = 256
    blocks = groups * ring
    set_bias(band_ref, bias_s, heads, block)
    set_spans(info, kv_refs, seg_s, span_s, groups, ring, block)
    set_keys(kv_refs, seg_s, heads, groups, block, 3, key_s, kt_s, 0, value_s)
    for i in range(groups):
        dmix_s[i, :, : heads * 64] = dmix_refs[i][...].astype(F32)
        dmix_s[i, :, heads * 64 :] = jnp.zeros((block, wide - heads * 64), F32)

    @pl.loop(0, blocks)
    def _(at):
        dkv_s[at] = jnp.zeros(dkv_s.shape[1:], F32)

    @pl.loop(0, heads)
    def _(h):
        dbias_s[h] = jnp.zeros(dbias_s.shape[1:], F32)

    @pl.loop(0, groups)
    def _(i):
        qb = (i ^ info[0]) * ring + info[1]
        rows = pl.ds(pl.multiple_of(i * block, block), block)
        seg_col = column(seg_s[pl.ds(i, 1), :], 128)
        dmix = dmix_s[i]
        dmix_t = dmix.T
        for h in range(heads):
            cut, lane = slice(h * 64, (h + 1) * 64), (h // 2) * 128
            delta = jnp.sum(dmix_t[cut, :] * ot_ref[i, cut, :], axis=0, keepdims=True)
            delta = three_parts(column(-delta, 128))
            lse = three_parts(column(-lse_ref[i, h : h + 1, :], 128))
            query = q_ref[rows, lane : lane + 128].astype(F32) * 0.125
            extras = [query_extras(seg_col)] + [(SEGMENTS + n, lse[n]) for n in range(3)]
            query_s[h] = with_extras(query, h % 2, extras).astype(BF16)
            plain_s[h] = with_extras(query, h % 2, []).astype(BF16)
            d_out = dmix[:, lane : lane + 128]
            extras = [(n, delta[n]) for n in range(3)]
            dout_s[h] = with_extras(d_out, h % 2, extras).astype(BF16)
            dplain_s[h] = with_extras(d_out, h % 2, []).astype(BF16)
        dqt_s[...] = jnp.zeros_like(dqt_s)

        @pl.loop(span_s[i, 0], span_s[i, 1])
        def _(kb):
            at = key_at(kb, info, ring, groups)
            d = jnp.clip(kb - qb, -2, 2) + 2
            softs = [
                jnp.exp(dot(key_s[at, h], query_s[h], NT) + bias_s[h, d]) for h in range(heads)
            ]
            d_scores = [
                (softs[h] * dot(value_s[at, h], dout_s[h], NT)).astype(BF16) for h in range(heads)
            ]
            for h in range(heads):
                lane = (h // 2) * 128
                dkv_s[at, :, wide + lane : wide + lane + 128] += dot(
                    softs[h].astype(BF16), dplain_s[h], NN
                )
                dkv_s[at, :, lane : lane + 128] += dot(d_scores[h], plain_s[h], NN)
                dqt_s[h * 64 : (h + 1) * 64, :] += dot(
                    kt_s[at, h * 64 : (h + 1) * 64, :], d_scores[h], NN
                )
                dbias_s[h, d] += d_scores[h].astype(F32)

        pad = jnp.zeros((wide - heads * 64, block), F32)
        dq_ref[rows, :] = (jnp.concatenate([dqt_s[...], pad], axis=0) * 0.125).T.astype(BF16)

    for r in range(ring):

        @pl.loop(0, groups)
        def _(g):
            at, rows = r * groups + g, pl.ds(pl.multiple_of(g * block, block), block)
            if r == 0:
                own_ref[rows, :] = dkv_s[at]
            else:
                other_refs[r - 1][rows, :] = dkv_s[at].astype(BF16)

    buckets = band_buckets(block)
    zero = jnp.zeros((block, block), F32)
    lane = lax.broadcasted_iota(jnp.int32, (1, 128), 1)
    column_at = lax.broadcasted_iota(jnp.int32, (1, 2 * block), 1)
    dband_ref[...] = jnp.zeros_like(dband_ref)

    @pl.loop(0, heads)
    def _(h):
        table = jnp.zeros((1, 128), F32)
        for d in range(5):
            if d in (0, 4):
                tile = jnp.sum(dbias_s[h, d], axis=0, keepdims=True)
                tile = jnp.concatenate([tile, zero[:1]], axis=1)
            else:
                tile = jnp.concatenate([zero, dbias_s[h, d]], axis=1)
                tall = block
                while tall > 1:
                    tall = tall // 2
                    tile = tile[:tall] + pltpu.roll(tile[tall:], 2 * block - tall, 1)
            for bucket in sorted(set(buckets[d].tolist())):
                held = np.nonzero(buckets[d] == bucket)[0]
                keep = (column_at >= int(held[0])) & (column_at <= int(held[-1]))
                held_sum = jnp.sum(jnp.where(keep, tile, 0.0), axis=1, keepdims=True)
                table += jnp.where(lane == bucket, held_sum, 0.0)
        dband_ref[pl.ds(h, 1), :] = table


def attend_back(q, kv_all, band, d_mix, out_t, lse, heads, groups, ring, block):
    own = groups * block
    blocks = groups * ring
    return kernel_call(
        functools.partial(attend_back_kernel, heads=heads, groups=groups, ring=ring, block=block),
        "attend_back",
        [q, *kv_all, band, *d_mix, out_t, lse],
        [((own, 256), BF16), ((own, 512), F32)]
        + [((own, 512), BF16)] * (ring - 1)
        + [((8, 128), F32)],
        [((heads, 5, block, block), F32), ((blocks, block), F32), ((groups, 2), jnp.int32)]
        + [((blocks, heads, block, 128), BF16)] * 2
        + [((blocks, 256, block), BF16)]
        + [((heads, block, 128), BF16)] * 4
        + [
            ((heads * 64, block), F32),
            ((blocks, block, 512), F32),
            ((heads, 5, block, block), F32),
            ((groups, block, 256), F32),
        ],
    )


def expert_kernel(*refs, experts, ring, batch):
    info = place(ring)
    piece_refs, refs = refs[:batch], refs[batch:]
    dz_ref, router_ref, w1_ref, w2_ref = refs[:4]
    prod_ref, back_ref, d_logits_ref, rows_ref, dret_ref, hidden_ref, d_pre_ref = refs[4:11]
    prob_s, prod_s, back_s = refs[11:]
    capacity = piece_refs[0].shape[0]
    step = pl.program_id(0)
    me = info[2]
    lane = lax.broadcasted_iota(jnp.int32, prob_s.shape, 1)

    @pl.when(step == 0)
    def _():
        for m, ref in enumerate(piece_refs):
            start = pl.multiple_of((me ^ m) * capacity, capacity)
            rows_ref[pl.ds(start, capacity), :] = ref[...]
        logits = dot(rows_ref[...], router_ref[...], NN)
        logits = jnp.where(lane < experts, logits, MASKED)
        expo = jnp.exp(logits - jnp.max(logits, axis=1, keepdims=True))
        probs = expo / jnp.sum(expo, axis=1, keepdims=True)
        prob_s[...] = probs
        gate = jnp.sum(jnp.where(lane == me, probs, 0.0), axis=1, keepdims=True)
        dret_ref[...] = (gate * dz_ref[...].astype(F32)).astype(BF16)
        prod_s[...] = jnp.zeros_like(prod_s)
        back_s[...] = jnp.zeros_like(back_s)

    w1 = w1_ref[...]
    w2 = w2_ref[...]
    pre = dot(rows_ref[...], w1, NN)
    cumulative = 0.5 * (1.0 + lax.erf(pre * (1.0 / math.sqrt(2.0))))
    density = jnp.exp(-0.5 * pre * pre) * (1.0 / math.sqrt(2.0 * math.pi))
    hidden = (pre * cumulative).astype(BF16)
    d_hidden = dot(dret_ref[...], w2, NT)
    d_pre = (d_hidden * (cumulative + pre * density)).astype(BF16)
    hidden_ref[...] = hidden
    d_pre_ref[...] = d_pre
    prod_s[...] += dot(hidden, w2, NN)
    back_s[...] += dot(d_pre, w1, NT)

    @pl.when(step == pl.num_programs(0) - 1)
    def _():
        probs = prob_s[...]
        gate = jnp.sum(jnp.where(lane == me, probs, 0.0), axis=1, keepdims=True)
        chosen = jnp.where(lane == me, 1.0, 0.0)
        produced = prod_s[...].astype(BF16)
        prod_ref[...] = produced
        d_gate = jnp.sum(
            dz_ref[...].astype(F32) * produced.astype(F32), axis=1, keepdims=True
        )
        d_logits = (d_gate * probs * (chosen - gate)).astype(BF16)
        back = back_s[...].astype(BF16).astype(F32) + dot(d_logits, router_ref[...], NT)
        back_ref[...] = back.astype(BF16)
        d_logits_ref[...] = d_logits


def expert_layer(pieces, dz, w_both, w1, w2, ring):
    batch = len(pieces)
    capacity, width = pieces[0].shape
    slots = batch * capacity
    lanes = 128
    hidden = w1.shape[1]
    cut = width
    fixed = lambda j: (0, 0)
    whole = pl.BlockSpec((slots, width), fixed)
    return pl.pallas_call(
        functools.partial(expert_kernel, experts=batch, ring=ring, batch=batch),
        grid=(hidden // cut,),
        in_specs=[pl.BlockSpec((capacity, width), fixed)] * batch
        + [
            whole,
            pl.BlockSpec((width, lanes), lambda j: (0, width // lanes)),
            pl.BlockSpec((width, cut), lambda j: (0, j)),
            pl.BlockSpec((cut, width), lambda j: (j, 0)),
        ],
        out_specs=[
            whole,
            whole,
            pl.BlockSpec((slots, lanes), fixed),
            whole,
            whole,
            pl.BlockSpec((slots, cut), lambda j: (0, j)),
            pl.BlockSpec((slots, cut), lambda j: (0, j)),
        ],
        scratch_shapes=[
            pltpu.VMEM((slots, lanes), F32),
            pltpu.VMEM((slots, width), F32),
            pltpu.VMEM((slots, width), F32),
        ],
        out_shape=(
            jax.ShapeDtypeStruct((slots, width), BF16),
            jax.ShapeDtypeStruct((slots, width), BF16),
            jax.ShapeDtypeStruct((slots, lanes), BF16),
            jax.ShapeDtypeStruct((slots, width), BF16),
            jax.ShapeDtypeStruct((slots, width), BF16),
            jax.ShapeDtypeStruct((slots, hidden), BF16),
            jax.ShapeDtypeStruct((slots, hidden), BF16),
        ),
        compiler_params=pltpu.CompilerParams(
            dimension_semantics=("arbitrary",), vmem_limit_bytes=56 << 20
        ),
        name="experts",
    )(*pieces, dz, w_both, w1, w2)


def expert_grad_kernel(
    d_logits_ref, rows_ref, dret_ref, hidden_ref, d_pre_ref, *refs, groups, ring
):
    info = place(ring)
    router_ref, g1_refs, g2_refs, rows_t = refs[0], refs[1 : 1 + ring], refs[1 + ring : -1], refs[-1]

    @pl.when(pl.program_id(0) == 0)
    def _():
        rows_t[...] = rows_ref[...].astype(F32).T.astype(BF16)
        router_ref[...] = dot(rows_t[...], d_logits_ref[...], NN)

    g2 = dot(hidden_ref[...], dret_ref[...], TN).astype(BF16)
    share = g2.shape[0] // ring
    parts = [g2[c * share : (c + 1) * share, :] for c in range(ring)]
    for ref, rows in zip(g2_refs, xor_order(parts, info[1])):
        ref[pl.program_id(0) ^ info[0]] = rows
    g1 = dot(rows_t[...], d_pre_ref[...], NN).astype(BF16)
    tall = g1.shape[0] // (groups * ring)
    for g in range(groups):
        parts = [
            g1[(g * ring + c) * tall : (g * ring + c + 1) * tall, :] for c in range(ring)
        ]
        for ref, rows in zip(g1_refs, xor_order(parts, info[1])):
            ref[g ^ info[0]] = rows


def expert_grads(d_logits, rows, d_ret, hidden, d_pre, groups, ring):
    slots, width = rows.shape
    lanes = d_logits.shape[1]
    devices = groups * ring
    share = hidden.shape[1] // devices
    cut = share * ring
    tall = width // devices
    tiles = hidden.shape[1] // cut
    return pl.pallas_call(
        functools.partial(expert_grad_kernel, groups=groups, ring=ring),
        grid=(tiles,),
        in_specs=[
            pl.BlockSpec((slots, lanes), lambda j: (0, 0)),
            pl.BlockSpec((slots, width), lambda j: (0, 0)),
            pl.BlockSpec((slots, width), lambda j: (0, 0)),
            pl.BlockSpec((slots, cut), lambda j: (0, j)),
            pl.BlockSpec((slots, cut), lambda j: (0, j)),
        ],
        out_specs=[pl.BlockSpec((width, lanes), lambda j: (0, 0))]
        + [pl.BlockSpec((groups, tall, cut), lambda j: (0, j, 0))] * ring
        + [pl.BlockSpec((groups, share, width), lambda j: (0, 0, 0))] * ring,
        scratch_shapes=[pltpu.VMEM((width, slots), BF16)],
        out_shape=(jax.ShapeDtypeStruct((width, lanes), F32),)
        + (jax.ShapeDtypeStruct((groups, tiles * tall, cut), BF16),) * ring
        + (jax.ShapeDtypeStruct((groups, share, width), BF16),) * ring,
        compiler_params=pltpu.CompilerParams(
            dimension_semantics=("arbitrary",), vmem_limit_bytes=56 << 20
        ),
        name="expert_grads",
    )(d_logits, rows, d_ret, hidden, d_pre)


def body(
    tokens,
    seg_ids,
    routes,
    attn_gain,
    query_key_value_weight,
    attention_output_weight,
    bias_table,
    ffn_gain,
    router_weight,
    expert_in,
    expert_out,
    out_grad,
):
    n_ctx = lax.axis_size("ctx")
    n_batch = lax.axis_size("batch")
    per, width = tokens.shape[1:]
    head_count = bias_table.shape[1]
    groups = math.gcd(head_count, n_ctx)
    ring = n_ctx // groups
    heads = head_count // groups
    part = heads * 64
    tall = query_key_value_weight.shape[0]
    lanes = 128
    wide = 256
    rows_own = groups * per
    capacity = max(2, 2 * per // n_batch)
    slots = n_batch * capacity
    fine = tall % 8 == 0
    ctx = lax.axis_index("ctx").astype(jnp.int32)
    zed = lax.axis_index("batch").astype(jnp.int32)
    group, own = ctx // ring, ctx % ring

    def over_groups(parts):
        return [
            parts[m] if m == 0 else swap(parts[m], "ctx", n_ctx, ring * m) for m in range(groups)
        ]

    def over_ring(parts):
        return [parts[m] if m == 0 else swap(parts[m], "ctx", n_ctx, m) for m in range(ring)]

    def over_batch(parts):
        return [
            parts[m] if m == 0 else swap(parts[m], "batch", n_batch, m) for m in range(n_batch)
        ]

    def turn_batch(rows):
        rows = rows.reshape(n_batch, capacity, width)
        rows = lax.all_to_all(rows, "batch", split_axis=0, concat_axis=0, tiled=True)
        return rows.reshape(slots, width)

    def natural(pieces, columns):
        pieces = [p.reshape(n_batch, groups, tall, columns) for p in pieces]
        pieces = xor_order(pieces, own)
        pieces = [xor_order([c[z] for z in range(n_batch)], zed) for c in pieces]
        pieces = [[xor_order([b[g] for g in range(groups)], group) for b in c] for c in pieces]
        order = [(g, r, z) for g in range(groups) for r in range(ring) for z in range(n_batch)]
        return [jnp.concatenate([pieces[r][z][g] for g, r, z in order], axis=0)]

    first = kernel_call(
        functools.partial(first_kernel, part=part, ring=ring),
        "first",
        [tokens[0], seg_ids, attn_gain, query_key_value_weight],
        [((per + 16, width), BF16)] + [((tall, 3 * part), BF16)] * groups,
    )
    message, cuts = first[0], list(first[1:])
    cuts = over_groups(cuts)
    message, cuts = lax.optimization_barrier((message, cuts))
    arrived = over_groups([message] * groups)
    both = jnp.concatenate(
        [attention_output_weight, jnp.pad(router_weight, ((0, 0), (0, lanes - n_batch)))], axis=1
    )
    cuts = jnp.concatenate(cuts, axis=0)
    step = 1
    while step < n_batch:
        cuts = jnp.concatenate([cuts, swap(cuts, "batch", n_batch, step)], axis=0)
        step = step * 2
    route_row = routes.reshape(1, per)
    d_result = out_grad[0]
    pick, pick_t, dz_sent = kernel_call(
        functools.partial(dispatch_kernel, capacity=capacity),
        "dispatch",
        [route_row, d_result],
        [((slots, per), BF16), ((per, slots), BF16), ((slots, width), BF16)],
    )
    both, pick = lax.optimization_barrier((both, pick))
    step = 1
    while step < n_batch:
        both = jnp.concatenate([both, swap(both, "batch", n_batch, step)], axis=0)
        step = step * 2
    table = sum(
        jnp.where(group == g, bias_table[:, g * heads : (g + 1) * heads], 0) for g in range(groups)
    )
    band = jnp.einsum(
        "dbc,bh->hdc",
        jnp.asarray(band_onehot(per), BF16),
        table,
        preferred_element_type=F32,
    )
    band = jnp.pad(band, ((0, 0), (0, 3), (0, 0)))
    arrived, cuts, dz_sent, band, both = lax.optimization_barrier(
        (arrived, cuts, dz_sent, band, both)
    )
    cuts = over_ring([cuts] * ring)
    dz_there = turn_batch(dz_sent)
    if not fine:
        cuts = natural(cuts, 3 * part)
    kv_rows = rows_own + 16
    q, kv_own, w_head = kernel_call(
        functools.partial(
            project_kernel,
            groups=groups,
            ring=ring,
            batch=n_batch,
            tall=tall,
            part=part,
            per=per,
            pieces=len(cuts),
        ),
        "project",
        [*arrived, *cuts],
        [
            ((rows_own, wide), BF16),
            ((kv_rows, 2 * wide), BF16),
            ((width, 3 * wide), BF16),
        ],
        [((width, 3 * part), F32)],
    )
    kv_own, both = lax.optimization_barrier((kv_own, both))
    kv_all = over_ring([kv_own] * ring)
    both = over_groups([both] * groups)

    out_t, lse, *mixed = attend(q, kv_all, band, heads, groups, ring, per)

    mixed, dz_there, both = lax.optimization_barrier((mixed, dz_there, both))
    both = jnp.stack([b.reshape(n_batch, tall, width + lanes) for b in both], axis=1)
    both = over_ring([both.reshape(n_batch * groups * tall, width + lanes)] * ring)
    if fine:
        both = kernel_call(
            functools.partial(gather_kernel, groups=groups, ring=ring, batch=n_batch, tall=tall),
            "gather",
            both,
            [((width, width + lanes), BF16)],
            [((width, width + lanes), F32)],
        )[0]
    else:
        both = natural(both, width + lanes)[0]
    mixed = over_groups(mixed)
    mixed, both = lax.optimization_barrier((mixed, both))
    middle, gate, *rows_sent = kernel_call(
        functools.partial(
            middle_kernel, groups=groups, ring=ring, batch=n_batch, part=part, capacity=capacity
        ),
        "middle",
        [*mixed, both, tokens[0], ffn_gain, pick, route_row],
        [((per, width), F32), ((per, 1), F32)] + [((capacity, width), BF16)] * n_batch,
    )
    rows_there = over_batch(rows_sent)
    produced, back, *saved = expert_layer(
        rows_there, dz_there, both, expert_in[0], expert_out[0], ring
    )
    back = turn_batch(back)
    router_part, *grads = expert_grads(*saved, groups, ring)
    g1, g2 = grads[:ring], grads[ring:]

    back, g1, g2 = lax.optimization_barrier((back, g1, g2))
    g1, g2 = over_ring(g1), over_ring(g2)
    grads_one, grads_two = merge(g1, g2)
    sums_shape = (n_batch, groups, tall, width + lanes)
    sums_shape = (
        [(sums_shape, F32)] + [(sums_shape, BF16)] * (ring - 1)
        if fine
        else [((width, width + lanes), F32)]
    )
    d_middle, ffn_gain_part, *rest = kernel_call(
        functools.partial(
            branch_kernel,
            groups=groups,
            ring=ring,
            batch=n_batch,
            tall=tall,
            part=part,
        ),
        "branch",
        [back, *mixed, pick_t, middle, d_result, ffn_gain, both, router_part],
        [((per, width), F32), ((1, width), F32)] + [((per, part), BF16)] * groups + sums_shape,
    )
    d_mix, out_parts = rest[:groups], rest[groups:]

    def by_place(parts, turn):
        if fine:
            return parts
        grad = parts[0].reshape(groups, ring, n_batch, tall, parts[0].shape[1])
        parts = xor_order([grad[:, r] for r in range(ring)], own)
        parts = [xor_order([p[:, z] for z in range(n_batch)], turn) for p in parts]
        parts = [[xor_order([z[g] for g in range(groups)], group) for z in p] for p in parts]
        parts = [jnp.stack([jnp.stack(z) for z in p]) for p in parts]
        return [parts[0]] + [p.astype(BF16) for p in parts[1:]]

    d_mix = over_groups(d_mix)
    out_parts = over_ring(by_place(out_parts, zed * 0))
    d_mix, grads_one, grads_two, out_parts = lax.optimization_barrier(
        (d_mix, grads_one, grads_two, out_parts)
    )
    out_part = kernel_call(
        functools.partial(half_kernel, ring=ring),
        "half_out",
        out_parts,
        [(out_parts[0].shape, BF16)],
    )[0]
    returned = turn_batch(produced)
    grads_one = swap(grads_one, "ctx", n_ctx, ring)
    grads_two = swap(grads_two, "ctx", n_ctx, 2 * ring)

    dq, dkv_own, *rest = attend_back(
        q, kv_all, band, d_mix, out_t, lse, heads, groups, ring, per
    )
    dkv_other, table_part = rest[: ring - 1], rest[ring - 1]
    dkv_other, grads_one, grads_two, out_part, returned = lax.optimization_barrier(
        (dkv_other, grads_one, grads_two, out_part, returned)
    )
    dkv_got = over_ring([dkv_own] + dkv_other)[1:]
    out_part = lax.all_to_all(out_part, "batch", split_axis=0, concat_axis=0, tiled=True)
    last_left, last_right = fold(g1, g2, grads_one, grads_two)
    last_left = swap(last_left, "ctx", n_ctx, 2 * ring)
    last_right = swap(last_right, "ctx", n_ctx, ring)

    grads_shape = (
        [((n_batch, groups, tall, 3 * part), F32)]
        + [((n_batch, groups, tall, 3 * part), BF16)] * (ring - 1)
        if fine
        else [((width, 3 * part), F32)]
    )
    d_packed, *packed_parts = kernel_call(
        functools.partial(
            weight_kernel,
            groups=groups,
            ring=ring,
            batch=n_batch,
            tall=tall,
            part=part,
            per=per,
        ),
        "weight",
        [dq, dkv_own, *dkv_got, *arrived],
        [((rows_own, 3 * wide), BF16)] + grads_shape,
        [((rows_own, width), BF16)],
    )
    late_rows = -(-(2 * width // lanes + head_count) // 8) * 8
    *d_normed, late = kernel_call(
        functools.partial(unproject_kernel, per=per, ring=ring, heads=heads, groups=groups),
        "unproject",
        [d_packed, w_head, attn_gain, ffn_gain_part, table_part, *arrived],
        [((per, width), F32)]
        + [((per, width), BF16)] * (groups - 1)
        + [((n_ctx * n_batch, late_rows, lanes), F32)],
    )
    packed_parts = over_ring(by_place(packed_parts, zed))
    packed_parts, d_normed, last_left, last_right, out_part = lax.optimization_barrier(
        (packed_parts, d_normed, last_left, last_right, out_part)
    )
    got = over_groups(d_normed)
    shape = packed_parts[0].shape[1:]
    packed_parts = kernel_call(
        functools.partial(half_kernel, ring=ring),
        "half_packed",
        packed_parts,
        [(shape, F32)] + [(shape, BF16)] * (n_batch - 1),
    )
    packed_parts = list(packed_parts)
    layer_out = kernel_call(
        combine_kernel,
        "combine",
        [returned, pick_t, middle, gate],
        [((per, width), BF16)],
    )[0][None]
    expert_in_grad, expert_out_grad = finish(
        g1,
        g2,
        grads_one,
        grads_two,
        last_left,
        last_right,
        width // n_ctx,
        expert_in.shape[2],
    )
    packed_parts[1], layer_out, expert_in_grad, expert_out_grad = lax.optimization_barrier(
        (packed_parts[1], layer_out, expert_in_grad, expert_out_grad)
    )
    packed_parts = over_batch(packed_parts)
    packed_parts, got = lax.optimization_barrier((packed_parts, got))
    tokens_grad = kernel_call(
        functools.partial(tokens_kernel, groups=groups),
        "tokens",
        [*got, tokens[0], attn_gain, d_middle],
        [((per, width), BF16)],
    )[0][None]
    parts = kernel_call(
        functools.partial(quarter_kernel, batch=n_batch),
        "quarter",
        [out_part, *packed_parts],
        [((tall, 3 * part + width + lanes), BF16)] * groups,
    )

    late = lax.all_to_all(late, ("ctx", "batch"), split_axis=0, concat_axis=0, tiled=True)
    attn_gain_grad, ffn_gain_grad, d_table = kernel_call(
        late_kernel,
        "late",
        [late],
        [((width // lanes, lanes), F32)] * 2 + [((head_count, lanes), F32)],
    )
    attn_gain_grad = attn_gain_grad.reshape(width)
    ffn_gain_grad = ffn_gain_grad.reshape(width)
    bias_grad = d_table[:, : bias_table.shape[0]].T
    qkv_grad, out_weight_grad, router_grad = kernel_call(
        functools.partial(columns_kernel, groups=groups, ring=ring, part=part),
        "columns",
        over_groups(parts),
        [((tall, 3 * width), F32), ((tall, width), F32), ((n_batch, tall), F32)],
    )
    router_grad = router_grad.T
    return (
        layer_out,
        tokens_grad,
        attn_gain_grad,
        qkv_grad,
        out_weight_grad,
        bias_grad,
        ffn_gain_grad,
        router_grad,
        expert_in_grad[None],
        expert_out_grad[None],
    )


def solution(mesh):
    return jax.shard_map(
        body,
        mesh=mesh,
        in_specs=(
            P("batch", "ctx", None),
            P("batch", "ctx"),
            P("ctx", "batch", None, None),
            P(),
            P(("ctx", "batch"), None),
            P(("ctx", "batch"), None),
            P(),
            P(),
            P(("ctx", "batch"), None),
            P("batch", None, None),
            P("batch", None, None),
            P("batch", "ctx", None),
        ),
        out_specs=(
            P("batch", "ctx", None),
            P("batch", "ctx", None),
            P(),
            P(("ctx", "batch"), None),
            P(("ctx", "batch"), None),
            P(),
            P(),
            P(("ctx", "batch"), None),
            P("batch", "ctx", None),
            P("batch", "ctx", None),
        ),
        check_vma=False,
    )
```
